256 devices in a mesh: tile: 32 (over x, z), lev: 8 (over y, core).
Axes of the slice: x: 4, y: 4, z: 8, core: 2. Of those that a mesh axis runs over, the one named last changes fastest.
Arguments:
- probes: float32 [64, 512, 32, 128], P('lev', 'tile')
- sigma: float32 [64, 512, 32], P('lev', 'tile'), may hold values from 0.5 to 2
- obs_count: int32 [1024], P('tile'), may hold values from 0 to 128, as said below
- obs_cell: int32 [1024, 128], P('tile'), may hold values from 0 to 511
- obs_rinv: float32 [1024, 128], P('tile'), may hold values from 0.25 to 4
- obs_jac: float32 [1024, 64, 128], P('tile', 'lev'), may hold values from -0.75 to 0.75
Outputs:
- qpanel: float32 [64, 512, 32, 128], P('lev', 'tile')
- rfac: float32 [128, 128], replicated
The draws below stay inside these ranges and needn't reach their ends.
Inputs may be any that keep to these rules, and one draw needn't show every extreme that they name: obs_count[s * 32 + t] is the number of live slots that band s sends to band t; in every draw some destination band receives 128 live slots from every source. `obs_cell`: index row * 32 + column of a cell inside the destination band.
All inputs are finite; a program needn't handle non-finite values.
Results may differ from the reference program's by a relative error of at most 0.0003.
Values sent between devices are 32-bit elements; how exact they have to be, the bound alone decides.
No kernel may reach another device: no remote copies, remote signals or barrier semaphores. Data moves between devices by JAX's collectives and lax.ppermute only.
A program may use at most 128 MiB of HBM per device.

```python
import math
import jax
import jax.numpy as jnp
from jax import lax

P_SIZE = 128
ROWS = 16
COLS = 32
CAP = 128
TILES = 32
LEVELS = 64
NY = 512
BINS = 1024


def draw_probes(key, part):
    noise_key, scale_key = jax.random.split(key, 2)
    shape = (LEVELS, NY, COLS, P_SIZE)
    base = jax.random.normal(noise_key, shape, jnp.float32)
    mixed = base + 0.6 * jnp.roll(base, 1, axis=3)
    cell_scale = jnp.exp(jnp.log(10.0) * jax.random.uniform(scale_key, (LEVELS, NY, COLS, 1), jnp.float32))
    latitude = 1.0 + 2.0 * jnp.arange(NY, dtype=jnp.float32) / max(NY - 1, 1)
    return (mixed * cell_scale * latitude[None, :, None, None]).astype(jnp.float32)


def draw_obs_count(key, part):
    order_key, heavy_key, light_key = jax.random.split(key, 3)
    ranking = jax.random.permutation(order_key, TILES)
    dense = ranking < max(TILES // 4, 1)
    heavy = CAP - jax.random.randint(heavy_key, (TILES, TILES), 0, max(CAP // 8, 1))
    light = jax.random.randint(light_key, (TILES, TILES), 0, CAP // 4 + 1)
    counts = jnp.where(dense[None, :], heavy, light)
    counts = jnp.where((ranking == 0)[None, :], CAP, counts)
    return counts.reshape(TILES * TILES).astype(jnp.int32)


def plant(drawn, own_key, least, largest):
    index_at = [jax.random.randint(jax.random.fold_in(own_key, axis), (), 0, length) for axis, length in enumerate(drawn.shape)]
    main_axis = drawn.shape.index(max(drawn.shape))
    neighbour = index_at[:main_axis] + [(index_at[main_axis] + 1) % drawn.shape[main_axis]] + index_at[main_axis + 1:]
    return drawn.at[tuple(index_at)].set(least).at[tuple(neighbour)].set(largest)


def steps_of(own_key, dims, cuts, smallest, largest):
    loudness = 1.0
    for dim, shards_of in cuts:
        draws = jax.random.uniform(jax.random.fold_in(jax.random.fold_in(own_key, 6), dim), (shards_of,), jnp.float32, smallest / len(cuts), largest / len(cuts))
        loudness = loudness * jnp.repeat(jnp.exp(draws), dims[dim] // shards_of).reshape((-1,) + (1,) * (len(dims) - 1 - dim))
    return loudness


def noise(stream_key, dims, scale, bound, cuts=(), kind=jnp.bfloat16):
    drawn = jax.random.normal(stream_key, dims, jnp.float32) * scale
    if len(cuts) > 0:
        drawn = steps_of(stream_key, dims, cuts, -0.22, 0.18) * drawn
    return jnp.clip(drawn, min=-bound, max=bound).astype(kind)


def setup_inputs(seed: int = 0) -> dict:
    keys = jax.random.split(jax.random.key(seed), 7)
    probes = draw_probes(jax.random.fold_in(keys[6], 71), 0)
    sigma = jnp.clip(jnp.exp(math.log(2.0) - 1.3862944 * jax.random.uniform(keys[1], (LEVELS, NY, COLS), jnp.float32) ** steps_of(keys[1], (LEVELS, NY, COLS), ((0, 8), (1, 32)), -0.2, 0.2)), 0.5, 2.0)
    obs_count = draw_obs_count(jax.random.fold_in(keys[6], 71), 0)
    obs_cell = plant(jax.random.randint(keys[3], (BINS, CAP), 0, ROWS * COLS), jax.random.fold_in(keys[3], 1), 0, (ROWS * COLS) - 1).astype(jnp.int32)
    obs_rinv = jnp.clip(jnp.exp(math.log(4.0) - 2.7725887 * jax.random.uniform(keys[4], (BINS, CAP), jnp.float32) ** steps_of(keys[4], (BINS, CAP), ((0, 32),), -0.2, 0.2)), 0.25, 4.0)
    obs_jac = noise(keys[5], (BINS, LEVELS, CAP), LEVELS ** -0.5, 0.75, ((0, 32), (1, 8)), jnp.float32)
    return dict(probes=probes, sigma=sigma, obs_count=obs_count, obs_cell=obs_cell, obs_rinv=obs_rinv, obs_jac=obs_jac)


def tap_weights():
    profile = [math.exp(-(offset / 6.0) * (offset / 6.0)) for offset in range(-7, 8)]
    scaling = math.sqrt(sum((element * element for element in profile)))
    return [element / scaling for element in profile]

def spread(padded, axis, length):
    weights = tap_weights()
    total = weights[0] * lax.slice_in_dim(padded, 0, length, axis=axis)
    for offset in range(1, 15):
        total = total + weights[offset] * lax.slice_in_dim(padded, offset, offset + length, axis=axis)
    return total

def smooth(field):
    length = field.shape[2]
    wrapped = jnp.concatenate([field[:, :, length - 7:], field, field[:, :, :7]], axis=2)
    across = spread(wrapped, 2, length)
    rows_padded = jnp.pad(across, ((0, 0), (7, 7), (0, 0), (0, 0)))
    northward = spread(rows_padded, 1, field.shape[1])
    stacked = jnp.pad(northward, ((7, 7), (0, 0), (0, 0), (0, 0)))
    return spread(stacked, 0, field.shape[0])

def reference(probes, sigma, obs_count, obs_cell, obs_rinv, obs_jac):
    scaled = smooth(probes) * sigma[..., None]
    cell_table = obs_cell.reshape(TILES, TILES, CAP)
    count_table = obs_count.reshape(TILES, TILES)
    rinv_table = obs_rinv.reshape(TILES, TILES, CAP)
    jac_table = obs_jac.reshape(TILES, TILES, LEVELS, CAP)

    def per_tile(target):
        block = lax.dynamic_slice_in_dim(scaled, target * ROWS, ROWS, 1).reshape(LEVELS, ROWS * COLS, P_SIZE)
        cells = lax.dynamic_index_in_dim(cell_table, target, 1, keepdims=False).reshape(-1)
        counts = lax.dynamic_index_in_dim(count_table, target, 1, keepdims=False)
        rinv = lax.dynamic_index_in_dim(rinv_table, target, 1, keepdims=False)
        jacobian = lax.dynamic_index_in_dim(jac_table, target, 1, keepdims=False)
        jacobian = jacobian.transpose(1, 0, 2).reshape(LEVELS, TILES * CAP)
        live = jnp.arange(CAP, dtype=jnp.int32)[None, :] < counts[:, None]
        factor = jnp.where(live, rinv, 0.0).reshape(-1)
        picked = block[:, cells, :]
        column = jnp.einsum('ko,kop->op', jacobian, picked, precision=lax.Precision.HIGHEST)
        weighted = column * factor[:, None]
        spread_back = jacobian[:, :, None] * weighted[None, :, :]
        return jnp.zeros((LEVELS, ROWS * COLS, P_SIZE), jnp.float32).at[:, cells].add(spread_back)
    adjoints = lax.map(per_tile, jnp.arange(TILES, dtype=jnp.int32))
    adjoint = adjoints.reshape(TILES, LEVELS, ROWS, COLS, P_SIZE).transpose(1, 0, 2, 3, 4).reshape(LEVELS, NY, COLS, P_SIZE)
    panel = probes + smooth(adjoint * sigma[..., None])
    flat = panel.reshape(-1, P_SIZE)
    gram = jnp.einsum('cp,cq->pq', flat, flat, precision=lax.Precision.HIGHEST) / (LEVELS * NY * COLS)
    lower = jnp.linalg.cholesky(gram)
    inverse = lax.linalg.triangular_solve(lower, jnp.eye(P_SIZE, dtype=jnp.float32), left_side=True, lower=True)
    qpanel = jnp.einsum('cp,qp->cq', flat, inverse, precision=lax.Precision.HIGHEST).reshape(panel.shape)
    return (qpanel, lower.T)
```

```python
import math

import jax
import jax.numpy as jnp
import numpy as np
from jax import lax
from jax.experimental import pallas as pl
from jax.experimental.pallas import tpu as pltpu
from jax.sharding import PartitionSpec as P

F32 = jnp.float32
BF16 = jnp.bfloat16
REACH = 7


def tap_weights():
    profile = [math.exp(-(offset / 6.0) * (offset / 6.0)) for offset in range(-7, 8)]
    scaling = math.sqrt(sum((element * element for element in profile)))
    return [element / scaling for element in profile]


TAPS = tap_weights()


def ring_matrix(cols, size):
    one = np.zeros((cols, cols), np.float64)
    for c in range(cols):
        for d in range(-REACH, REACH + 1):
            one[c, (c + d) % cols] += TAPS[d + REACH]
    return np.kron(np.eye(size // cols), one).astype(np.float32)


def level_matrix(levels, width):
    band = np.zeros((levels, width), np.float32)
    for k in range(levels):
        for d in range(-REACH, REACH + 1):
            band[k, levels + k + d] = TAPS[d + REACH]
    return band


def split(x):
    hi = x.astype(BF16)
    return hi, (x - hi.astype(F32)).astype(BF16)


def dot(a, b):
    return jnp.dot(a, b, preferred_element_type=F32)


def zonal(mhi, mlo, pair):
    outs = []
    for h in range(2):
        hi, lo = split(pair[256 * h : 256 * h + 256])
        outs.append(dot(mhi, hi) + (dot(mlo, hi) + dot(mhi, lo)))
    return jnp.concatenate(outs, axis=0)


def put_zonal(x, kp, rim, out_ref, head_ref, tail_ref):
    cells = x.shape[0]
    for j in range(2):
        part = x[:, 128 * j : 128 * j + 128]
        out_ref[2 * kp + j] = part
        head_ref[2 * kp + j] = part[:rim]
        tail_ref[2 * kp + j] = part[cells - rim :]


def zonal_kernel(field_ref, mhi_ref, mlo_ref, out_ref, head_ref, tail_ref):
    levels = field_ref.shape[0]
    rim = head_ref.shape[1]
    mhi, mlo = mhi_ref[...], mlo_ref[...]
    for kp in range(levels // 2):
        pair = jnp.concatenate([field_ref[2 * kp], field_ref[2 * kp + 1]], axis=1)
        put_zonal(zonal(mhi, mlo, pair), kp, rim, out_ref, head_ref, tail_ref)


def meridional(k, j, north_ref, own_ref, south_ref):
    cut = pl.ds(8 * j, 8)
    rows = jnp.concatenate(
        [north_ref[k, :, cut, :], own_ref[k, :, cut, :], south_ref[k, :, cut, :]], axis=0
    )
    length = own_ref.shape[1]
    total = TAPS[REACH] * rows[REACH : REACH + length]
    for d in range(1, REACH + 1):
        total = total + TAPS[REACH + d] * (
            rows[REACH - d : REACH - d + length] + rows[REACH + d : REACH + d + length]
        )
    return total


CHUNK = 1024
GROUP = 256


def source_at(order_ref, position):
    return position ^ order_ref[(position >> 3) & 1]


def prepare_kernel(order_ref, sent_ref, sigma_ref, seen_ref, pick_ref, place_ref):
    levels, cells = sigma_ref.shape
    sources, _, slots = sent_ref.shape
    stacked = jnp.concatenate(split(sigma_ref[...]), axis=0)
    cell_down = lax.broadcasted_iota(jnp.int32, (cells, slots), 0).astype(F32)
    cell_along = lax.broadcasted_iota(jnp.int32, (slots, cells), 1).astype(F32)
    for s in range(sources):
        source = source_at(order_ref, s)
        here = sent_ref[source, levels + 1 : levels + 2]
        onehot = jnp.where(cell_down == here, 1.0, 0.0).astype(BF16)
        place_ref[:, slots * s : slots * s + slots] = onehot
        picked = dot(stacked, onehot)
        seen_ref[source] = sent_ref[source, :levels] * (picked[:levels] + picked[levels:])
        turned = jnp.broadcast_to(here, (8, slots)).T
        pick_ref[slots * s : slots * s + slots, :] = jnp.where(
            cell_along == turned[:, :1], 1.0, 0.0
        ).astype(BF16)


def column_kernel(
    order_ref, north_ref, own_ref, south_ref, sent_ref, below_ref, seen_ref, above_ref,
    band_ref, pick_ref,
    other_ref, first_ref, second_ref, turned_ref,
    w_ref, table_ref,
):
    levels, rows, cols, width = own_ref.shape
    cells = rows * cols
    sources, _, slots = sent_ref.shape
    total = sources * slots

    def level_pass(k, carry):
        for j in range(cols // 8):
            w_ref[k, :, pl.ds(8 * j, 8), :] = meridional(k, j, north_ref, own_ref, south_ref)
        return carry

    lax.fori_loop(0, levels, level_pass, 0)

    for s in range(0, sources, 4):
        stack = jnp.concatenate(
            [
                jnp.concatenate([below_ref[i], seen_ref[i], above_ref[i]], axis=0)
                for i in range(s, s + 4)
            ],
            axis=1,
        )
        spread = jnp.dot(
            band_ref[...], stack, precision=lax.Precision.HIGHEST, preferred_element_type=F32
        )
        for i in range(4):
            table_ref[s + i] = spread[:, slots * i : slots * i + slots]
    for s in range(sources):
        source = source_at(order_ref, s)
        at = slice(slots * s, slots * s + slots)
        turned_ref[at, :levels] = table_ref[source].T
        rinv = jnp.broadcast_to(sent_ref[source, levels : levels + 1], (8, slots))
        turned_ref[at, levels : 2 * levels] = rinv.T

    half = total // 2
    for kp in range(levels // 2):
        pair = jnp.concatenate(
            [w_ref[2 * kp].reshape(cells, width), w_ref[2 * kp + 1].reshape(cells, width)], axis=1
        )
        hi, lo = split(pair)
        for dst_ref, start in ((other_ref, 0), (first_ref, half), (second_ref, half + half // 2)):

            def chunk_pass(c, carry, dst_ref=dst_ref, start=start):
                to = pl.ds(pl.multiple_of(c * CHUNK, CHUNK), CHUNK)
                at = pl.ds(pl.multiple_of(start + c * CHUNK, CHUNK), CHUNK)
                pick = pick_ref[at, :]
                seen = dot(pick, hi) + dot(pick, lo)
                part = (
                    turned_ref[at, 2 * kp : 2 * kp + 1] * seen[:, :width]
                    + turned_ref[at, 2 * kp + 1 : 2 * kp + 2] * seen[:, width:]
                )
                if kp == 0:
                    dst_ref[to, :] = part
                else:
                    dst_ref[to, :] += part
                return carry

            lax.fori_loop(0, dst_ref.shape[0] // CHUNK, chunk_pass, 0)


def adjoint_kernel(
    other_ref, own_ref, turned_ref, place_ref, mhi_ref, mlo_ref,
    out_ref, head_ref, tail_ref,
    weighted_ref, *, base,
):
    levels, cells, width = out_ref.shape
    rim = head_ref.shape[1]
    total = place_ref.shape[1]
    half = total // 2
    weighted_ref[:half] = other_ref[...] * turned_ref[:half, 8:9]
    weighted_ref[half:] = own_ref[...] * turned_ref[half:, 8:9]
    mhi, mlo = mhi_ref[...], mlo_ref[...]
    for kp in range(levels // 2):
        k = base + 2 * kp
        field = None
        for c in range(total // CHUNK):
            at = slice(c * CHUNK, c * CHUNK + CHUNK)
            weighted = weighted_ref[at, :]
            pair = jnp.concatenate(
                [turned_ref[at, k : k + 1] * weighted, turned_ref[at, k + 1 : k + 2] * weighted],
                axis=1,
            )
            hi, lo = split(pair)
            place = place_ref[:, at]
            part = dot(place, hi) + dot(place, lo)
            field = part if field is None else field + part
        put_zonal(zonal(mhi, mlo, field), kp, rim, out_ref, head_ref, tail_ref)


def panel_kernel(north_ref, own_ref, south_ref, probes_ref, panel_ref, gram_ref):
    levels, rows, cols, width = own_ref.shape

    def level_pass(k, carry):
        for j in range(cols // 8):
            cut = pl.ds(8 * j, 8)
            panel_ref[k, :, cut, :] = probes_ref[k, :, cut, :] + meridional(
                k, j, north_ref, own_ref, south_ref
            )
        hi, lo = split(panel_ref[k].reshape(rows * cols, width))
        turn = (((0,), (0,)), ((), ()))
        cross = lax.dot_general(hi, lo, turn, preferred_element_type=F32)
        main = lax.dot_general(hi, hi, turn, preferred_element_type=F32)
        return carry[0] + main, carry[1] + cross

    zero = jnp.zeros((width, width), F32)
    main, cross = lax.fori_loop(0, levels, level_pass, (zero, zero))
    gram_ref[...] = main + (cross + cross.T)


BLOCK = 8


def split3(x):
    hi, rest = split(x)
    mid = (x - hi.astype(F32)).astype(BF16)
    lo = (x - hi.astype(F32) - mid.astype(F32)).astype(BF16)
    return hi, mid, lo


def factor_kernel(gram_ref, low_ref, high_ref, q_ref, rfac_ref, both_ref, inv_ref, *, scale):
    width = gram_ref.shape[0]
    down = lax.broadcasted_iota(jnp.int32, (BLOCK, width), 0)
    along = lax.broadcasted_iota(jnp.int32, (BLOCK, width), 1)
    rows_all = lax.broadcasted_iota(jnp.int32, (width, width), 0)
    cols_all = lax.broadcasted_iota(jnp.int32, (width, width), 1)
    both_ref[:, :width] = gram_ref[...] * scale
    both_ref[:, width:] = jnp.where(rows_all == cols_all, 1.0, 0.0)
    for start in range(0, width, BLOCK):
        block = both_ref[start : start + BLOCK, :]
        a, w = block[:, :width], block[:, width:]
        a = jnp.where(along >= start, a, 0.0)
        lanes = [
            jnp.broadcast_to(a[:, start + b : start + b + 1], (BLOCK, width)) for b in range(BLOCK)
        ]
        roots = jnp.zeros((BLOCK, width), F32)
        for p in range(BLOCK):
            pivot = jnp.broadcast_to(lanes[p][p : p + 1], (BLOCK, width))
            root = lax.rsqrt(pivot)
            root = root * (1.5 - 0.5 * pivot * root * root)
            roots = jnp.where(down == p, root, roots)
            if p == BLOCK - 1:
                break
            f = jnp.where(down > p, lanes[p] * (root * root), 0.0)
            for b in range(p + 1, BLOCK):
                lanes[b] = lanes[b] - f * lanes[b][p : p + 1]
            a = a - f * a[p : p + 1]
            w = w - f * w[p : p + 1]
        u = jnp.where(along >= down + start, a * roots, 0.0)
        w = w * roots
        rfac_ref[start : start + BLOCK, :] = u
        inv_ref[start : start + BLOCK, :] = w
        if start + BLOCK < width:
            right = jnp.concatenate([u, w], axis=1)
            uh, um, ul = split3(u)
            rh, rm, rl = split3(right)
            left = jnp.concatenate([uh, uh, um, uh, ul, um], axis=0)
            right = jnp.concatenate([rh, rm, rh, rl, rh, rm], axis=0)
            both_ref[...] -= lax.dot_general(
                left, right, (((0,), (0,)), ((), ())), preferred_element_type=F32
            )
    ih, il = split(inv_ref[...])
    turn = (((1,), (1,)), ((), ()))
    part = low_ref.shape[0]
    for src_ref, base in ((low_ref, 0), (high_ref, part)):
        for k in range(part):
            hi, lo = split(src_ref[k])
            q_ref[base + k] = lax.dot_general(hi, ih, turn, preferred_element_type=F32) + (
                lax.dot_general(lo, ih, turn, preferred_element_type=F32)
                + lax.dot_general(hi, il, turn, preferred_element_type=F32)
            )


def steps(axis_size, fn):
    return [(i, fn(i)) for i in range(axis_size)]


def core_swap(n):
    return steps(n, lambda l: l ^ 1)


def ring_swap(n, odd):
    chips = n // 2

    def partner(l):
        y = l >> 1
        y = chips - 1 - y if odd else y ^ 1
        return (y << 1) | (l & 1)

    return steps(n, partner)


def level_sum(other, first, second):
    n = lax.axis_size("lev")
    core, even, odd = core_swap(n), ring_swap(n, False), ring_swap(n, True)

    def send(x, perm):
        return lax.ppermute(x, "lev", perm)

    def reduced(x, perm):
        mid = x.shape[0] // 2
        return x[mid:] + send(x[:mid], perm)

    def gathered(x, perm):
        return jnp.concatenate([send(x, perm), x])

    mine = send(other, core)
    mid = first.shape[0]
    p, q = first + mine[:mid], second + mine[mid:]
    p, q = reduced(p, even), reduced(q, odd)
    p, q = reduced(p, odd), reduced(q, even)
    p, q = gathered(p, odd), gathered(q, even)
    p, q = gathered(p, even), gathered(q, odd)
    own = jnp.concatenate([p, q])
    return send(own, core), own


def own_order():
    l = lax.axis_index("lev")
    y, c = l >> 1, l & 1
    first, second = (y ^ (y >> 1)) & 1, y >> 1
    keep = (1 - c) << 4
    one = keep | ((1 - first) << 2) | ((1 - second) << 1)
    two = keep | ((1 - second) << 2) | ((1 - first) << 1)
    return jnp.stack([one, two]).astype(jnp.int32)


def gram_sum(x):
    n, m = lax.axis_size("lev"), lax.axis_size("tile")

    def quad(x, axis, size, shift):
        a, b, c = (lax.ppermute(x, axis, steps(size, lambda i, j=j: i ^ (j << shift))) for j in (1, 2, 3))
        return (x + a) + (b + c)

    x = x + lax.ppermute(x, "lev", core_swap(n))
    x = quad(x, "lev", n, 1)
    x = quad(x, "tile", m, 3)
    x = quad(x, "tile", m, 0)
    return x + lax.ppermute(x, "tile", steps(m, lambda t: t ^ 4))


def from_neighbours(lower_piece, upper_piece, axis):
    count = lax.axis_size(axis)
    below = lax.ppermute(lower_piece, axis, [(i, i + 1) for i in range(count - 1)])
    above = lax.ppermute(upper_piece, axis, [(i + 1, i) for i in range(count - 1)])
    return below, above


PARAMS = pltpu.CompilerParams(vmem_limit_bytes=40 << 20)


def shape(*dims, dtype=F32):
    return jax.ShapeDtypeStruct(dims, dtype)


SMALL = pl.BlockSpec(memory_space=pltpu.SMEM)
WHOLE = pl.BlockSpec(memory_space=pltpu.VMEM)


def shards(probes, sigma, obs_count, obs_cell, obs_rinv, obs_jac):
    levels, rows, cols, width = probes.shape
    cells = rows * cols
    rim = REACH * cols
    bins, slots = obs_cell.shape
    total = bins * slots
    part = levels // 2
    mhi, mlo = split(jnp.asarray(ring_matrix(cols, 256)))
    band = jnp.asarray(level_matrix(levels, 3 * levels))
    order = own_order()

    def field(n):
        return (shape(n, cells, width), shape(n, rim, width), shape(n, rim, width))

    across, head, tail = pl.pallas_call(
        zonal_kernel, out_shape=field(levels), compiler_params=PARAMS, name="zonal"
    )(probes.reshape(levels, cells, width), mhi, mlo)
    north, south = from_neighbours(tail, head, "tile")

    live = jnp.arange(slots, dtype=jnp.int32)[None, :] < obs_count[:, None]
    rinv = jnp.where(live, obs_rinv, 0.0)
    packed = jnp.concatenate([obs_jac, rinv[:, None], obs_cell.astype(F32)[:, None]], axis=1)
    sent = lax.all_to_all(packed, "tile", split_axis=0, concat_axis=0, tiled=True)
    seen, pick, place = pl.pallas_call(
        prepare_kernel,
        out_shape=(
            shape(bins, levels, slots),
            shape(total, cells, dtype=BF16),
            shape(cells, total, dtype=BF16),
        ),
        in_specs=[SMALL, WHOLE, WHOLE],
        compiler_params=PARAMS,
        name="prepare",
    )(order, sent, sigma.reshape(levels, cells))
    below, above = from_neighbours(seen, seen, "lev")

    grid4 = (levels, rows, cols, width)
    rim4 = (levels, REACH, cols, width)
    other, first, second, turned = pl.pallas_call(
        column_kernel,
        out_shape=(
            shape(total // 2, width),
            shape(total // 4, width),
            shape(total // 4, width),
            shape(total, 2 * levels),
        ),
        in_specs=[SMALL] + [WHOLE] * 9,
        scratch_shapes=[pltpu.VMEM(grid4, F32), pltpu.VMEM((bins, levels, slots), F32)],
        compiler_params=PARAMS,
        name="column",
    )(
        order, north.reshape(rim4), across.reshape(grid4), south.reshape(rim4),
        sent, below, seen, above, band, pick,
    )
    other, own = level_sum(other, first, second)

    grid4 = (part, rows, cols, width)
    rim4 = (part, REACH, cols, width)
    fields = []
    for h in range(2):

        def adjoint_body(*refs, base=part * h):
            adjoint_kernel(*refs, base=base)

        across, head, tail = pl.pallas_call(
            adjoint_body,
            out_shape=field(part),
            scratch_shapes=[pltpu.VMEM((total, width), F32)],
            compiler_params=PARAMS,
            name="adjoint" + str(h),
        )(other, own, turned, place, mhi, mlo)
        north, south = from_neighbours(tail, head, "tile")
        fields.append((north.reshape(rim4), across.reshape(grid4), south.reshape(rim4)))
    panels, gram = [], None
    for h in range(2):
        specs = [pl.BlockSpec(x.shape, lambda i: (0, 0, 0, 0)) for x in fields[h]]
        panel, piece = pl.pallas_call(
            panel_kernel,
            grid=(1,),
            in_specs=specs + [pl.BlockSpec(grid4, lambda i, h=h: (h, 0, 0, 0))],
            out_specs=[
                pl.BlockSpec(grid4, lambda i: (0, 0, 0, 0)),
                pl.BlockSpec((width, width), lambda i: (0, 0)),
            ],
            out_shape=(shape(*grid4), shape(width, width)),
            compiler_params=PARAMS,
            name="panel" + str(h),
        )(*fields[h], probes)
        panels.append(panel.reshape(part, cells, width))
        gram = piece if gram is None else gram + piece
    gram = gram_sum(gram)
    whole = cells * levels * lax.axis_size("tile") * lax.axis_size("lev")

    def factor_body(*refs):
        factor_kernel(*refs, scale=1.0 / whole)

    qpanel, rfac = pl.pallas_call(
        factor_body,
        out_shape=(shape(levels, cells, width), shape(width, width)),
        scratch_shapes=[pltpu.VMEM((width, 2 * width), F32), pltpu.VMEM((width, width), F32)],
        compiler_params=PARAMS,
        name="factor",
    )(gram, *panels)
    return (qpanel.reshape(probes.shape), rfac)


def solution(mesh):
    in_specs = (
        P("lev", "tile", None, None),
        P("lev", "tile", None),
        P("tile"),
        P("tile", None),
        P("tile", None),
        P("tile", "lev", None),
    )
    out_specs = (P("lev", "tile", None, None), P())
    return jax.shard_map(shards, mesh=mesh, in_specs=in_specs, out_specs=out_specs, check_vma=False)
```

```python
import math

import jax
import jax.numpy as jnp
import numpy as np
from jax import lax
from jax.experimental import pallas as pl
from jax.experimental.pallas import tpu as pltpu
from jax.sharding import PartitionSpec as P

F32 = jnp.float32
BF16 = jnp.bfloat16
REACH = 7


def tap_weights():
    profile = [math.exp(-(offset / 6.0) * (offset / 6.0)) for offset in range(-7, 8)]
    scaling = math.sqrt(sum((element * element for element in profile)))
    return [element / scaling for element in profile]


TAPS = tap_weights()


def ring_matrix(cols, size):
    one = np.zeros((cols, cols), np.float64)
    for c in range(cols):
        for d in range(-REACH, REACH + 1):
            one[c, (c + d) % cols] += TAPS[d + REACH]
    return np.kron(np.eye(size // cols), one).astype(np.float32)


def level_matrix(levels, width):
    band = np.zeros((levels, width), np.float32)
    for k in range(levels):
        for d in range(-REACH, REACH + 1):
            band[k, levels + k + d] = TAPS[d + REACH]
    return band


def split(x):
    hi = x.astype(BF16)
    return hi, (x - hi.astype(F32)).astype(BF16)


def dot(a, b):
    return jnp.dot(a, b, preferred_element_type=F32)


def zonal(mhi, mlo, pair):
    outs = []
    for h in range(2):
        hi, lo = split(pair[256 * h : 256 * h + 256])
        outs.append(dot(mhi, hi) + (dot(mlo, hi) + dot(mhi, lo)))
    return jnp.concatenate(outs, axis=0)


def put_zonal(x, kp, rim, out_ref, head_ref, tail_ref):
    cells = x.shape[0]
    for j in range(2):
        part = x[:, 128 * j : 128 * j + 128]
        out_ref[2 * kp + j] = part
        head_ref[2 * kp + j] = part[:rim]
        tail_ref[2 * kp + j] = part[cells - rim :]


def zonal_kernel(field_ref, mhi_ref, mlo_ref, out_ref, head_ref, tail_ref):
    levels = field_ref.shape[0]
    rim = head_ref.shape[1]
    mhi, mlo = mhi_ref[...], mlo_ref[...]
    for kp in range(levels // 2):
        pair = jnp.concatenate([field_ref[2 * kp], field_ref[2 * kp + 1]], axis=1)
        put_zonal(zonal(mhi, mlo, pair), kp, rim, out_ref, head_ref, tail_ref)


def meridional(k, j, north_ref, own_ref, south_ref):
    cut = pl.ds(8 * j, 8)
    rows = jnp.concatenate(
        [north_ref[k, :, cut, :], own_ref[k, :, cut, :], south_ref[k, :, cut, :]], axis=0
    )
    length = own_ref.shape[1]
    total = TAPS[REACH] * rows[REACH : REACH + length]
    for d in range(1, REACH + 1):
        total = total + TAPS[REACH + d] * (
            rows[REACH - d : REACH - d + length] + rows[REACH + d : REACH + d + length]
        )
    return total


CHUNK = 1024
GROUP = 256


def source_at(order_ref, position):
    return position ^ order_ref[(position >> 3) & 1]


def prepare_kernel(order_ref, sent_ref, sigma_ref, seen_ref, pick_ref, place_ref):
    levels, cells = sigma_ref.shape
    sources, _, slots = sent_ref.shape
    stacked = jnp.concatenate(split(sigma_ref[...]), axis=0)
    cell_down = lax.broadcasted_iota(jnp.int32, (cells, slots), 0).astype(F32)
    cell_along = lax.broadcasted_iota(jnp.int32, (slots, cells), 1).astype(F32)
    for s in range(sources):
        source = source_at(order_ref, s)
        here = sent_ref[source, levels + 1 : levels + 2]
        onehot = jnp.where(cell_down == here, 1.0, 0.0).astype(BF16)
        place_ref[:, slots * s : slots * s + slots] = onehot
        picked = dot(stacked, onehot)
        seen_ref[source] = sent_ref[source, :levels] * (picked[:levels] + picked[levels:])
        turned = jnp.broadcast_to(here, (8, slots)).T
        pick_ref[slots * s : slots * s + slots, :] = jnp.where(
            cell_along == turned[:, :1], 1.0, 0.0
        ).astype(BF16)


def column_kernel(
    order_ref, north_ref, own_ref, south_ref, sent_ref, below_ref, seen_ref, above_ref,
    band_ref, pick_ref,
    other_ref, first_ref, second_ref, turned_ref,
    w_ref, table_ref,
):
    levels, rows, cols, width = own_ref.shape
    cells = rows * cols
    sources, _, slots = sent_ref.shape
    total = sources * slots

    def level_pass(k, carry):
        for j in range(cols // 8):
            w_ref[k, :, pl.ds(8 * j, 8), :] = meridional(k, j, north_ref, own_ref, south_ref)
        return carry

    lax.fori_loop(0, levels, level_pass, 0)

    for s in range(0, sources, 4):
        stack = jnp.concatenate(
            [
                jnp.concatenate([below_ref[i], seen_ref[i], above_ref[i]], axis=0)
                for i in range(s, s + 4)
            ],
            axis=1,
        )
        spread = jnp.dot(
            band_ref[...], stack, precision=lax.Precision.HIGHEST, preferred_element_type=F32
        )
        for i in range(4):
            table_ref[s + i] = spread[:, slots * i : slots * i + slots]
    for s in range(sources):
        source = source_at(order_ref, s)
        at = slice(slots * s, slots * s + slots)
        turned_ref[at, :levels] = table_ref[source].T
        rinv = jnp.broadcast_to(sent_ref[source, levels : levels + 1], (8, slots))
        turned_ref[at, levels : 2 * levels] = rinv.T

    half = total // 2
    for kp in range(levels // 2):
        pair = jnp.concatenate(
            [w_ref[2 * kp].reshape(cells, width), w_ref[2 * kp + 1].reshape(cells, width)], axis=1
        )
        hi, lo = split(pair)
        for dst_ref, start in ((other_ref, 0), (first_ref, half), (second_ref, half + half // 2)):

            def chunk_pass(c, carry, dst_ref=dst_ref, start=start):
                to = pl.ds(pl.multiple_of(c * CHUNK, CHUNK), CHUNK)
                at = pl.ds(pl.multiple_of(start + c * CHUNK, CHUNK), CHUNK)
                pick = pick_ref[at, :]
                seen = dot(pick, hi) + dot(pick, lo)
                part = (
                    turned_ref[at, 2 * kp : 2 * kp + 1] * seen[:, :width]
                    + turned_ref[at, 2 * kp + 1 : 2 * kp + 2] * seen[:, width:]
                )
                if kp == 0:
                    dst_ref[to, :] = part
                else:
                    dst_ref[to, :] += part
                return carry

            lax.fori_loop(0, dst_ref.shape[0] // CHUNK, chunk_pass, 0)


def scattered(weighted_ref, turned_ref, place_ref, start, k):
    field = None
    for c in range(weighted_ref.shape[0] // CHUNK):
        at = slice(c * CHUNK, c * CHUNK + CHUNK)
        to = slice(start + c * CHUNK, start + c * CHUNK + CHUNK)
        weighted = weighted_ref[at, :]
        pair = jnp.concatenate(
            [turned_ref[to, k : k + 1] * weighted, turned_ref[to, k + 1 : k + 2] * weighted],
            axis=1,
        )
        hi, lo = split(pair)
        place = place_ref[:, to]
        part = dot(place, hi) + dot(place, lo)
        field = part if field is None else field + part
    return field


def own_kernel(own_ref, turned_ref, place_ref, field_ref, weighted_ref):
    half = own_ref.shape[0]
    weighted_ref[...] = own_ref[...] * turned_ref[half:, 8:9]
    for kp in range(field_ref.shape[0]):
        field_ref[kp] = scattered(weighted_ref, turned_ref, place_ref, half, 2 * kp)


def adjoint_kernel(
    other_ref, turned_ref, place_ref, field_ref, mhi_ref, mlo_ref,
    out_ref, head_ref, tail_ref,
    weighted_ref, *, base,
):
    levels = out_ref.shape[0]
    rim = head_ref.shape[1]
    half = other_ref.shape[0]
    weighted_ref[...] = other_ref[...] * turned_ref[:half, 8:9]
    mhi, mlo = mhi_ref[...], mlo_ref[...]
    for kp in range(levels // 2):
        k = base + 2 * kp
        field = field_ref[k // 2] + scattered(weighted_ref, turned_ref, place_ref, 0, k)
        put_zonal(zonal(mhi, mlo, field), kp, rim, out_ref, head_ref, tail_ref)


def panel_part(north_ref, own_ref, south_ref, probes_ref, panel_ref, base):
    levels, rows, cols, width = own_ref.shape

    def level_pass(k, carry):
        for j in range(cols // 8):
            cut = pl.ds(8 * j, 8)
            panel_ref[k, :, cut, :] = probes_ref[base + k, :, cut, :] + meridional(
                k, j, north_ref, own_ref, south_ref
            )
        hi, lo = split(panel_ref[k].reshape(rows * cols, width))
        turn = (((0,), (0,)), ((), ()))
        cross = lax.dot_general(hi, lo, turn, preferred_element_type=F32)
        main = lax.dot_general(hi, hi, turn, preferred_element_type=F32)
        return carry[0] + main, carry[1] + cross

    zero = jnp.zeros((width, width), F32)
    main, cross = lax.fori_loop(0, levels, level_pass, (zero, zero))
    return main + (cross + cross.T)


def panel_kernel(north_ref, own_ref, south_ref, probes_ref, panel_ref, gram_ref):
    gram_ref[...] = panel_part(north_ref, own_ref, south_ref, probes_ref, panel_ref, 0)


def panel_end_kernel(
    north_ref, own_ref, south_ref, probes_ref, before_ref, panel_ref, packed_ref, *, base
):
    gram = before_ref[...] + panel_part(
        north_ref, own_ref, south_ref, probes_ref, panel_ref, base
    )
    packed_ref[...] = packed_gram(gram)


def packed_gram(gram):
    width = gram.shape[0]
    mid = width // 2
    row = lax.broadcasted_iota(jnp.int32, (mid, width), 0)
    col = lax.broadcasted_iota(jnp.int32, (mid, width), 1)
    top, low = gram[:mid], pltpu.roll(gram[mid:], mid, axis=1)
    body = jnp.where(col >= row, top, low)
    diag = jnp.sum(jnp.where(col == row, low, 0.0), axis=0, keepdims=True)
    return jnp.concatenate([body, jnp.broadcast_to(diag, (8, width))], axis=0)


def unpacked_gram(packed):
    width = packed.shape[1]
    mid = width // 2
    row = lax.broadcasted_iota(jnp.int32, (mid, width), 0)
    col = lax.broadcasted_iota(jnp.int32, (mid, width), 1)
    body = packed[:mid]
    turned = jnp.concatenate([body, body], axis=0).T
    top = jnp.where(col >= row, body, turned[:mid])
    far = col - mid
    body, flip = pltpu.roll(body, mid, axis=1), pltpu.roll(turned[:mid], mid, axis=1)
    diag = pltpu.roll(packed[mid:], mid, axis=1)[:1]
    corner = jnp.where(row > far, body, jnp.where(row < far, flip, diag))
    return jnp.concatenate([top, jnp.where(col < mid, turned[mid:], corner)], axis=0)


BLOCK = 8


def split3(x):
    hi, rest = split(x)
    mid = (x - hi.astype(F32)).astype(BF16)
    lo = (x - hi.astype(F32) - mid.astype(F32)).astype(BF16)
    return hi, mid, lo


def factor_kernel(gram_ref, low_ref, high_ref, q_ref, rfac_ref, both_ref, inv_ref, *, scale):
    width = gram_ref.shape[1]
    down = lax.broadcasted_iota(jnp.int32, (BLOCK, width), 0)
    along = lax.broadcasted_iota(jnp.int32, (BLOCK, width), 1)
    rows_all = lax.broadcasted_iota(jnp.int32, (width, width), 0)
    cols_all = lax.broadcasted_iota(jnp.int32, (width, width), 1)
    both_ref[:, :width] = unpacked_gram(gram_ref[...]) * scale
    both_ref[:, width:] = jnp.where(rows_all == cols_all, 1.0, 0.0)
    for start in range(0, width, BLOCK):
        block = both_ref[start : start + BLOCK, :]
        a, w = block[:, :width], block[:, width:]
        a = jnp.where(along >= start, a, 0.0)
        lanes = [
            jnp.broadcast_to(a[:, start + b : start + b + 1], (BLOCK, width)) for b in range(BLOCK)
        ]
        roots = jnp.zeros((BLOCK, width), F32)
        for p in range(BLOCK):
            pivot = jnp.broadcast_to(lanes[p][p : p + 1], (BLOCK, width))
            root = lax.rsqrt(pivot)
            root = root * (1.5 - 0.5 * pivot * root * root)
            roots = jnp.where(down == p, root, roots)
            if p == BLOCK - 1:
                break
            f = jnp.where(down > p, lanes[p] * (root * root), 0.0)
            for b in range(p + 1, BLOCK):
                lanes[b] = lanes[b] - f * lanes[b][p : p + 1]
            a = a - f * a[p : p + 1]
            w = w - f * w[p : p + 1]
        u = jnp.where(along >= down + start, a * roots, 0.0)
        w = w * roots
        rfac_ref[start : start + BLOCK, :] = u
        inv_ref[start : start + BLOCK, :] = w
        if start + BLOCK < width:
            right = jnp.concatenate([u, w], axis=1)
            uh, um, ul = split3(u)
            rh, rm, rl = split3(right)
            left = jnp.concatenate([uh, uh, um, uh, ul, um], axis=0)
            right = jnp.concatenate([rh, rm, rh, rl, rh, rm], axis=0)
            both_ref[...] -= lax.dot_general(
                left, right, (((0,), (0,)), ((), ())), preferred_element_type=F32
            )
    ih, il = split(inv_ref[...])
    turn = (((1,), (1,)), ((), ()))
    for src_ref, base in ((low_ref, 0), (high_ref, low_ref.shape[0])):
        for k in range(src_ref.shape[0]):
            hi, lo = split(src_ref[k])
            q_ref[base + k] = lax.dot_general(hi, ih, turn, preferred_element_type=F32) + (
                lax.dot_general(lo, ih, turn, preferred_element_type=F32)
                + lax.dot_general(hi, il, turn, preferred_element_type=F32)
            )


def steps(axis_size, fn):
    return [(i, fn(i)) for i in range(axis_size)]


def core_swap(n):
    return steps(n, lambda l: l ^ 1)


def ring_swap(n, odd):
    chips = n // 2

    def partner(l):
        y = l >> 1
        y = chips - 1 - y if odd else y ^ 1
        return (y << 1) | (l & 1)

    return steps(n, partner)


def level_sum(other, first, second):
    n = lax.axis_size("lev")
    core, even, odd = core_swap(n), ring_swap(n, False), ring_swap(n, True)

    def send(x, perm):
        return lax.ppermute(x, "lev", perm)

    def reduced(x, perm):
        mid = x.shape[0] // 2
        return x[mid:] + send(x[:mid], perm)

    def gathered(x, perm):
        return jnp.concatenate([send(x, perm), x])

    def summed(x, perm):
        return x + send(x, perm)

    together = lax.optimization_barrier
    mine = send(other, core)
    mid = first.shape[0]
    p, q = first + mine[:mid], second + mine[mid:]
    p, q = together((reduced(p, even), reduced(q, odd)))
    p, q = together((summed(p, odd), summed(q, even)))
    own = jnp.concatenate([gathered(p, even), gathered(q, odd)])
    return send(own, core), own


def own_order():
    l = lax.axis_index("lev")
    y, c = l >> 1, l & 1
    first, second = (y ^ (y >> 1)) & 1, y >> 1
    keep = (1 - c) << 4
    one = keep | ((1 - first) << 2)
    two = keep | ((1 - second) << 2)
    return jnp.stack([one, two]).astype(jnp.int32)


def gram_sum(x):
    n, m = lax.axis_size("lev"), lax.axis_size("tile")

    for perm in (core_swap(n), ring_swap(n, False), ring_swap(n, True)):
        x = x + lax.ppermute(x, "lev", perm)
    for fn in (
        lambda t: t ^ 1,
        lambda t: (t & ~3) | (3 - (t & 3)),
        lambda t: (t & ~7) | (7 - (t & 7)),
        lambda t: t ^ 8,
        lambda t: (t & 7) | ((3 - (t >> 3)) << 3),
    ):
        x = x + lax.ppermute(x, "tile", steps(m, fn))
    return x


def from_neighbours(lower_piece, upper_piece, axis):
    count = lax.axis_size(axis)
    below = lax.ppermute(lower_piece, axis, [(i, i + 1) for i in range(count - 1)])
    above = lax.ppermute(upper_piece, axis, [(i + 1, i) for i in range(count - 1)])
    return below, above


PARAMS = pltpu.CompilerParams(vmem_limit_bytes=40 << 20)


def shape(*dims, dtype=F32):
    return jax.ShapeDtypeStruct(dims, dtype)


PARTS = ((0, 4), (4, 4))
SMALL = pl.BlockSpec(memory_space=pltpu.SMEM)
WHOLE = pl.BlockSpec(memory_space=pltpu.VMEM)


def shards(probes, sigma, obs_count, obs_cell, obs_rinv, obs_jac):
    levels, rows, cols, width = probes.shape
    cells = rows * cols
    rim = REACH * cols
    bins, slots = obs_cell.shape
    total = bins * slots
    mhi, mlo = split(jnp.asarray(ring_matrix(cols, 256)))
    band = jnp.asarray(level_matrix(levels, 3 * levels))
    order = own_order()

    def field(n):
        return (shape(n, cells, width), shape(n, rim, width), shape(n, rim, width))

    across, head, tail = pl.pallas_call(
        zonal_kernel, out_shape=field(levels), compiler_params=PARAMS, name="zonal"
    )(probes.reshape(levels, cells, width), mhi, mlo)

    live = jnp.arange(slots, dtype=jnp.int32)[None, :] < obs_count[:, None]
    rinv = jnp.where(live, obs_rinv, 0.0)
    packed = jnp.concatenate([obs_jac, rinv[:, None], obs_cell.astype(F32)[:, None]], axis=1)
    sent = lax.all_to_all(packed, "tile", split_axis=0, concat_axis=0, tiled=True)
    sent, head, tail = lax.optimization_barrier((sent, head, tail))
    north, south = from_neighbours(tail, head, "tile")
    seen, pick, place = pl.pallas_call(
        prepare_kernel,
        out_shape=(
            shape(bins, levels, slots),
            shape(total, cells, dtype=BF16),
            shape(cells, total, dtype=BF16),
        ),
        in_specs=[SMALL, WHOLE, WHOLE],
        compiler_params=PARAMS,
        name="prepare",
    )(order, sent, sigma.reshape(levels, cells))
    below, above = from_neighbours(seen, seen, "lev")

    grid4 = (levels, rows, cols, width)
    rim4 = (levels, REACH, cols, width)
    other, first, second, turned = pl.pallas_call(
        column_kernel,
        out_shape=(
            shape(total // 2, width),
            shape(total // 4, width),
            shape(total // 4, width),
            shape(total, 2 * levels),
        ),
        in_specs=[SMALL] + [WHOLE] * 9,
        scratch_shapes=[pltpu.VMEM(grid4, F32), pltpu.VMEM((bins, levels, slots), F32)],
        compiler_params=PARAMS,
        name="column",
    )(
        order, north.reshape(rim4), across.reshape(grid4), south.reshape(rim4),
        sent, below, seen, above, band, pick,
    )
    other, own = level_sum(other, first, second)

    field_own = pl.pallas_call(
        own_kernel,
        out_shape=shape(levels // 2, cells, 2 * width),
        scratch_shapes=[pltpu.VMEM((total // 2, width), F32)],
        compiler_params=PARAMS,
        name="own",
    )(own, turned, place)
    fields = []
    for base, n in PARTS:

        def adjoint_body(*refs, base=base):
            adjoint_kernel(*refs, base=base)

        if fields:
            other, _ = lax.optimization_barrier((other, fields[0][1]))
        across, head, tail = pl.pallas_call(
            adjoint_body,
            out_shape=field(n),
            scratch_shapes=[pltpu.VMEM((total // 2, width), F32)],
            compiler_params=PARAMS,
            name="adjoint" + str(base),
        )(other, turned, place, field_own, mhi, mlo)
        north, south = from_neighbours(tail, head, "tile")
        rim4 = (n, REACH, cols, width)
        fields.append(
            (north.reshape(rim4), across.reshape(n, rows, cols, width), south.reshape(rim4))
        )

    base, n = PARTS[0]
    first, gram = pl.pallas_call(
        panel_kernel,
        out_shape=(shape(n, rows, cols, width), shape(width, width)),
        compiler_params=PARAMS,
        name="panel",
    )(*fields[0], probes)
    base, n = PARTS[1]

    def end_body(*refs):
        panel_end_kernel(*refs, base=base)

    second, gram = pl.pallas_call(
        end_body,
        out_shape=(shape(n, rows, cols, width), shape(width // 2 + 8, width)),
        compiler_params=PARAMS,
        name="panel_end",
    )(*fields[1], probes, gram)
    panels = [p.reshape(-1, cells, width) for p in (first, second)]
    gram = gram_sum(gram)
    whole = cells * levels * lax.axis_size("tile") * lax.axis_size("lev")

    def factor_body(*refs):
        factor_kernel(*refs, scale=1.0 / whole)

    qpanel, rfac = pl.pallas_call(
        factor_body,
        out_shape=(shape(levels, cells, width), shape(width, width)),
        scratch_shapes=[pltpu.VMEM((width, 2 * width), F32), pltpu.VMEM((width, width), F32)],
        compiler_params=PARAMS,
        name="factor",
    )(gram, *panels)
    return (qpanel.reshape(probes.shape), rfac)


def solution(mesh):
    in_specs = (
        P("lev", "tile", None, None),
        P("lev", "tile", None),
        P("tile"),
        P("tile", None),
        P("tile", None),
        P("tile", "lev", None),
    )
    out_specs = (P("lev", "tile", None, None), P())
    return jax.shard_map(shards, mesh=mesh, in_specs=in_specs, out_specs=out_specs, check_vma=False)
```

```python
import math

import jax
import jax.numpy as jnp
import numpy as np
from jax import lax
from jax.experimental import pallas as pl
from jax.experimental.pallas import tpu as pltpu
from jax.sharding import PartitionSpec as P

F32 = jnp.float32
BF16 = jnp.bfloat16
REACH = 7


def tap_weights():
    profile = [math.exp(-(offset / 6.0) * (offset / 6.0)) for offset in range(-7, 8)]
    scaling = math.sqrt(sum((element * element for element in profile)))
    return [element / scaling for element in profile]


TAPS = tap_weights()


def ring_matrix(cols, size):
    one = np.zeros((cols, cols), np.float64)
    for c in range(cols):
        for d in range(-REACH, REACH + 1):
            one[c, (c + d) % cols] += TAPS[d + REACH]
    return np.kron(np.eye(size // cols), one).astype(np.float32)


def level_matrix(levels, width):
    band = np.zeros((levels, width), np.float32)
    for k in range(levels):
        for d in range(-REACH, REACH + 1):
            band[k, levels + k + d] = TAPS[d + REACH]
    return band


def split(x):
    hi = x.astype(BF16)
    return hi, (x - hi.astype(F32)).astype(BF16)


def dot(a, b):
    return jnp.dot(a, b, preferred_element_type=F32)


def zonal(mhi, mlo, pair):
    outs = []
    for h in range(2):
        hi, lo = split(pair[256 * h : 256 * h + 256])
        outs.append(dot(mhi, hi) + (dot(mlo, hi) + dot(mhi, lo)))
    return jnp.concatenate(outs, axis=0)


def put_zonal(x, kp, rim, out_ref, head_ref, tail_ref):
    cells = x.shape[0]
    for j in range(2):
        part = x[:, 128 * j : 128 * j + 128]
        out_ref[2 * kp + j] = part
        head_ref[2 * kp + j] = part[:rim]
        tail_ref[2 * kp + j] = part[cells - rim :]


def zonal_kernel(field_ref, mhi_ref, mlo_ref, out_ref, head_ref, tail_ref, *, base):
    rim = head_ref.shape[1]
    mhi, mlo = mhi_ref[...], mlo_ref[...]
    for kp in range(out_ref.shape[0] // 2):
        k = base + 2 * kp
        pair = jnp.concatenate([field_ref[k], field_ref[k + 1]], axis=1)
        put_zonal(zonal(mhi, mlo, pair), kp, rim, out_ref, head_ref, tail_ref)


def pack_kernel(count_ref, cell_ref, rinv_ref, jac_ref, packed_ref):
    bins, levels, slots = jac_ref.shape
    slot = lax.broadcasted_iota(jnp.int32, (1, slots), 1)
    for s in range(bins):
        packed_ref[s, :levels] = jac_ref[s]
        live = slot < count_ref[s]
        packed_ref[s, levels : levels + 1] = jnp.where(live, rinv_ref[s : s + 1], 0.0)
        packed_ref[s, levels + 1 : levels + 2] = cell_ref[s : s + 1].astype(F32)


def meridional(k, j, north_ref, own_ref, south_ref):
    cut = pl.ds(8 * j, 8)
    rows = jnp.concatenate(
        [north_ref[k, :, cut, :], own_ref[k, :, cut, :], south_ref[k, :, cut, :]], axis=0
    )
    length = own_ref.shape[1]
    total = TAPS[REACH] * rows[REACH : REACH + length]
    for d in range(1, REACH + 1):
        total = total + TAPS[REACH + d] * (
            rows[REACH - d : REACH - d + length] + rows[REACH + d : REACH + d + length]
        )
    return total


CHUNK = 1024
GROUP = 256


def source_at(order_ref, position):
    return position ^ order_ref[(position >> 3) & 1]


def prepare_kernel(order_ref, sent_ref, sigma_ref, seen_ref, pick_ref, place_ref):
    levels, cells = sigma_ref.shape
    sources, _, slots = sent_ref.shape
    stacked = jnp.concatenate(split(sigma_ref[...]), axis=0)
    cell_down = lax.broadcasted_iota(jnp.int32, (cells, slots), 0).astype(F32)
    cell_along = lax.broadcasted_iota(jnp.int32, (slots, cells), 1).astype(F32)
    for s in range(sources):
        source = source_at(order_ref, s)
        here = sent_ref[source, levels + 1 : levels + 2]
        onehot = jnp.where(cell_down == here, 1.0, 0.0).astype(BF16)
        place_ref[:, slots * s : slots * s + slots] = onehot
        picked = dot(stacked, onehot)
        seen_ref[source] = sent_ref[source, :levels] * (picked[:levels] + picked[levels:])
        turned = jnp.broadcast_to(here, (8, slots)).T
        pick_ref[slots * s : slots * s + slots, :] = jnp.where(
            cell_along == turned[:, :1], 1.0, 0.0
        ).astype(BF16)


def smoothed_rows(north_ref, own_ref, south_ref, w_ref):
    levels, _, cols, _ = own_ref.shape

    def level_pass(k, carry):
        for j in range(cols // 8):
            w_ref[k, :, pl.ds(8 * j, 8), :] = meridional(k, j, north_ref, own_ref, south_ref)
        return carry

    lax.fori_loop(0, levels, level_pass, 0)


def level_pair(w_ref, kp):
    _, rows, cols, width = w_ref.shape
    flat = (rows * cols, width)
    return split(
        jnp.concatenate([w_ref[2 * kp].reshape(flat), w_ref[2 * kp + 1].reshape(flat)], axis=1)
    )


def observed(dst_ref, before_ref, turned_ref, pick_ref, pairs, base, start, skip):
    width = dst_ref.shape[1]

    def chunk_pass(c, carry):
        to = pl.ds(pl.multiple_of(c * CHUNK, CHUNK), CHUNK)
        at = pl.ds(pl.multiple_of(start + c * CHUNK, CHUNK), CHUNK)
        pick = pick_ref[at, :]
        total = None
        if before_ref is not None:
            total = before_ref[pl.ds(pl.multiple_of(skip + c * CHUNK, CHUNK), CHUNK), :]
        for kp, (hi, lo) in enumerate(pairs):
            k = base + 2 * kp
            seen = dot(pick, hi) + dot(pick, lo)
            part = (
                turned_ref[at, k : k + 1] * seen[:, :width]
                + turned_ref[at, k + 1 : k + 2] * seen[:, width:]
            )
            total = part if total is None else total + part
        dst_ref[to, :] = total
        return carry

    lax.fori_loop(0, dst_ref.shape[0] // CHUNK, chunk_pass, 0)


def column_kernel(
    order_ref, north_ref, near_ref, south_ref, sent_ref, below_ref, seen_ref, above_ref,
    band_ref, pick_ref,
    other_ref, own_ref, turned_ref,
    w_ref, table_ref,
):
    sources, levels, slots = seen_ref.shape
    smoothed_rows(north_ref, near_ref, south_ref, w_ref)
    for s in range(0, sources, 4):
        stack = jnp.concatenate(
            [
                jnp.concatenate([below_ref[i], seen_ref[i], above_ref[i]], axis=0)
                for i in range(s, s + 4)
            ],
            axis=1,
        )
        spread = jnp.dot(
            band_ref[...], stack, precision=lax.Precision.HIGHEST, preferred_element_type=F32
        )
        for i in range(4):
            table_ref[s + i] = spread[:, slots * i : slots * i + slots]
    for s in range(sources):
        source = source_at(order_ref, s)
        at = slice(slots * s, slots * s + slots)
        turned_ref[at, :levels] = table_ref[source].T
        rinv = jnp.broadcast_to(sent_ref[source, levels : levels + 1], (8, slots))
        turned_ref[at, levels : 2 * levels] = rinv.T
    pairs = [level_pair(w_ref, kp) for kp in range(w_ref.shape[0] // 2)]
    half = other_ref.shape[0]
    observed(other_ref, None, turned_ref, pick_ref, pairs, 0, 0, 0)
    observed(own_ref, None, turned_ref, pick_ref, pairs, 0, half, 0)


def column_other_kernel(
    north_ref, near_ref, south_ref, before_ref, turned_ref, pick_ref,
    other_ref, hi_ref, lo_ref,
    w_ref, *, base,
):
    smoothed_rows(north_ref, near_ref, south_ref, w_ref)
    pairs = []
    for kp in range(w_ref.shape[0] // 2):
        hi, lo = level_pair(w_ref, kp)
        hi_ref[kp], lo_ref[kp] = hi, lo
        pairs.append((hi, lo))
    observed(other_ref, before_ref, turned_ref, pick_ref, pairs, base, 0, 0)


def column_own_kernel(
    hi_ref, lo_ref, before_ref, turned_ref, pick_ref, first_ref, second_ref, *, base
):
    pairs = [(hi_ref[kp], lo_ref[kp]) for kp in range(hi_ref.shape[0])]
    half, n = before_ref.shape[0], first_ref.shape[0]
    observed(first_ref, before_ref, turned_ref, pick_ref, pairs, base, half, 0)
    observed(second_ref, before_ref, turned_ref, pick_ref, pairs, base, half + n, n)


def scattered(weighted_ref, turned_ref, place_ref, start, k):
    field = None
    for c in range(weighted_ref.shape[0] // CHUNK):
        at = slice(c * CHUNK, c * CHUNK + CHUNK)
        to = slice(start + c * CHUNK, start + c * CHUNK + CHUNK)
        weighted = weighted_ref[at, :]
        pair = jnp.concatenate(
            [turned_ref[to, k : k + 1] * weighted, turned_ref[to, k + 1 : k + 2] * weighted],
            axis=1,
        )
        hi, lo = split(pair)
        place = place_ref[:, to]
        part = dot(place, hi) + dot(place, lo)
        field = part if field is None else field + part
    return field


def own_kernel(own_ref, turned_ref, place_ref, field_ref, weighted_ref):
    half = own_ref.shape[0]
    weighted_ref[...] = own_ref[...] * turned_ref[half:, 8:9]
    for kp in range(field_ref.shape[0]):
        field_ref[kp] = scattered(weighted_ref, turned_ref, place_ref, half, 2 * kp)


def adjoint_kernel(
    other_ref, turned_ref, place_ref, field_ref, mhi_ref, mlo_ref,
    out_ref, head_ref, tail_ref,
    weighted_ref,
):
    rim = head_ref.shape[1]
    half = other_ref.shape[0]
    weighted_ref[...] = other_ref[...] * turned_ref[:half, 8:9]
    mhi, mlo = mhi_ref[...], mlo_ref[...]
    for kp in range(out_ref.shape[0] // 2):
        field = field_ref[kp] + scattered(weighted_ref, turned_ref, place_ref, 0, 2 * kp)
        put_zonal(zonal(mhi, mlo, field), kp, rim, out_ref, head_ref, tail_ref)


def adjoint_end_kernel(
    other_ref, own_ref, turned_ref, place_ref, mhi_ref, mlo_ref,
    out_ref, head_ref, tail_ref,
    one_ref, two_ref, *, base,
):
    rim = head_ref.shape[1]
    half = other_ref.shape[0]
    one_ref[...] = other_ref[...] * turned_ref[:half, 8:9]
    two_ref[...] = own_ref[...] * turned_ref[half:, 8:9]
    mhi, mlo = mhi_ref[...], mlo_ref[...]
    for kp in range(out_ref.shape[0] // 2):
        k = base + 2 * kp
        field = scattered(one_ref, turned_ref, place_ref, 0, k)
        field = field + scattered(two_ref, turned_ref, place_ref, half, k)
        put_zonal(zonal(mhi, mlo, field), kp, rim, out_ref, head_ref, tail_ref)


def panel_part(north_ref, own_ref, south_ref, probes_ref, panel_ref, base):
    levels, rows, cols, width = own_ref.shape

    def level_pass(k, carry):
        for j in range(cols // 8):
            cut = pl.ds(8 * j, 8)
            panel_ref[k, :, cut, :] = probes_ref[base + k, :, cut, :] + meridional(
                k, j, north_ref, own_ref, south_ref
            )
        hi, lo = split(panel_ref[k].reshape(rows * cols, width))
        turn = (((0,), (0,)), ((), ()))
        cross = lax.dot_general(hi, lo, turn, preferred_element_type=F32)
        main = lax.dot_general(hi, hi, turn, preferred_element_type=F32)
        return carry[0] + main, carry[1] + cross

    zero = jnp.zeros((width, width), F32)
    main, cross = lax.fori_loop(0, levels, level_pass, (zero, zero))
    return main + (cross + cross.T)


def panel_kernel(north_ref, own_ref, south_ref, probes_ref, panel_ref, gram_ref):
    gram_ref[...] = panel_part(north_ref, own_ref, south_ref, probes_ref, panel_ref, 0)


def panel_end_kernel(
    north_ref, own_ref, south_ref, probes_ref, before_ref, panel_ref, packed_ref, *, base
):
    gram = before_ref[...] + panel_part(
        north_ref, own_ref, south_ref, probes_ref, panel_ref, base
    )
    packed_ref[...] = packed_gram(gram)


def packed_gram(gram):
    width = gram.shape[0]
    mid = width // 2
    row = lax.broadcasted_iota(jnp.int32, (mid, width), 0)
    col = lax.broadcasted_iota(jnp.int32, (mid, width), 1)
    top, low = gram[:mid], pltpu.roll(gram[mid:], mid, axis=1)
    body = jnp.where(col >= row, top, low)
    diag = jnp.sum(jnp.where(col == row, low, 0.0), axis=0, keepdims=True)
    return jnp.concatenate([body, jnp.broadcast_to(diag, (8, width))], axis=0)


def unpacked_gram(packed):
    width = packed.shape[1]
    mid = width // 2
    row = lax.broadcasted_iota(jnp.int32, (mid, width), 0)
    col = lax.broadcasted_iota(jnp.int32, (mid, width), 1)
    body = packed[:mid]
    turned = jnp.concatenate([body, body], axis=0).T
    top = jnp.where(col >= row, body, turned[:mid])
    far = col - mid
    body, flip = pltpu.roll(body, mid, axis=1), pltpu.roll(turned[:mid], mid, axis=1)
    diag = pltpu.roll(packed[mid:], mid, axis=1)[:1]
    corner = jnp.where(row > far, body, jnp.where(row < far, flip, diag))
    return jnp.concatenate([top, jnp.where(col < mid, turned[mid:], corner)], axis=0)


BLOCK = 8


def split3(x):
    hi, rest = split(x)
    mid = (x - hi.astype(F32)).astype(BF16)
    lo = (x - hi.astype(F32) - mid.astype(F32)).astype(BF16)
    return hi, mid, lo


def factor_kernel(gram_ref, low_ref, high_ref, q_ref, rfac_ref, both_ref, inv_ref, *, scale):
    width = gram_ref.shape[1]
    down = lax.broadcasted_iota(jnp.int32, (BLOCK, width), 0)
    along = lax.broadcasted_iota(jnp.int32, (BLOCK, width), 1)
    rows_all = lax.broadcasted_iota(jnp.int32, (width, width), 0)
    cols_all = lax.broadcasted_iota(jnp.int32, (width, width), 1)
    both_ref[:, :width] = unpacked_gram(gram_ref[...]) * scale
    both_ref[:, width:] = jnp.where(rows_all == cols_all, 1.0, 0.0)
    for start in range(0, width, BLOCK):
        block = both_ref[start : start + BLOCK, :]
        a, w = block[:, :width], block[:, width:]
        a = jnp.where(along >= start, a, 0.0)
        lanes = [
            jnp.broadcast_to(a[:, start + b : start + b + 1], (BLOCK, width)) for b in range(BLOCK)
        ]
        roots = jnp.zeros((BLOCK, width), F32)
        for p in range(BLOCK):
            pivot = jnp.broadcast_to(lanes[p][p : p + 1], (BLOCK, width))
            root = lax.rsqrt(pivot)
            root = root * (1.5 - 0.5 * pivot * root * root)
            roots = jnp.where(down == p, root, roots)
            if p == BLOCK - 1:
                break
            f = jnp.where(down > p, lanes[p] * (root * root), 0.0)
            for b in range(p + 1, BLOCK):
                lanes[b] = lanes[b] - f * lanes[b][p : p + 1]
            a = a - f * a[p : p + 1]
            w = w - f * w[p : p + 1]
        u = jnp.where(along >= down + start, a * roots, 0.0)
        w = w * roots
        rfac_ref[start : start + BLOCK, :] = u
        inv_ref[start : start + BLOCK, :] = w
        if start + BLOCK < width:
            right = jnp.concatenate([u, w], axis=1)
            uh, um, ul = split3(u)
            rh, rm, rl = split3(right)
            left = jnp.concatenate([uh, uh, um, uh, ul, um], axis=0)
            right = jnp.concatenate([rh, rm, rh, rl, rh, rm], axis=0)
            both_ref[...] -= lax.dot_general(
                left, right, (((0,), (0,)), ((), ())), preferred_element_type=F32
            )
    ih, il = split(inv_ref[...])
    turn = (((1,), (1,)), ((), ()))
    for src_ref, base in ((low_ref, 0), (high_ref, low_ref.shape[0])):
        for k in range(src_ref.shape[0]):
            hi, lo = split(src_ref[k])
            q_ref[base + k] = lax.dot_general(hi, ih, turn, preferred_element_type=F32) + (
                lax.dot_general(lo, ih, turn, preferred_element_type=F32)
                + lax.dot_general(hi, il, turn, preferred_element_type=F32)
            )


def steps(axis_size, fn):
    return [(i, fn(i)) for i in range(axis_size)]


def core_swap(n):
    return steps(n, lambda l: l ^ 1)


def ring_swap(n, odd):
    chips = n // 2

    def partner(l):
        y = l >> 1
        y = chips - 1 - y if odd else y ^ 1
        return (y << 1) | (l & 1)

    return steps(n, partner)


def level_sum(other, first, second):
    n = lax.axis_size("lev")
    core, even, odd = core_swap(n), ring_swap(n, False), ring_swap(n, True)

    def send(x, perm):
        return lax.ppermute(x, "lev", perm)

    def reduced(x, perm):
        mid = x.shape[0] // 2
        return x[mid:] + send(x[:mid], perm)

    def gathered(x, perm):
        return jnp.concatenate([send(x, perm), x])

    def summed(x, perm):
        return x + send(x, perm)

    together = lax.optimization_barrier
    mine = send(other, core)
    mid = first.shape[0]
    p, q = first + mine[:mid], second + mine[mid:]
    p, q = together((reduced(p, even), reduced(q, odd)))
    p, q = together((summed(p, odd), summed(q, even)))
    own = jnp.concatenate([gathered(p, even), gathered(q, odd)])
    return send(own, core), own


def own_order():
    l = lax.axis_index("lev")
    y, c = l >> 1, l & 1
    first, second = (y ^ (y >> 1)) & 1, y >> 1
    keep = (1 - c) << 4
    one = keep | ((1 - first) << 2)
    two = keep | ((1 - second) << 2)
    return jnp.stack([one, two]).astype(jnp.int32)


def gram_sum(x):
    n, m = lax.axis_size("lev"), lax.axis_size("tile")

    for perm in (core_swap(n), ring_swap(n, False), ring_swap(n, True)):
        x = x + lax.ppermute(x, "lev", perm)
    for fn in (
        lambda t: t ^ 1,
        lambda t: (t & ~3) | (3 - (t & 3)),
        lambda t: (t & ~7) | (7 - (t & 7)),
        lambda t: t ^ 8,
        lambda t: (t & 7) | ((3 - (t >> 3)) << 3),
    ):
        x = x + lax.ppermute(x, "tile", steps(m, fn))
    return x


def from_neighbours(lower_piece, upper_piece, axis):
    count = lax.axis_size(axis)
    below = lax.ppermute(lower_piece, axis, [(i, i + 1) for i in range(count - 1)])
    above = lax.ppermute(upper_piece, axis, [(i + 1, i) for i in range(count - 1)])
    return below, above


PARAMS = pltpu.CompilerParams(vmem_limit_bytes=16 << 20)


def shape(*dims, dtype=F32):
    return jax.ShapeDtypeStruct(dims, dtype)


NEAR = ((0, 4), (4, 4))
PARTS = ((0, 6), (6, 2))
SMALL = pl.BlockSpec(memory_space=pltpu.SMEM)
WHOLE = pl.BlockSpec()
tied = lax.optimization_barrier


def call(kernel, outs, *args, scratch=(), scalars=0, name=None, **static):
    def body(*refs):
        kernel(*refs, **static)

    return pl.pallas_call(
        body,
        out_shape=outs,
        in_specs=[SMALL] * scalars + [WHOLE] * (len(args) - scalars),
        scratch_shapes=list(scratch),
        compiler_params=PARAMS,
        name=name,
    )(*args)


def shards(probes, sigma, obs_count, obs_cell, obs_rinv, obs_jac):
    levels, rows, cols, width = probes.shape
    cells = rows * cols
    rim = REACH * cols
    bins, slots = obs_cell.shape
    total = bins * slots
    half = total // 2
    mhi, mlo = split(jnp.asarray(ring_matrix(cols, 256)))
    band = jnp.asarray(level_matrix(levels, 3 * levels))
    order = own_order()

    def field(n):
        return (shape(n, cells, width), shape(n, rim, width), shape(n, rim, width))

    def banded(across, head, tail):
        n = across.shape[0]
        north, south = from_neighbours(tail, head, "tile")
        edge = (n, REACH, cols, width)
        return north.reshape(edge), across.reshape(n, rows, cols, width), south.reshape(edge)

    packed = call(
        pack_kernel, shape(bins, levels + 2, slots),
        obs_count, obs_cell, obs_rinv, obs_jac, scalars=1, name="pack",
    )
    sent = lax.all_to_all(packed, "tile", split_axis=0, concat_axis=0, tiled=True)
    flat, _ = tied((probes.reshape(levels, cells, width), packed))
    near = [
        call(zonal_kernel, field(n), flat, mhi, mlo, base=base, name="zonal" + str(base))
        for base, n in NEAR
    ]
    near[0] = banded(*near[0])
    seen, pick, place = call(
        prepare_kernel,
        (
            shape(bins, levels, slots),
            shape(total, cells, dtype=BF16),
            shape(cells, total, dtype=BF16),
        ),
        order, sent, sigma.reshape(levels, cells), scalars=1, name="prepare",
    )
    below, above = from_neighbours(seen, seen, "lev")
    across, head, tail, _ = tied((*near[1], seen))
    near[1] = banded(across, head, tail)

    def grid(n):
        return pltpu.VMEM((n, rows, cols, width), F32)

    base, n = NEAR[0]
    other, own, turned = call(
        column_kernel,
        (shape(half, width), shape(half, width), shape(total, 2 * levels)),
        order, *near[0], sent, below, seen, above, band, pick,
        scratch=[grid(n), pltpu.VMEM((bins, levels, slots), F32)], scalars=1, name="column",
    )
    base, n = NEAR[1]
    wide = shape(n // 2, cells, 2 * width, dtype=BF16)
    other, high, low = call(
        column_other_kernel, (shape(half, width), wide, wide),
        *near[1], other, turned, pick, scratch=[grid(n)], base=base, name="column_other",
    )
    first, second = call(
        column_own_kernel, (shape(half // 2, width), shape(half // 2, width)),
        high, low, own, turned, pick, base=base, name="column_own",
    )
    other, own = level_sum(other, first, second)

    weights = pltpu.VMEM((half, width), F32)
    base, n = PARTS[0]
    field_own = call(
        own_kernel, shape(n // 2, cells, 2 * width), own, turned, place,
        scratch=[weights], name="own",
    )
    near = call(
        adjoint_kernel, field(n), other, turned, place, field_own, mhi, mlo,
        scratch=[weights], name="adjoint",
    )
    other, _ = tied((other, near[1]))
    fields = [banded(*near)]
    base, n = PARTS[1]
    near = call(
        adjoint_end_kernel, field(n), other, own, turned, place, mhi, mlo,
        scratch=[weights, weights], base=base, name="adjoint_end",
    )
    fields.append(banded(*near))

    base, n = PARTS[0]
    first, gram = pl.pallas_call(
        panel_kernel,
        out_shape=(shape(n, rows, cols, width), shape(width, width)),
        compiler_params=PARAMS,
        name="panel",
    )(*fields[0], probes)
    base, n = PARTS[1]

    def end_body(*refs):
        panel_end_kernel(*refs, base=base)

    second, gram = pl.pallas_call(
        end_body,
        out_shape=(shape(n, rows, cols, width), shape(width // 2 + 8, width)),
        compiler_params=PARAMS,
        name="panel_end",
    )(*fields[1], probes, gram)
    panels = [p.reshape(-1, cells, width) for p in (first, second)]
    gram = gram_sum(gram)
    whole = cells * levels * lax.axis_size("tile") * lax.axis_size("lev")

    def factor_body(*refs):
        factor_kernel(*refs, scale=1.0 / whole)

    qpanel, rfac = pl.pallas_call(
        factor_body,
        out_shape=(shape(levels, cells, width), shape(width, width)),
        scratch_shapes=[pltpu.VMEM((width, 2 * width), F32), pltpu.VMEM((width, width), F32)],
        compiler_params=PARAMS,
        name="factor",
    )(gram, *panels)
    return (qpanel.reshape(probes.shape), rfac)


def solution(mesh):
    in_specs = (
        P("lev", "tile", None, None),
        P("lev", "tile", None),
        P("tile"),
        P("tile", None),
        P("tile", None),
        P("tile", "lev", None),
    )
    out_specs = (P("lev", "tile", None, None), P())
    return jax.shard_map(shards, mesh=mesh, in_specs=in_specs, out_specs=out_specs, check_vma=False)
```

```python
import math

import jax
import jax.numpy as jnp
import numpy as np
from jax import lax
from jax.experimental import pallas as pl
from jax.experimental.pallas import tpu as pltpu
from jax.sharding import PartitionSpec as P

F32 = jnp.float32
BF16 = jnp.bfloat16
REACH = 7


def tap_weights():
    profile = [math.exp(-(offset / 6.0) * (offset / 6.0)) for offset in range(-7, 8)]
    scaling = math.sqrt(sum((element * element for element in profile)))
    return [element / scaling for element in profile]


TAPS = tap_weights()


def ring_matrix(cols, size):
    one = np.zeros((cols, cols), np.float64)
    for c in range(cols):
        for d in range(-REACH, REACH + 1):
            one[c, (c + d) % cols] += TAPS[d + REACH]
    return np.kron(np.eye(size // cols), one).astype(np.float32)


def level_matrix(levels):
    at = (levels, 3 * levels)
    d = lax.broadcasted_iota(jnp.int32, at, 1) - lax.broadcasted_iota(jnp.int32, at, 0) - levels
    band = jnp.zeros(at, F32)
    for offset in range(-REACH, REACH + 1):
        band = jnp.where(d == offset, TAPS[offset + REACH], band)
    return band


def split(x):
    hi = x.astype(BF16)
    return hi, (x - hi.astype(F32)).astype(BF16)


def dot(a, b):
    return jnp.dot(a, b, preferred_element_type=F32)


def zonal(mhi, mlo, pair):
    outs = []
    for h in range(2):
        hi, lo = split(pair[256 * h : 256 * h + 256])
        outs.append(dot(mhi, hi) + (dot(mlo, hi) + dot(mhi, lo)))
    return jnp.concatenate(outs, axis=0)


def put_zonal(x, kp, rim, out_ref, head_ref, tail_ref):
    cells = x.shape[0]
    for j in range(2):
        part = x[:, 128 * j : 128 * j + 128]
        out_ref[2 * kp + j] = part
        head_ref[2 * kp + j] = part[:rim]
        tail_ref[2 * kp + j] = part[cells - rim :]


def rim_kernel(field_ref, ring_ref, head_ref, tail_ref, *, base):
    rim = head_ref.shape[1]
    mhi, mlo = ring_ref[0], ring_ref[1]
    for kp in range(head_ref.shape[0] // 2):
        k = base + 2 * kp
        pair = zonal(mhi, mlo, jnp.concatenate([field_ref[k], field_ref[k + 1]], axis=1))
        cells, wide = pair.shape
        for j in range(2):
            part = pair[:, wide // 2 * j : wide // 2 * (j + 1)]
            head_ref[2 * kp + j] = part[:rim]
            tail_ref[2 * kp + j] = part[cells - rim :]


def meridional(k, j, north_ref, own_ref, south_ref):
    cut = pl.ds(8 * j, 8)
    rows = jnp.concatenate(
        [north_ref[k, :, cut, :], own_ref[k, :, cut, :], south_ref[k, :, cut, :]], axis=0
    )
    length = own_ref.shape[1]
    total = TAPS[REACH] * rows[REACH : REACH + length]
    for d in range(1, REACH + 1):
        total = total + TAPS[REACH + d] * (
            rows[REACH - d : REACH - d + length] + rows[REACH + d : REACH + d + length]
        )
    return total


CHUNK = 1024
GROUP = 256


def source_at(order, position):
    return position ^ order[(position >> 3) & 1]


def pack_kernel(below_ref, local_ref, above_ref, extra_ref, packed_ref):
    levels = local_ref.shape[1]
    for s in range(extra_ref.shape[0]):
        packed_ref[s, :levels] = below_ref[s]
        packed_ref[s, levels : 2 * levels] = local_ref[s]
        packed_ref[s, 2 * levels : 3 * levels] = above_ref[s]
        packed_ref[s, 3 * levels :] = extra_ref[s]


def prepare_kernel(
    sent_ref, below_ref, local_ref, above_ref,
    turned_ref, pick_ref, place_ref,
):
    sources, deep, slots = sent_ref.shape
    cells = place_ref.shape[0]
    levels = local_ref.shape[1]
    wide = 3 * levels
    band, order = level_matrix(levels), own_order()
    sigma = jnp.concatenate(
        [
            jnp.concatenate([below_ref[i], local_ref[i], above_ref[i]], axis=0)
            for i in range(sources, local_ref.shape[0])
        ],
        axis=1,
    )
    stacked = jnp.concatenate(split(sigma), axis=0)
    cell_down = lax.broadcasted_iota(jnp.int32, (cells, slots), 0).astype(F32)
    cell_along = lax.broadcasted_iota(jnp.int32, (slots, cells), 1).astype(F32)
    for first in range(0, sources, 2):
        ats = [slice(slots * s, slots * s + slots) for s in (first, first + 1)]
        froms = [source_at(order, s) for s in (first, first + 1)]
        hots = []
        for source in froms:
            here = sent_ref[source, deep - 1 : deep]
            hots.append(jnp.where(cell_down == here, 1.0, 0.0).astype(BF16))
        onehot = jnp.concatenate(hots, axis=1)
        place_ref[:, slots * first : slots * (first + 2)] = onehot
        picked = dot(stacked, onehot)
        jac = jnp.concatenate([sent_ref[source, :wide] for source in froms], axis=1)
        spread = jnp.dot(
            band,
            jac * (picked[:wide] + picked[wide:]),
            precision=lax.Precision.HIGHEST,
            preferred_element_type=F32,
        )
        for i in range(2):
            extra = jnp.broadcast_to(sent_ref[froms[i], deep - 2 : deep - 1], (levels, slots))
            cell = jnp.broadcast_to(sent_ref[froms[i], deep - 1 : deep], (levels, slots))
            turned_ref[ats[i], :levels] = spread[:, slots * i : slots * i + slots].T
            turned_ref[ats[i], levels:] = extra.T
            pick_ref[ats[i], :] = jnp.where(cell_along == cell.T[:, :1], 1.0, 0.0).astype(BF16)


def smoothed_rows(north_ref, field_ref, south_ref, ring_ref, near_ref, w_ref, base):
    levels, rows, cols, width = w_ref.shape
    mhi, mlo = ring_ref[0], ring_ref[1]
    for kp in range(levels // 2):
        k = base + 2 * kp
        pair = zonal(mhi, mlo, jnp.concatenate([field_ref[k], field_ref[k + 1]], axis=1))
        for j in range(2):
            near_ref[2 * kp + j] = pair[:, width * j : width * (j + 1)].reshape(rows, cols, width)

    def level_pass(k, carry):
        for j in range(cols // 8):
            w_ref[k, :, pl.ds(8 * j, 8), :] = meridional(k, j, north_ref, near_ref, south_ref)
        return carry

    lax.fori_loop(0, levels, level_pass, 0)


def level_pair(w_ref, kp):
    _, rows, cols, width = w_ref.shape
    flat = (rows * cols, width)
    return split(
        jnp.concatenate([w_ref[2 * kp].reshape(flat), w_ref[2 * kp + 1].reshape(flat)], axis=1)
    )


def observed(dst_ref, before_ref, turned_ref, pick_ref, pairs, base, start, skip):
    width = dst_ref.shape[1]

    def chunk_pass(c, carry):
        to = pl.ds(pl.multiple_of(c * CHUNK, CHUNK), CHUNK)
        at = pl.ds(pl.multiple_of(start + c * CHUNK, CHUNK), CHUNK)
        pick = pick_ref[at, :]
        total = None
        if before_ref is not None:
            total = before_ref[pl.ds(pl.multiple_of(skip + c * CHUNK, CHUNK), CHUNK), :]
        for kp, (hi, lo) in enumerate(pairs):
            k = base + 2 * kp
            seen = dot(pick, hi) + dot(pick, lo)
            part = (
                turned_ref[at, k : k + 1] * seen[:, :width]
                + turned_ref[at, k + 1 : k + 2] * seen[:, width:]
            )
            total = part if total is None else total + part
        dst_ref[to, :] = total
        return carry

    lax.fori_loop(0, dst_ref.shape[0] // CHUNK, chunk_pass, 0)


def column_kernel(
    north_ref, south_ref, field_ref, ring_ref, turned_ref, pick_ref,
    other_ref, own_ref,
    near_ref, w_ref,
):
    smoothed_rows(north_ref, field_ref, south_ref, ring_ref, near_ref, w_ref, 0)
    pairs = [level_pair(w_ref, kp) for kp in range(w_ref.shape[0] // 2)]
    half = other_ref.shape[0]
    observed(other_ref, None, turned_ref, pick_ref, pairs, 0, 0, 0)
    observed(own_ref, None, turned_ref, pick_ref, pairs, 0, half, 0)


def column_other_kernel(
    north_ref, south_ref, field_ref, ring_ref, before_ref, turned_ref, pick_ref,
    other_ref, hi_ref, lo_ref,
    near_ref, w_ref, *, base,
):
    smoothed_rows(north_ref, field_ref, south_ref, ring_ref, near_ref, w_ref, base)
    pairs = []
    for kp in range(w_ref.shape[0] // 2):
        hi, lo = level_pair(w_ref, kp)
        hi_ref[kp], lo_ref[kp] = hi, lo
        pairs.append((hi, lo))
    observed(other_ref, before_ref, turned_ref, pick_ref, pairs, base, 0, 0)


def column_own_kernel(
    hi_ref, lo_ref, before_ref, turned_ref, pick_ref, first_ref, second_ref, *, base
):
    pairs = [(hi_ref[kp], lo_ref[kp]) for kp in range(hi_ref.shape[0])]
    half, n = before_ref.shape[0], first_ref.shape[0]
    observed(first_ref, before_ref, turned_ref, pick_ref, pairs, base, half, 0)
    observed(second_ref, before_ref, turned_ref, pick_ref, pairs, base, half + n, n)


def scattered(weighted_ref, turned_ref, place_ref, start, k):
    field = None
    for c in range(weighted_ref.shape[0] // CHUNK):
        at = slice(c * CHUNK, c * CHUNK + CHUNK)
        to = slice(start + c * CHUNK, start + c * CHUNK + CHUNK)
        weighted = weighted_ref[at, :]
        pair = jnp.concatenate(
            [turned_ref[to, k : k + 1] * weighted, turned_ref[to, k + 1 : k + 2] * weighted],
            axis=1,
        )
        hi, lo = split(pair)
        place = place_ref[:, to]
        part = dot(place, hi) + dot(place, lo)
        field = part if field is None else field + part
    return field


def own_kernel(own_ref, turned_ref, place_ref, field_ref, weighted_ref):
    half = own_ref.shape[0]
    weighted_ref[...] = own_ref[...] * turned_ref[half:, 8:9]
    for kp in range(field_ref.shape[0]):
        field_ref[kp] = scattered(weighted_ref, turned_ref, place_ref, half, 2 * kp)


def adjoint_kernel(
    other_ref, turned_ref, place_ref, field_ref, ring_ref,
    out_ref, head_ref, tail_ref,
    weighted_ref,
):
    rim = head_ref.shape[1]
    half = other_ref.shape[0]
    weighted_ref[...] = other_ref[...] * turned_ref[:half, 8:9]
    mhi, mlo = ring_ref[0], ring_ref[1]
    for kp in range(out_ref.shape[0] // 2):
        field = field_ref[kp] + scattered(weighted_ref, turned_ref, place_ref, 0, 2 * kp)
        put_zonal(zonal(mhi, mlo, field), kp, rim, out_ref, head_ref, tail_ref)


def adjoint_end_kernel(
    other_ref, own_ref, turned_ref, place_ref, ring_ref,
    out_ref, head_ref, tail_ref,
    one_ref, two_ref, *, base,
):
    rim = head_ref.shape[1]
    half = other_ref.shape[0]
    one_ref[...] = other_ref[...] * turned_ref[:half, 8:9]
    two_ref[...] = own_ref[...] * turned_ref[half:, 8:9]
    mhi, mlo = ring_ref[0], ring_ref[1]
    for kp in range(out_ref.shape[0] // 2):
        k = base + 2 * kp
        field = scattered(one_ref, turned_ref, place_ref, 0, k)
        field = field + scattered(two_ref, turned_ref, place_ref, half, k)
        put_zonal(zonal(mhi, mlo, field), kp, rim, out_ref, head_ref, tail_ref)


def panel_part(north_ref, own_ref, south_ref, probes_ref, panel_ref, base):
    levels, rows, cols, width = own_ref.shape

    def level_pass(k, carry):
        for j in range(cols // 8):
            cut = pl.ds(8 * j, 8)
            panel_ref[k, :, cut, :] = probes_ref[base + k, :, cut, :] + meridional(
                k, j, north_ref, own_ref, south_ref
            )
        hi, lo = split(panel_ref[k].reshape(rows * cols, width))
        turn = (((0,), (0,)), ((), ()))
        cross = lax.dot_general(hi, lo, turn, preferred_element_type=F32)
        main = lax.dot_general(hi, hi, turn, preferred_element_type=F32)
        return carry[0] + main, carry[1] + cross

    zero = jnp.zeros((width, width), F32)
    main, cross = lax.fori_loop(0, levels, level_pass, (zero, zero))
    return main + (cross + cross.T)


def panel_kernel(north_ref, own_ref, south_ref, probes_ref, panel_ref, gram_ref):
    gram_ref[...] = panel_part(north_ref, own_ref, south_ref, probes_ref, panel_ref, 0)


def panel_end_kernel(
    north_ref, own_ref, south_ref, probes_ref, before_ref, panel_ref, packed_ref, *, base
):
    gram = before_ref[...] + panel_part(
        north_ref, own_ref, south_ref, probes_ref, panel_ref, base
    )
    packed_ref[...] = packed_gram(gram)


def packed_gram(gram):
    width = gram.shape[0]
    mid = width // 2
    row = lax.broadcasted_iota(jnp.int32, (mid, width), 0)
    col = lax.broadcasted_iota(jnp.int32, (mid, width), 1)
    top, low = gram[:mid], pltpu.roll(gram[mid:], mid, axis=1)
    body = jnp.where(col >= row, top, low)
    diag = jnp.sum(jnp.where(col == row, low, 0.0), axis=0, keepdims=True)
    return jnp.concatenate([body, jnp.broadcast_to(diag, (8, width))], axis=0)


def unpacked_gram(packed):
    width = packed.shape[1]
    mid = width // 2
    row = lax.broadcasted_iota(jnp.int32, (mid, width), 0)
    col = lax.broadcasted_iota(jnp.int32, (mid, width), 1)
    body = packed[:mid]
    turned = jnp.concatenate([body, body], axis=0).T
    top = jnp.where(col >= row, body, turned[:mid])
    far = col - mid
    body, flip = pltpu.roll(body, mid, axis=1), pltpu.roll(turned[:mid], mid, axis=1)
    diag = pltpu.roll(packed[mid:], mid, axis=1)[:1]
    corner = jnp.where(row > far, body, jnp.where(row < far, flip, diag))
    return jnp.concatenate([top, jnp.where(col < mid, turned[mid:], corner)], axis=0)


BLOCK = 8


def split3(x):
    hi, rest = split(x)
    mid = (x - hi.astype(F32)).astype(BF16)
    lo = (x - hi.astype(F32) - mid.astype(F32)).astype(BF16)
    return hi, mid, lo


def factor_kernel(gram_ref, low_ref, high_ref, q_ref, rfac_ref, both_ref, inv_ref, *, scale):
    width = gram_ref.shape[1]
    down = lax.broadcasted_iota(jnp.int32, (BLOCK, width), 0)
    along = lax.broadcasted_iota(jnp.int32, (BLOCK, width), 1)
    rows_all = lax.broadcasted_iota(jnp.int32, (width, width), 0)
    cols_all = lax.broadcasted_iota(jnp.int32, (width, width), 1)
    both_ref[:, :width] = unpacked_gram(gram_ref[...]) * scale
    both_ref[:, width:] = jnp.where(rows_all == cols_all, 1.0, 0.0)
    for start in range(0, width, BLOCK):
        block = both_ref[start : start + BLOCK, :]
        a, w = block[:, :width], block[:, width:]
        a = jnp.where(along >= start, a, 0.0)
        lanes = [
            jnp.broadcast_to(a[:, start + b : start + b + 1], (BLOCK, width)) for b in range(BLOCK)
        ]
        roots = jnp.zeros((BLOCK, width), F32)
        for p in range(BLOCK):
            pivot = jnp.broadcast_to(lanes[p][p : p + 1], (BLOCK, width))
            root = lax.rsqrt(pivot)
            root = root * (1.5 - 0.5 * pivot * root * root)
            roots = jnp.where(down == p, root, roots)
            if p == BLOCK - 1:
                break
            f = jnp.where(down > p, lanes[p] * (root * root), 0.0)
            for b in range(p + 1, BLOCK):
                lanes[b] = lanes[b] - f * lanes[b][p : p + 1]
            a = a - f * a[p : p + 1]
            w = w - f * w[p : p + 1]
        u = jnp.where(along >= down + start, a * roots, 0.0)
        w = w * roots
        rfac_ref[start : start + BLOCK, :] = u
        inv_ref[start : start + BLOCK, :] = w
        if start + BLOCK < width:
            right = jnp.concatenate([u, w], axis=1)
            uh, um, ul = split3(u)
            rh, rm, rl = split3(right)
            left = jnp.concatenate([uh, uh, um, uh, ul, um], axis=0)
            right = jnp.concatenate([rh, rm, rh, rl, rh, rm], axis=0)
            both_ref[...] -= lax.dot_general(
                left, right, (((0,), (0,)), ((), ())), preferred_element_type=F32
            )
    ih, il = split(inv_ref[...])
    turn = (((1,), (1,)), ((), ()))
    for src_ref, base in ((low_ref, 0), (high_ref, low_ref.shape[0])):
        for k in range(src_ref.shape[0]):
            hi, lo = split(src_ref[k])
            q_ref[base + k] = lax.dot_general(hi, ih, turn, preferred_element_type=F32) + (
                lax.dot_general(lo, ih, turn, preferred_element_type=F32)
                + lax.dot_general(hi, il, turn, preferred_element_type=F32)
            )


def steps(axis_size, fn):
    return [(i, fn(i)) for i in range(axis_size)]


def core_swap(n):
    return steps(n, lambda l: l ^ 1)


def ring_swap(n, odd):
    chips = n // 2

    def partner(l):
        y = l >> 1
        y = chips - 1 - y if odd else y ^ 1
        return (y << 1) | (l & 1)

    return steps(n, partner)


def level_sum(other, first, second):
    n = lax.axis_size("lev")
    core, even, odd = core_swap(n), ring_swap(n, False), ring_swap(n, True)

    def send(x, perm):
        return lax.ppermute(x, "lev", perm)

    def reduced(x, perm):
        mid = x.shape[0] // 2
        return x[mid:] + send(x[:mid], perm)

    def gathered(x, perm):
        return jnp.concatenate([send(x, perm), x])

    def summed(x, perm):
        return x + send(x, perm)

    together = lax.optimization_barrier
    mine = send(other, core)
    mid = first.shape[0]
    p, q = first + mine[:mid], second + mine[mid:]
    p, q = together((reduced(p, even), reduced(q, odd)))
    p, q = together((summed(p, odd), summed(q, even)))
    own = jnp.concatenate([gathered(p, even), gathered(q, odd)])
    return send(own, core), own


def own_order():
    l = lax.axis_index("lev")
    y, c = l >> 1, l & 1
    first, second = (y ^ (y >> 1)) & 1, y >> 1
    keep = (1 - c) << 4
    one = keep | ((1 - first) << 2)
    two = keep | ((1 - second) << 2)
    return one, two


def gram_sum(x):
    n, m = lax.axis_size("lev"), lax.axis_size("tile")

    for perm in (core_swap(n), ring_swap(n, False), ring_swap(n, True)):
        x = x + lax.ppermute(x, "lev", perm)
    for fn in (
        lambda t: t ^ 1,
        lambda t: (t & ~3) | (3 - (t & 3)),
        lambda t: (t & ~7) | (7 - (t & 7)),
        lambda t: t ^ 8,
        lambda t: (t & 7) | ((3 - (t >> 3)) << 3),
    ):
        x = x + lax.ppermute(x, "tile", steps(m, fn))
    return x


def from_neighbours(lower_piece, upper_piece, axis):
    count = lax.axis_size(axis)
    below = lax.ppermute(lower_piece, axis, [(i, i + 1) for i in range(count - 1)])
    above = lax.ppermute(upper_piece, axis, [(i + 1, i) for i in range(count - 1)])
    return below, above


PARAMS = pltpu.CompilerParams(vmem_limit_bytes=16 << 20)


def shape(*dims, dtype=F32):
    return jax.ShapeDtypeStruct(dims, dtype)


NEAR = ((0, 4), (4, 4))
PARTS = ((0, 4), (4, 4))
tied = lax.optimization_barrier


def call(kernel, outs, *args, scratch=(), name=None, **static):
    def body(*refs):
        kernel(*refs, **static)

    return pl.pallas_call(
        body,
        out_shape=outs,
        scratch_shapes=list(scratch),
        compiler_params=PARAMS,
        name=name,
    )(*args)


def shards(probes, sigma, obs_count, obs_cell, obs_rinv, obs_jac):
    levels, rows, cols, width = probes.shape
    cells = rows * cols
    rim = REACH * cols
    bins, slots = obs_cell.shape
    total = bins * slots
    half = total // 2
    ring = jnp.stack(split(jnp.asarray(ring_matrix(cols, 256))))

    def field(n):
        return (shape(n, cells, width), shape(n, rim, width), shape(n, rim, width))

    def banded(across, head, tail):
        n = across.shape[0]
        north, south = from_neighbours(tail, head, "tile")
        edge = (n, REACH, cols, width)
        return north.reshape(edge), across.reshape(n, rows, cols, width), south.reshape(edge)

    local = jnp.concatenate(
        [obs_jac, sigma.reshape(levels, cells // slots, slots).transpose(1, 0, 2)]
    )
    below, above = from_neighbours(local, local, "lev")
    live = jnp.arange(slots, dtype=jnp.int32)[None, :] < obs_count[:, None]
    extra = jnp.stack([jnp.where(live, obs_rinv, 0.0), obs_cell.astype(F32)], axis=1)
    packed = call(
        pack_kernel, shape(bins, 3 * levels + 2, slots), below, local, above, extra, name="pack"
    )
    sent = lax.all_to_all(packed, "tile", split_axis=0, concat_axis=0, tiled=True)
    flat = probes.reshape(levels, cells, width)

    def rims(after, base, n):
        source, _ = tied((flat, after))
        edge = shape(n, rim, width)
        head, tail = call(
            rim_kernel, (edge, edge), source, ring, base=base, name="rim" + str(base)
        )
        north, south = from_neighbours(tail, head, "tile")
        return north.reshape(n, REACH, cols, width), south.reshape(n, REACH, cols, width)

    near = rims(packed, *NEAR[0])
    turned, pick, place = call(
        prepare_kernel,
        (
            shape(total, 2 * levels),
            shape(total, cells, dtype=BF16),
            shape(cells, total, dtype=BF16),
        ),
        sent, below, local, above, name="prepare",
    )
    far = rims(turned, *NEAR[1])

    def grid(n):
        return pltpu.VMEM((n, rows, cols, width), F32)

    base, n = NEAR[0]
    other, own = call(
        column_kernel, (shape(half, width), shape(half, width)),
        *near, flat, ring, turned, pick, scratch=[grid(n), grid(n)], name="column",
    )
    base, n = NEAR[1]
    wide = shape(n // 2, cells, 2 * width, dtype=BF16)
    other, high, low = call(
        column_other_kernel, (shape(half, width), wide, wide),
        *far, flat, ring, other, turned, pick,
        scratch=[grid(n), grid(n)], base=base, name="column_other",
    )
    first, second = call(
        column_own_kernel, (shape(half // 2, width), shape(half // 2, width)),
        high, low, own, turned, pick, base=base, name="column_own",
    )
    other, own = level_sum(other, first, second)

    weights = pltpu.VMEM((half, width), F32)
    base, n = PARTS[0]
    field_own = call(
        own_kernel, shape(n // 2, cells, 2 * width), own, turned, place,
        scratch=[weights], name="own",
    )
    near = call(
        adjoint_kernel, field(n), other, turned, place, field_own, ring,
        scratch=[weights], name="adjoint",
    )
    other, _ = tied((other, near[1]))
    fields = [banded(*near)]
    base, n = PARTS[1]
    near = call(
        adjoint_end_kernel, field(n), other, own, turned, place, ring,
        scratch=[weights, weights], base=base, name="adjoint_end",
    )
    fields.append(banded(*near))

    base, n = PARTS[0]
    first, gram = pl.pallas_call(
        panel_kernel,
        out_shape=(shape(n, rows, cols, width), shape(width, width)),
        compiler_params=PARAMS,
        name="panel",
    )(*fields[0], probes)
    base, n = PARTS[1]

    def end_body(*refs):
        panel_end_kernel(*refs, base=base)

    second, gram = pl.pallas_call(
        end_body,
        out_shape=(shape(n, rows, cols, width), shape(width // 2 + 8, width)),
        compiler_params=PARAMS,
        name="panel_end",
    )(*fields[1], probes, gram)
    panels = [p.reshape(-1, cells, width) for p in (first, second)]
    gram = gram_sum(gram)
    whole = cells * levels * lax.axis_size("tile") * lax.axis_size("lev")

    def factor_body(*refs):
        factor_kernel(*refs, scale=1.0 / whole)

    qpanel, rfac = pl.pallas_call(
        factor_body,
        out_shape=(shape(levels, cells, width), shape(width, width)),
        scratch_shapes=[pltpu.VMEM((width, 2 * width), F32), pltpu.VMEM((width, width), F32)],
        compiler_params=PARAMS,
        name="factor",
    )(gram, *panels)
    return (qpanel.reshape(probes.shape), rfac)


def solution(mesh):
    in_specs = (
        P("lev", "tile", None, None),
        P("lev", "tile", None),
        P("tile"),
        P("tile", None),
        P("tile", None),
        P("tile", "lev", None),
    )
    out_specs = (P("lev", "tile", None, None), P())
    return jax.shard_map(shards, mesh=mesh, in_specs=in_specs, out_specs=out_specs, check_vma=False)
```

```python
import math

import jax
import jax.numpy as jnp
import numpy as np
from jax import lax
from jax.experimental import pallas as pl
from jax.experimental.pallas import tpu as pltpu
from jax.sharding import PartitionSpec as P

F32 = jnp.float32
BF16 = jnp.bfloat16
REACH = 7


def tap_weights():
    profile = [math.exp(-(offset / 6.0) * (offset / 6.0)) for offset in range(-7, 8)]
    scaling = math.sqrt(sum((element * element for element in profile)))
    return [element / scaling for element in profile]


TAPS = tap_weights()


def ring_matrix(cols, size):
    one = np.zeros((cols, cols), np.float64)
    for c in range(cols):
        for d in range(-REACH, REACH + 1):
            one[c, (c + d) % cols] += TAPS[d + REACH]
    return np.kron(np.eye(size // cols), one).astype(np.float32)


def level_matrix(levels):
    at = (levels, 3 * levels)
    d = lax.broadcasted_iota(jnp.int32, at, 1) - lax.broadcasted_iota(jnp.int32, at, 0) - levels
    band = jnp.zeros(at, F32)
    for offset in range(-REACH, REACH + 1):
        band = jnp.where(d == offset, TAPS[offset + REACH], band)
    return band


def split(x):
    hi = x.astype(BF16)
    return hi, (x - hi.astype(F32)).astype(BF16)


def dot(a, b):
    return jnp.dot(a, b, preferred_element_type=F32)


def zonal(mhi, mlo, pair):
    outs = []
    for h in range(2):
        hi, lo = split(pair[256 * h : 256 * h + 256])
        outs.append(dot(mhi, hi) + (dot(mlo, hi) + dot(mhi, lo)))
    return jnp.concatenate(outs, axis=0)


def put_levels(pair, kp, out_ref):
    width = out_ref.shape[-1]
    for j in range(2):
        out_ref[2 * kp + j] = pair[:, width * j : width * j + width]


def finish_zonal(mhi, mlo, out_ref, head_ref, tail_ref):
    levels, cells, _ = out_ref.shape
    rim = head_ref.shape[1]
    for kp in range(levels // 2):
        pair = jnp.concatenate([out_ref[2 * kp], out_ref[2 * kp + 1]], axis=1)
        put_levels(zonal(mhi, mlo, pair), kp, out_ref)
    for k in range(levels):
        head_ref[k] = out_ref[k, :rim]
        tail_ref[k] = out_ref[k, cells - rim :]


def rim_kernel(field_ref, ring_ref, head_ref, tail_ref, *, base):
    rim = head_ref.shape[1]
    mhi, mlo = ring_ref[0], ring_ref[1]
    for kp in range(head_ref.shape[0] // 2):
        k = base + 2 * kp
        pair = zonal(mhi, mlo, jnp.concatenate([field_ref[k], field_ref[k + 1]], axis=1))
        cells, wide = pair.shape
        for j in range(2):
            part = pair[:, wide // 2 * j : wide // 2 * (j + 1)]
            head_ref[2 * kp + j] = part[:rim]
            tail_ref[2 * kp + j] = part[cells - rim :]


def meridional(k, j, north_ref, own_ref, south_ref):
    cut = pl.ds(8 * j, 8)
    rows = jnp.concatenate(
        [north_ref[k, :, cut, :], own_ref[k, :, cut, :], south_ref[k, :, cut, :]], axis=0
    )
    length = own_ref.shape[1]
    total = TAPS[REACH] * rows[REACH : REACH + length]
    for d in range(1, REACH + 1):
        total = total + TAPS[REACH + d] * (
            rows[REACH - d : REACH - d + length] + rows[REACH + d : REACH + d + length]
        )
    return total


CHUNK = 1024
GROUP = 256


def source_at(order, position):
    return position ^ order[(position >> 3) & 1]


def pack_kernel(below_ref, local_ref, above_ref, extra_ref, packed_ref):
    levels = local_ref.shape[1]
    for s in range(extra_ref.shape[0]):
        packed_ref[s, :levels] = below_ref[s]
        packed_ref[s, levels : 2 * levels] = local_ref[s]
        packed_ref[s, 2 * levels : 3 * levels] = above_ref[s]
        packed_ref[s, 3 * levels :] = extra_ref[s]


def prepare_kernel(
    sent_ref, below_ref, local_ref, above_ref,
    turned_ref, pick_ref, place_ref,
):
    sources, deep, slots = sent_ref.shape
    cells = place_ref.shape[0]
    levels = local_ref.shape[1]
    wide = 3 * levels
    band, order = level_matrix(levels), own_order()
    sigma = jnp.concatenate(
        [
            jnp.concatenate([below_ref[i], local_ref[i], above_ref[i]], axis=0)
            for i in range(sources, local_ref.shape[0])
        ],
        axis=1,
    )
    stacked = jnp.concatenate(split(sigma), axis=0)
    cell_down = lax.broadcasted_iota(jnp.int32, (cells, slots), 0).astype(F32)
    cell_along = lax.broadcasted_iota(jnp.int32, (slots, cells), 1).astype(F32)
    for first in range(0, sources, 2):
        ats = [slice(slots * s, slots * s + slots) for s in (first, first + 1)]
        froms = [source_at(order, s) for s in (first, first + 1)]
        hots = []
        for source in froms:
            here = sent_ref[source, deep - 1 : deep]
            hots.append(jnp.where(cell_down == here, 1.0, 0.0).astype(BF16))
        onehot = jnp.concatenate(hots, axis=1)
        place_ref[:, slots * first : slots * (first + 2)] = onehot
        picked = dot(stacked, onehot)
        jac = jnp.concatenate([sent_ref[source, :wide] for source in froms], axis=1)
        spread = jnp.dot(
            band,
            jac * (picked[:wide] + picked[wide:]),
            precision=lax.Precision.HIGHEST,
            preferred_element_type=F32,
        )
        for i in range(2):
            extra = jnp.broadcast_to(sent_ref[froms[i], deep - 2 : deep - 1], (levels, slots))
            cell = jnp.broadcast_to(sent_ref[froms[i], deep - 1 : deep], (levels, slots))
            turned_ref[ats[i], :levels] = spread[:, slots * i : slots * i + slots].T
            turned_ref[ats[i], levels:] = extra.T
            pick_ref[ats[i], :] = jnp.where(cell_along == cell.T[:, :1], 1.0, 0.0).astype(BF16)


def smoothed_rows(north_ref, field_ref, south_ref, ring_ref, near_ref, w_ref, base):
    levels, rows, cols, width = w_ref.shape
    mhi, mlo = ring_ref[0], ring_ref[1]
    for kp in range(levels // 2):
        k = base + 2 * kp
        pair = zonal(mhi, mlo, jnp.concatenate([field_ref[k], field_ref[k + 1]], axis=1))
        for j in range(2):
            near_ref[2 * kp + j] = pair[:, width * j : width * (j + 1)].reshape(rows, cols, width)

    def level_pass(k, carry):
        for j in range(cols // 8):
            w_ref[k, :, pl.ds(8 * j, 8), :] = meridional(k, j, north_ref, near_ref, south_ref)
        return carry

    lax.fori_loop(0, levels, level_pass, 0)


def level_pair(w_ref, kp):
    _, rows, cols, width = w_ref.shape
    flat = (rows * cols, width)
    return split(
        jnp.concatenate([w_ref[2 * kp].reshape(flat), w_ref[2 * kp + 1].reshape(flat)], axis=1)
    )


def observed(dst_ref, before_ref, turned_ref, pick_ref, pairs, base, start, skip):
    width = dst_ref.shape[1]

    def chunk_pass(c, carry):
        to = pl.ds(pl.multiple_of(c * CHUNK, CHUNK), CHUNK)
        at = pl.ds(pl.multiple_of(start + c * CHUNK, CHUNK), CHUNK)
        pick = pick_ref[at, :]
        total = None
        if before_ref is not None:
            total = before_ref[pl.ds(pl.multiple_of(skip + c * CHUNK, CHUNK), CHUNK), :]
        for kp, (hi, lo) in enumerate(pairs):
            k = base + 2 * kp
            seen = dot(pick, hi) + dot(pick, lo)
            part = (
                turned_ref[at, k : k + 1] * seen[:, :width]
                + turned_ref[at, k + 1 : k + 2] * seen[:, width:]
            )
            total = part if total is None else total + part
        dst_ref[to, :] = total
        return carry

    lax.fori_loop(0, dst_ref.shape[0] // CHUNK, chunk_pass, 0)


def column_kernel(
    north_ref, south_ref, field_ref, ring_ref, turned_ref, pick_ref,
    other_ref, own_ref,
    near_ref, w_ref,
):
    smoothed_rows(north_ref, field_ref, south_ref, ring_ref, near_ref, w_ref, 0)
    pairs = [level_pair(w_ref, kp) for kp in range(w_ref.shape[0] // 2)]
    half = other_ref.shape[0]
    observed(other_ref, None, turned_ref, pick_ref, pairs, 0, 0, 0)
    observed(own_ref, None, turned_ref, pick_ref, pairs, 0, half, 0)


def column_other_kernel(
    north_ref, south_ref, field_ref, ring_ref, before_ref, turned_ref, pick_ref,
    other_ref, hi_ref, lo_ref,
    near_ref, w_ref, *, base,
):
    smoothed_rows(north_ref, field_ref, south_ref, ring_ref, near_ref, w_ref, base)
    pairs = []
    for kp in range(w_ref.shape[0] // 2):
        hi, lo = level_pair(w_ref, kp)
        hi_ref[kp], lo_ref[kp] = hi, lo
        pairs.append((hi, lo))
    observed(other_ref, before_ref, turned_ref, pick_ref, pairs, base, 0, 0)


def column_own_kernel(
    hi_ref, lo_ref, before_ref, turned_ref, pick_ref, first_ref, second_ref, *, base
):
    pairs = [(hi_ref[kp], lo_ref[kp]) for kp in range(hi_ref.shape[0])]
    half, n = before_ref.shape[0], first_ref.shape[0]
    observed(first_ref, before_ref, turned_ref, pick_ref, pairs, base, half, 0)
    observed(second_ref, before_ref, turned_ref, pick_ref, pairs, base, half + n, n)


def weigh(sums, turned_ref, weighted_ref):
    chunks, row = [], 0
    for sum_ref, start in sums:
        count = sum_ref.shape[0]
        weight = turned_ref[start : start + count, 8:9]
        weighted_ref[row : row + count] = sum_ref[...] * weight
        size = min(count, CHUNK)
        chunks += [(row + at, start + at, size) for at in range(0, count, size)]
        row += count
    return chunks


def scattered(field, chunks, weighted_ref, turned_ref, place_ref, k):
    for row, start, size in chunks:
        to = slice(start, start + size)
        weighted = weighted_ref[row : row + size, :]
        pair = jnp.concatenate(
            [turned_ref[to, k : k + 1] * weighted, turned_ref[to, k + 1 : k + 2] * weighted],
            axis=1,
        )
        hi, lo = split(pair)
        place = place_ref[:, to]
        part = dot(place, hi) + dot(place, lo)
        field = part if field is None else field + part
    return field


def kept_kernel(p_ref, q_ref, turned_ref, place_ref, field_ref, weighted_ref):
    half, n = turned_ref.shape[0] // 2, p_ref.shape[0]
    sums = ((p_ref, half + n), (q_ref, half + 3 * n))
    chunks = weigh(sums, turned_ref, weighted_ref)
    for kp in range(field_ref.shape[0]):
        field_ref[kp] = scattered(None, chunks, weighted_ref, turned_ref, place_ref, 2 * kp)


def own_kernel(p_ref, q_ref, turned_ref, place_ref, kept_ref, field_ref, weighted_ref):
    half, n = turned_ref.shape[0] // 2, p_ref.shape[0]
    chunks = weigh(((p_ref, half), (q_ref, half + 2 * n)), turned_ref, weighted_ref)
    for kp in range(field_ref.shape[0]):
        field_ref[kp] = scattered(
            kept_ref[kp], chunks, weighted_ref, turned_ref, place_ref, 2 * kp
        )


def adjoint_kernel(
    other_ref, turned_ref, place_ref, field_ref, ring_ref,
    out_ref, head_ref, tail_ref,
    weighted_ref,
):
    chunks = weigh(((other_ref, 0),), turned_ref, weighted_ref)
    for kp in range(out_ref.shape[0] // 2):
        put_levels(
            scattered(field_ref[kp], chunks, weighted_ref, turned_ref, place_ref, 2 * kp),
            kp,
            out_ref,
        )
    finish_zonal(ring_ref[0], ring_ref[1], out_ref, head_ref, tail_ref)


def adjoint_end_kernel(
    other_ref, p_ref, q_ref, turned_ref, place_ref, kept_ref, ring_ref,
    out_ref, head_ref, tail_ref,
    weighted_ref, *, base,
):
    half, n = other_ref.shape[0], p_ref.shape[0]
    sums = ((other_ref, 0), (p_ref, half), (q_ref, half + 2 * n))
    chunks = weigh(sums, turned_ref, weighted_ref)
    for kp in range(out_ref.shape[0] // 2):
        k = base + 2 * kp
        put_levels(
            scattered(kept_ref[k // 2], chunks, weighted_ref, turned_ref, place_ref, k),
            kp,
            out_ref,
        )
    finish_zonal(ring_ref[0], ring_ref[1], out_ref, head_ref, tail_ref)


def panel_part(north_ref, own_ref, south_ref, probes_ref, panel_ref, base):
    levels, rows, cols, width = own_ref.shape

    def level_pass(k, carry):
        for j in range(cols // 8):
            cut = pl.ds(8 * j, 8)
            panel_ref[k, :, cut, :] = probes_ref[base + k, :, cut, :] + meridional(
                k, j, north_ref, own_ref, south_ref
            )
        hi, lo = split(panel_ref[k].reshape(rows * cols, width))
        turn = (((0,), (0,)), ((), ()))
        cross = lax.dot_general(hi, lo, turn, preferred_element_type=F32)
        main = lax.dot_general(hi, hi, turn, preferred_element_type=F32)
        return carry[0] + main, carry[1] + cross

    zero = jnp.zeros((width, width), F32)
    main, cross = lax.fori_loop(0, levels, level_pass, (zero, zero))
    return main + (cross + cross.T)


def panel_kernel(north_ref, own_ref, south_ref, probes_ref, panel_ref, gram_ref):
    gram_ref[...] = panel_part(north_ref, own_ref, south_ref, probes_ref, panel_ref, 0)


def panel_end_kernel(
    north_ref, own_ref, south_ref, probes_ref, before_ref, panel_ref, packed_ref, *, base
):
    gram = before_ref[...] + panel_part(
        north_ref, own_ref, south_ref, probes_ref, panel_ref, base
    )
    packed_ref[...] = packed_gram(gram)


def packed_gram(gram):
    width = gram.shape[0]
    mid = width // 2
    row = lax.broadcasted_iota(jnp.int32, (mid, width), 0)
    col = lax.broadcasted_iota(jnp.int32, (mid, width), 1)
    top, low = gram[:mid], pltpu.roll(gram[mid:], mid, axis=1)
    body = jnp.where(col >= row, top, low)
    diag = jnp.sum(jnp.where(col == row, low, 0.0), axis=0, keepdims=True)
    return jnp.concatenate([body, jnp.broadcast_to(diag, (8, width))], axis=0)


def unpacked_gram(packed):
    width = packed.shape[1]
    mid = width // 2
    row = lax.broadcasted_iota(jnp.int32, (mid, width), 0)
    col = lax.broadcasted_iota(jnp.int32, (mid, width), 1)
    body = packed[:mid]
    turned = jnp.concatenate([body, body], axis=0).T
    top = jnp.where(col >= row, body, turned[:mid])
    far = col - mid
    body, flip = pltpu.roll(body, mid, axis=1), pltpu.roll(turned[:mid], mid, axis=1)
    diag = pltpu.roll(packed[mid:], mid, axis=1)[:1]
    corner = jnp.where(row > far, body, jnp.where(row < far, flip, diag))
    return jnp.concatenate([top, jnp.where(col < mid, turned[mid:], corner)], axis=0)


BLOCK = 8


def split3(x):
    hi, rest = split(x)
    mid = (x - hi.astype(F32)).astype(BF16)
    lo = (x - hi.astype(F32) - mid.astype(F32)).astype(BF16)
    return hi, mid, lo


def factor_kernel(gram_ref, low_ref, high_ref, q_ref, rfac_ref, both_ref, inv_ref, *, scale):
    width = gram_ref.shape[1]
    down = lax.broadcasted_iota(jnp.int32, (BLOCK, width), 0)
    along = lax.broadcasted_iota(jnp.int32, (BLOCK, width), 1)
    rows_all = lax.broadcasted_iota(jnp.int32, (width, width), 0)
    cols_all = lax.broadcasted_iota(jnp.int32, (width, width), 1)
    both_ref[:, :width] = unpacked_gram(gram_ref[...]) * scale
    both_ref[:, width:] = jnp.where(rows_all == cols_all, 1.0, 0.0)
    for start in range(0, width, BLOCK):
        block = both_ref[start : start + BLOCK, :]
        a, w = block[:, :width], block[:, width:]
        a = jnp.where(along >= start, a, 0.0)
        lanes = [
            jnp.broadcast_to(a[:, start + b : start + b + 1], (BLOCK, width)) for b in range(BLOCK)
        ]
        roots = jnp.zeros((BLOCK, width), F32)
        for p in range(BLOCK):
            pivot = jnp.broadcast_to(lanes[p][p : p + 1], (BLOCK, width))
            root = lax.rsqrt(pivot)
            root = root * (1.5 - 0.5 * pivot * root * root)
            roots = jnp.where(down == p, root, roots)
            if p == BLOCK - 1:
                break
            f = jnp.where(down > p, lanes[p] * (root * root), 0.0)
            for b in range(p + 1, BLOCK):
                lanes[b] = lanes[b] - f * lanes[b][p : p + 1]
            a = a - f * a[p : p + 1]
            w = w - f * w[p : p + 1]
        u = jnp.where(along >= down + start, a * roots, 0.0)
        w = w * roots
        rfac_ref[start : start + BLOCK, :] = u
        inv_ref[start : start + BLOCK, :] = w
        if start + BLOCK < width:
            right = jnp.concatenate([u, w], axis=1)
            uh, um, ul = split3(u)
            rh, rm, rl = split3(right)
            left = jnp.concatenate([uh, uh, um, uh, ul, um], axis=0)
            right = jnp.concatenate([rh, rm, rh, rl, rh, rm], axis=0)
            both_ref[...] -= lax.dot_general(
                left, right, (((0,), (0,)), ((), ())), preferred_element_type=F32
            )
    ih, il = split(inv_ref[...])
    turn = (((1,), (1,)), ((), ()))
    for src_ref, base in ((low_ref, 0), (high_ref, low_ref.shape[0])):
        for k in range(src_ref.shape[0]):
            hi, lo = split(src_ref[k])
            q_ref[base + k] = lax.dot_general(hi, ih, turn, preferred_element_type=F32) + (
                lax.dot_general(lo, ih, turn, preferred_element_type=F32)
                + lax.dot_general(hi, il, turn, preferred_element_type=F32)
            )


def steps(axis_size, fn):
    return [(i, fn(i)) for i in range(axis_size)]


def core_swap(n):
    return steps(n, lambda l: l ^ 1)


def ring_swap(n, odd):
    chips = n // 2

    def partner(l):
        y = l >> 1
        y = chips - 1 - y if odd else y ^ 1
        return (y << 1) | (l & 1)

    return steps(n, partner)


def level_sum(other, first, second, meanwhile):
    n = lax.axis_size("lev")
    core, even, odd = core_swap(n), ring_swap(n, False), ring_swap(n, True)

    def send(x, perm):
        return lax.ppermute(x, "lev", perm)

    def reduced(x, perm):
        mid = x.shape[0] // 2
        return x[mid:] + send(x[:mid], perm)

    def summed(x, perm):
        return x + send(x, perm)

    together = lax.optimization_barrier
    mine = send(other, core)
    mid = first.shape[0]
    p, q = first + mine[:mid], second + mine[mid:]
    p, q = together((reduced(p, even), reduced(q, odd)))
    p, q = together((summed(p, odd), summed(q, even)))
    *got, used = together((send(p, even), send(q, odd), meanwhile(p, q)))
    own = jnp.concatenate([got[0], p, got[1], q])
    return send(own, core), got, used


def own_order():
    l = lax.axis_index("lev")
    y, c = l >> 1, l & 1
    first, second = (y ^ (y >> 1)) & 1, y >> 1
    keep = (1 - c) << 4
    one = keep | ((1 - first) << 2)
    two = keep | ((1 - second) << 2)
    return one, two


def gram_sum(x):
    n, m = lax.axis_size("lev"), lax.axis_size("tile")

    for perm in (core_swap(n), ring_swap(n, False), ring_swap(n, True)):
        x = x + lax.ppermute(x, "lev", perm)
    for fn in (
        lambda t: t ^ 1,
        lambda t: (t & ~3) | (3 - (t & 3)),
        lambda t: (t & ~7) | (7 - (t & 7)),
        lambda t: t ^ 8,
        lambda t: (t & 7) | ((3 - (t >> 3)) << 3),
    ):
        x = x + lax.ppermute(x, "tile", steps(m, fn))
    return x


def from_neighbours(lower_piece, upper_piece, axis):
    count = lax.axis_size(axis)
    below = lax.ppermute(lower_piece, axis, [(i, i + 1) for i in range(count - 1)])
    above = lax.ppermute(upper_piece, axis, [(i + 1, i) for i in range(count - 1)])
    return below, above


PARAMS = pltpu.CompilerParams(vmem_limit_bytes=16 << 20)


def shape(*dims, dtype=F32):
    return jax.ShapeDtypeStruct(dims, dtype)


NEAR = ((0, 4), (4, 4))
PARTS = ((0, 4), (4, 4))
tied = lax.optimization_barrier


def call(kernel, outs, *args, scratch=(), name=None, **static):
    def body(*refs):
        kernel(*refs, **static)

    return pl.pallas_call(
        body,
        out_shape=outs,
        scratch_shapes=list(scratch),
        compiler_params=PARAMS,
        name=name,
    )(*args)


def shards(probes, sigma, obs_count, obs_cell, obs_rinv, obs_jac):
    levels, rows, cols, width = probes.shape
    cells = rows * cols
    rim = REACH * cols
    bins, slots = obs_cell.shape
    total = bins * slots
    half = total // 2
    ring = jnp.stack(split(jnp.asarray(ring_matrix(cols, 256))))

    def field(n):
        return (shape(n, cells, width), shape(n, rim, width), shape(n, rim, width))

    def banded(across, head, tail):
        n = across.shape[0]
        north, south = from_neighbours(tail, head, "tile")
        edge = (n, REACH, cols, width)
        return north.reshape(edge), across.reshape(n, rows, cols, width), south.reshape(edge)

    flat = probes.reshape(levels, cells, width)

    def rims(after, base, n):
        source = flat if after is None else tied((flat, after))[0]
        edge = shape(n, rim, width)
        head, tail = call(
            rim_kernel, (edge, edge), source, ring, base=base, name="rim" + str(base)
        )
        north, south = from_neighbours(tail, head, "tile")
        return north.reshape(n, REACH, cols, width), south.reshape(n, REACH, cols, width)

    near = rims(None, *NEAR[0])
    local = jnp.concatenate(
        [obs_jac, sigma.reshape(levels, cells // slots, slots).transpose(1, 0, 2)]
    )
    below, above = from_neighbours(local, local, "lev")
    live = jnp.arange(slots, dtype=jnp.int32)[None, :] < obs_count[:, None]
    extra = jnp.stack([jnp.where(live, obs_rinv, 0.0), obs_cell.astype(F32)], axis=1)
    packed = call(
        pack_kernel, shape(bins, 3 * levels + 2, slots), below, local, above, extra, name="pack"
    )
    sent = lax.all_to_all(packed, "tile", split_axis=0, concat_axis=0, tiled=True)
    turned, pick, place = call(
        prepare_kernel,
        (
            shape(total, 2 * levels),
            shape(total, cells, dtype=BF16),
            shape(cells, total, dtype=BF16),
        ),
        sent, below, local, above, name="prepare",
    )
    far = rims(packed, *NEAR[1])

    def grid(n):
        return pltpu.VMEM((n, rows, cols, width), F32)

    base, n = NEAR[0]
    other, own = call(
        column_kernel, (shape(half, width), shape(half, width)),
        *near, flat, ring, turned, pick, scratch=[grid(n), grid(n)], name="column",
    )
    base, n = NEAR[1]
    wide = shape(n // 2, cells, 2 * width, dtype=BF16)
    other, high, low = call(
        column_other_kernel, (shape(half, width), wide, wide),
        *far, flat, ring, other, turned, pick,
        scratch=[grid(n), grid(n)], base=base, name="column_other",
    )
    first, second = call(
        column_own_kernel, (shape(half // 2, width), shape(half // 2, width)),
        high, low, own, turned, pick, base=base, name="column_own",
    )
    def weights(n):
        return [pltpu.VMEM((n, width), F32)]

    wide = (cells, 2 * width)

    def scatter_kept(p, q):
        return call(
            kept_kernel, shape(levels // 2, *wide), p, q, turned, place,
            scratch=weights(half // 2), name="kept",
        )

    other, got, field_kept = level_sum(other, first, second, scatter_kept)
    base, n = PARTS[0]
    field_own = call(
        own_kernel, shape(n // 2, *wide), *got, turned, place, field_kept,
        scratch=weights(half // 2), name="own",
    )
    near = call(
        adjoint_kernel, field(n), other, turned, place, field_own, ring,
        scratch=weights(half), name="adjoint",
    )
    other, _ = tied((other, near[1]))
    fields = [banded(*near)]
    base, n = PARTS[1]
    near = call(
        adjoint_end_kernel, field(n), other, *got, turned, place, field_kept, ring,
        scratch=weights(half + half // 2), base=base, name="adjoint_end",
    )
    fields.append(banded(*near))

    base, n = PARTS[0]
    first, gram = pl.pallas_call(
        panel_kernel,
        out_shape=(shape(n, rows, cols, width), shape(width, width)),
        compiler_params=PARAMS,
        name="panel",
    )(*fields[0], probes)
    base, n = PARTS[1]

    def end_body(*refs):
        panel_end_kernel(*refs, base=base)

    second, gram = pl.pallas_call(
        end_body,
        out_shape=(shape(n, rows, cols, width), shape(width // 2 + 8, width)),
        compiler_params=PARAMS,
        name="panel_end",
    )(*fields[1], probes, gram)
    panels = [p.reshape(-1, cells, width) for p in (first, second)]
    gram = gram_sum(gram)
    whole = cells * levels * lax.axis_size("tile") * lax.axis_size("lev")

    def factor_body(*refs):
        factor_kernel(*refs, scale=1.0 / whole)

    qpanel, rfac = pl.pallas_call(
        factor_body,
        out_shape=(shape(levels, cells, width), shape(width, width)),
        scratch_shapes=[pltpu.VMEM((width, 2 * width), F32), pltpu.VMEM((width, width), F32)],
        compiler_params=PARAMS,
        name="factor",
    )(gram, *panels)
    return (qpanel.reshape(probes.shape), rfac)


def solution(mesh):
    in_specs = (
        P("lev", "tile", None, None),
        P("lev", "tile", None),
        P("tile"),
        P("tile", None),
        P("tile", None),
        P("tile", "lev", None),
    )
    out_specs = (P("lev", "tile", None, None), P())
    return jax.shard_map(shards, mesh=mesh, in_specs=in_specs, out_specs=out_specs, check_vma=False)
```

```python
import math

import jax
import jax.numpy as jnp
import numpy as np
from jax import lax
from jax.experimental import pallas as pl
from jax.experimental.pallas import tpu as pltpu
from jax.sharding import PartitionSpec as P

F32 = jnp.float32
BF16 = jnp.bfloat16
REACH = 7


def tap_weights():
    profile = [math.exp(-(offset / 6.0) * (offset / 6.0)) for offset in range(-7, 8)]
    scaling = math.sqrt(sum((element * element for element in profile)))
    return [element / scaling for element in profile]


TAPS = tap_weights()


def ring_matrix(cols, size):
    one = np.zeros((cols, cols), np.float64)
    for c in range(cols):
        for d in range(-REACH, REACH + 1):
            one[c, (c + d) % cols] += TAPS[d + REACH]
    return np.kron(np.eye(size // cols), one).astype(np.float32)


def level_matrix(levels):
    at = (levels, 3 * levels)
    d = lax.broadcasted_iota(jnp.int32, at, 1) - lax.broadcasted_iota(jnp.int32, at, 0) - levels
    band = jnp.zeros(at, F32)
    for offset in range(-REACH, REACH + 1):
        band = jnp.where(d == offset, TAPS[offset + REACH], band)
    return band


def split(x):
    hi = x.astype(BF16)
    return hi, (x - hi.astype(F32)).astype(BF16)


def dot(a, b):
    return jnp.dot(a, b, preferred_element_type=F32)


def zonal(mhi, mlo, pair):
    outs = []
    for h in range(2):
        hi, lo = split(pair[256 * h : 256 * h + 256])
        outs.append(dot(mhi, hi) + (dot(mlo, hi) + dot(mhi, lo)))
    return jnp.concatenate(outs, axis=0)


def put_levels(pair, kp, out_ref):
    width = out_ref.shape[-1]
    for j in range(2):
        out_ref[2 * kp + j] = pair[:, width * j : width * j + width]


def finish_zonal(mhi, mlo, out_ref, head_ref, tail_ref):
    levels, cells, _ = out_ref.shape
    rim = head_ref.shape[1]
    for kp in range(levels // 2):
        pair = jnp.concatenate([out_ref[2 * kp], out_ref[2 * kp + 1]], axis=1)
        put_levels(zonal(mhi, mlo, pair), kp, out_ref)
    for k in range(levels):
        head_ref[k] = out_ref[k, :rim]
        tail_ref[k] = out_ref[k, cells - rim :]


def rim_kernel(field_ref, ring_ref, head_ref, tail_ref, *, base):
    rim = head_ref.shape[1]
    mhi, mlo = ring_ref[0], ring_ref[1]
    for kp in range(head_ref.shape[0] // 2):
        k = base + 2 * kp
        pair = zonal(mhi, mlo, jnp.concatenate([field_ref[k], field_ref[k + 1]], axis=1))
        cells, wide = pair.shape
        for j in range(2):
            part = pair[:, wide // 2 * j : wide // 2 * (j + 1)]
            head_ref[2 * kp + j] = part[:rim]
            tail_ref[2 * kp + j] = part[cells - rim :]


def meridional(k, j, north_ref, own_ref, south_ref):
    cut = pl.ds(8 * j, 8)
    rows = jnp.concatenate(
        [north_ref[k, :, cut, :], own_ref[k, :, cut, :], south_ref[k, :, cut, :]], axis=0
    )
    length = own_ref.shape[1]
    total = TAPS[REACH] * rows[REACH : REACH + length]
    for d in range(1, REACH + 1):
        total = total + TAPS[REACH + d] * (
            rows[REACH - d : REACH - d + length] + rows[REACH + d : REACH + d + length]
        )
    return total


CHUNK = 1024
GROUP = 256


def source_at(order, position):
    return position ^ jnp.where((position >> 3) & 1 == 0, order[0], order[1])


def pack_kernel(below_ref, local_ref, above_ref, rinv_ref, cell_ref, packed_ref):
    levels = local_ref.shape[1]
    for s in range(rinv_ref.shape[0]):
        packed_ref[s, :levels] = below_ref[s]
        packed_ref[s, levels : 2 * levels] = local_ref[s]
        packed_ref[s, 2 * levels : 3 * levels] = above_ref[s]
        packed_ref[s, 3 * levels : 3 * levels + 1] = rinv_ref[s : s + 1]
        packed_ref[s, 3 * levels + 1 :] = cell_ref[s : s + 1].astype(F32)


def prepare_kernel(
    sent_ref, below_ref, local_ref, above_ref,
    turned_ref, pick_ref, place_ref,
):
    sources, deep, slots = sent_ref.shape
    cells = place_ref.shape[0]
    levels = local_ref.shape[1]
    wide = 3 * levels
    band, order = level_matrix(levels), own_order()
    sigma = jnp.concatenate(
        [
            jnp.concatenate([below_ref[i], local_ref[i], above_ref[i]], axis=0)
            for i in range(sources, local_ref.shape[0])
        ],
        axis=1,
    )
    stacked = jnp.concatenate(split(sigma), axis=0)
    cell_down = lax.broadcasted_iota(jnp.int32, (cells, slots), 0).astype(F32)
    cell_along = lax.broadcasted_iota(jnp.int32, (slots, cells), 1).astype(F32)

    def pair_pass(first):
        froms = [source_at(order, first + i) for i in range(2)]
        hots = []
        for source in froms:
            here = sent_ref[source, deep - 1 : deep]
            hots.append(jnp.where(cell_down == here, 1.0, 0.0).astype(BF16))
        onehot = jnp.concatenate(hots, axis=1)
        place_ref[:, pl.ds(pl.multiple_of(slots * first, 2 * slots), 2 * slots)] = onehot
        picked = dot(stacked, onehot)
        jac = jnp.concatenate([sent_ref[source, :wide] for source in froms], axis=1)
        spread = jnp.dot(
            band,
            jac * (picked[:wide] + picked[wide:]),
            precision=lax.Precision.HIGHEST,
            preferred_element_type=F32,
        )
        for i in range(2):
            at = pl.ds(pl.multiple_of(slots * (first + i), slots), slots)
            extra = jnp.broadcast_to(sent_ref[froms[i], deep - 2 : deep - 1], (levels, slots))
            cell = jnp.broadcast_to(sent_ref[froms[i], deep - 1 : deep], (levels, slots))
            turned_ref[at, :levels] = spread[:, slots * i : slots * i + slots].T
            turned_ref[at, levels:] = extra.T
            pick_ref[at, :] = jnp.where(cell_along == cell.T[:, :1], 1.0, 0.0).astype(BF16)

    def step(g, carry):
        for i in range(4):
            pair_pass(8 * g + 2 * i)
        return carry

    lax.fori_loop(0, sources // 8, step, 0)


def smoothed_rows(north_ref, field_ref, south_ref, ring_ref, near_ref, w_ref, base):
    levels, rows, cols, width = w_ref.shape
    mhi, mlo = ring_ref[0], ring_ref[1]
    for kp in range(levels // 2):
        k = base + 2 * kp
        pair = zonal(mhi, mlo, jnp.concatenate([field_ref[k], field_ref[k + 1]], axis=1))
        for j in range(2):
            near_ref[2 * kp + j] = pair[:, width * j : width * (j + 1)].reshape(rows, cols, width)

    def level_pass(k, carry):
        for j in range(cols // 8):
            w_ref[k, :, pl.ds(8 * j, 8), :] = meridional(k, j, north_ref, near_ref, south_ref)
        return carry

    lax.fori_loop(0, levels, level_pass, 0)


def level_pair(w_ref, kp):
    _, rows, cols, width = w_ref.shape
    flat = (rows * cols, width)
    return split(
        jnp.concatenate([w_ref[2 * kp].reshape(flat), w_ref[2 * kp + 1].reshape(flat)], axis=1)
    )


def observed(dst_ref, before_ref, turned_ref, pick_ref, pairs, base, start):
    width = dst_ref.shape[1]

    def chunk_pass(c, carry):
        to = pl.ds(pl.multiple_of(c * CHUNK, CHUNK), CHUNK)
        at = pl.ds(pl.multiple_of(start + c * CHUNK, CHUNK), CHUNK)
        pick = pick_ref[at, :]
        total = None
        if before_ref is not None:
            total = before_ref[to, :]
        for kp, (hi, lo) in enumerate(pairs):
            k = base + 2 * kp
            seen = dot(pick, hi) + dot(pick, lo)
            part = (
                turned_ref[at, k : k + 1] * seen[:, :width]
                + turned_ref[at, k + 1 : k + 2] * seen[:, width:]
            )
            total = part if total is None else total + part
        dst_ref[to, :] = total
        return carry

    lax.fori_loop(0, dst_ref.shape[0] // CHUNK, chunk_pass, 0)


def column_kernel(
    north_ref, south_ref, field_ref, ring_ref, turned_ref, pick_ref,
    other_ref, own_ref,
    near_ref, w_ref,
):
    smoothed_rows(north_ref, field_ref, south_ref, ring_ref, near_ref, w_ref, 0)
    pairs = [level_pair(w_ref, kp) for kp in range(w_ref.shape[0] // 2)]
    half = other_ref.shape[0]
    observed(other_ref, None, turned_ref, pick_ref, pairs, 0, 0)
    observed(own_ref, None, turned_ref, pick_ref, pairs, 0, half)


def column_other_kernel(
    north_ref, south_ref, field_ref, ring_ref, before_ref, turned_ref, pick_ref,
    other_ref, hi_ref, lo_ref,
    near_ref, w_ref, *, base,
):
    smoothed_rows(north_ref, field_ref, south_ref, ring_ref, near_ref, w_ref, base)
    pairs = []
    for kp in range(w_ref.shape[0] // 2):
        hi, lo = level_pair(w_ref, kp)
        hi_ref[kp], lo_ref[kp] = hi, lo
        pairs.append((hi, lo))
    observed(other_ref, before_ref, turned_ref, pick_ref, pairs, base, 0)


def column_own_kernel(hi_ref, lo_ref, before_ref, turned_ref, pick_ref, own_ref, *, base):
    pairs = [(hi_ref[kp], lo_ref[kp]) for kp in range(hi_ref.shape[0])]
    observed(own_ref, before_ref, turned_ref, pick_ref, pairs, base, before_ref.shape[0])


def weigh(runs, turned_ref, weighted_ref):
    row = 0
    for sum_ref, start in runs:
        count = sum_ref.shape[0]
        weight = turned_ref[start : start + count, 8:9]
        weighted_ref[row : row + count] = sum_ref[...] * weight
        row += count


def scatter(run, field_ref, weighted_ref, turned_ref, place_ref, k):
    row, start, size, count, stride = run

    def chunk_pass(i, carry):
        to = pl.ds(pl.multiple_of(start + stride * i, size), size)
        weighted = weighted_ref[pl.ds(pl.multiple_of(row + size * i, size), size), :]
        pair = jnp.concatenate(
            [turned_ref[to, k : k + 1] * weighted, turned_ref[to, k + 1 : k + 2] * weighted],
            axis=1,
        )
        hi, lo = split(pair)
        place = place_ref[:, to]
        field_ref[...] += dot(place, hi) + dot(place, lo)
        return carry

    lax.fori_loop(0, count, chunk_pass, 0)


def kept_kernel(p_ref, q_ref, turned_ref, place_ref, field_ref, weighted_ref):
    half, n = turned_ref.shape[0] // 2, p_ref.shape[0]
    weigh(((p_ref, half + n), (q_ref, half + 3 * n)), turned_ref, weighted_ref)
    field_ref[...] = jnp.zeros(field_ref.shape, F32)
    for kp in range(field_ref.shape[0]):
        run = (0, half + n, n, 2, 2 * n)
        scatter(run, field_ref.at[kp], weighted_ref, turned_ref, place_ref, 2 * kp)


def own_kernel(p_ref, q_ref, turned_ref, place_ref, kept_ref, field_ref, weighted_ref):
    half, n = turned_ref.shape[0] // 2, p_ref.shape[0]
    weigh(((p_ref, half), (q_ref, half + 2 * n)), turned_ref, weighted_ref)
    for kp in range(field_ref.shape[0]):
        field_ref[kp] = kept_ref[kp]
        run = (0, half, n, 2, 2 * n)
        scatter(run, field_ref.at[kp], weighted_ref, turned_ref, place_ref, 2 * kp)


def adjoint_kernel(
    other_ref, turned_ref, place_ref, field_ref, ring_ref,
    out_ref, head_ref, tail_ref,
    weighted_ref, sum_ref,
):
    half = other_ref.shape[0]
    weigh(((other_ref, 0),), turned_ref, weighted_ref)
    for kp in range(out_ref.shape[0] // 2):
        sum_ref[...] = field_ref[kp]
        run = (0, 0, CHUNK, half // CHUNK, CHUNK)
        scatter(run, sum_ref, weighted_ref, turned_ref, place_ref, 2 * kp)
        put_levels(sum_ref[...], kp, out_ref)
    finish_zonal(ring_ref[0], ring_ref[1], out_ref, head_ref, tail_ref)


def adjoint_end_kernel(
    other_ref, p_ref, q_ref, turned_ref, place_ref, kept_ref, ring_ref,
    out_ref, head_ref, tail_ref,
    weighted_ref, sum_ref, *, base,
):
    half, n = other_ref.shape[0], p_ref.shape[0]
    runs = ((other_ref, 0), (p_ref, half), (q_ref, half + 2 * n))
    weigh(runs, turned_ref, weighted_ref)
    for kp in range(out_ref.shape[0] // 2):
        k = base + 2 * kp
        sum_ref[...] = kept_ref[k // 2]
        for run in ((0, 0, CHUNK, half // CHUNK, CHUNK), (half, half, n, 2, 2 * n)):
            scatter(run, sum_ref, weighted_ref, turned_ref, place_ref, k)
        put_levels(sum_ref[...], kp, out_ref)
    finish_zonal(ring_ref[0], ring_ref[1], out_ref, head_ref, tail_ref)


def panel_part(north_ref, own_ref, south_ref, probes_ref, panel_ref, base):
    levels, rows, cols, width = own_ref.shape

    def level_pass(k, carry):
        for j in range(cols // 8):
            cut = pl.ds(8 * j, 8)
            panel_ref[k, :, cut, :] = probes_ref[base + k, :, cut, :] + meridional(
                k, j, north_ref, own_ref, south_ref
            )
        hi, lo = split(panel_ref[k].reshape(rows * cols, width))
        turn = (((0,), (0,)), ((), ()))
        cross = lax.dot_general(hi, lo, turn, preferred_element_type=F32)
        main = lax.dot_general(hi, hi, turn, preferred_element_type=F32)
        return carry[0] + main, carry[1] + cross

    zero = jnp.zeros((width, width), F32)
    main, cross = lax.fori_loop(0, levels, level_pass, (zero, zero))
    return main + (cross + cross.T)


def panel_kernel(north_ref, own_ref, south_ref, probes_ref, panel_ref, gram_ref):
    gram_ref[...] = panel_part(north_ref, own_ref, south_ref, probes_ref, panel_ref, 0)


def panel_end_kernel(
    north_ref, own_ref, south_ref, probes_ref, before_ref, panel_ref, packed_ref, *, base
):
    gram = before_ref[...] + panel_part(
        north_ref, own_ref, south_ref, probes_ref, panel_ref, base
    )
    packed_ref[...] = packed_gram(gram)


def packed_gram(gram):
    width = gram.shape[0]
    mid = width // 2
    row = lax.broadcasted_iota(jnp.int32, (mid, width), 0)
    col = lax.broadcasted_iota(jnp.int32, (mid, width), 1)
    top, low = gram[:mid], pltpu.roll(gram[mid:], mid, axis=1)
    body = jnp.where(col >= row, top, low)
    diag = jnp.sum(jnp.where(col == row, low, 0.0), axis=0, keepdims=True)
    return jnp.concatenate([body, jnp.broadcast_to(diag, (8, width))], axis=0)


def unpacked_gram(packed):
    width = packed.shape[1]
    mid = width // 2
    row = lax.broadcasted_iota(jnp.int32, (mid, width), 0)
    col = lax.broadcasted_iota(jnp.int32, (mid, width), 1)
    body = packed[:mid]
    turned = jnp.concatenate([body, body], axis=0).T
    top = jnp.where(col >= row, body, turned[:mid])
    far = col - mid
    body, flip = pltpu.roll(body, mid, axis=1), pltpu.roll(turned[:mid], mid, axis=1)
    diag = pltpu.roll(packed[mid:], mid, axis=1)[:1]
    corner = jnp.where(row > far, body, jnp.where(row < far, flip, diag))
    return jnp.concatenate([top, jnp.where(col < mid, turned[mid:], corner)], axis=0)


BLOCK = 8


def split3(x):
    hi, rest = split(x)
    mid = (x - hi.astype(F32)).astype(BF16)
    lo = (x - hi.astype(F32) - mid.astype(F32)).astype(BF16)
    return hi, mid, lo


def factor_kernel(gram_ref, low_ref, high_ref, q_ref, rfac_ref, both_ref, inv_ref, *, scale):
    width = gram_ref.shape[1]
    down = lax.broadcasted_iota(jnp.int32, (BLOCK, width), 0)
    along = lax.broadcasted_iota(jnp.int32, (BLOCK, width), 1)
    rows_all = lax.broadcasted_iota(jnp.int32, (width, width), 0)
    cols_all = lax.broadcasted_iota(jnp.int32, (width, width), 1)
    both_ref[:, :width] = unpacked_gram(gram_ref[...]) * scale
    both_ref[:, width:] = jnp.where(rows_all == cols_all, 1.0, 0.0)
    for start in range(0, width, BLOCK):
        block = both_ref[start : start + BLOCK, :]
        a, w = block[:, :width], block[:, width:]
        a = jnp.where(along >= start, a, 0.0)
        lanes = [
            jnp.broadcast_to(a[:, start + b : start + b + 1], (BLOCK, width)) for b in range(BLOCK)
        ]
        pivots = jnp.zeros((BLOCK, width), F32)
        for p in range(BLOCK):
            pivot = jnp.broadcast_to(lanes[p][p : p + 1], (BLOCK, width))
            pivots = jnp.where(down == p, pivot, pivots)
            if p == BLOCK - 1:
                break
            f = jnp.where(down > p, lanes[p] * (1.0 / pivot), 0.0)
            for b in range(p + 1, BLOCK):
                lanes[b] = lanes[b] - f * lanes[b][p : p + 1]
            a = a - f * a[p : p + 1]
            w = w - f * w[p : p + 1]
        roots = lax.rsqrt(pivots)
        roots = roots * (1.5 - 0.5 * pivots * roots * roots)
        u = jnp.where(along >= down + start, a * roots, 0.0)
        w = w * roots
        rfac_ref[start : start + BLOCK, :] = u
        inv_ref[start : start + BLOCK, :] = w
        if start + BLOCK < width:
            right = jnp.concatenate([u, w], axis=1)
            uh, um, ul = split3(u)
            rh, rm, rl = split3(right)
            left = jnp.concatenate([uh, uh, um, uh, ul, um], axis=0)
            right = jnp.concatenate([rh, rm, rh, rl, rh, rm], axis=0)
            both_ref[...] -= lax.dot_general(
                left, right, (((0,), (0,)), ((), ())), preferred_element_type=F32
            )
    ih, il = split(inv_ref[...])
    turn = (((1,), (1,)), ((), ()))
    for src_ref, base in ((low_ref, 0), (high_ref, low_ref.shape[0])):
        for k in range(src_ref.shape[0]):
            hi, lo = split(src_ref[k])
            q_ref[base + k] = lax.dot_general(hi, ih, turn, preferred_element_type=F32) + (
                lax.dot_general(lo, ih, turn, preferred_element_type=F32)
                + lax.dot_general(hi, il, turn, preferred_element_type=F32)
            )


def steps(axis_size, fn):
    return [(i, fn(i)) for i in range(axis_size)]


def core_swap(n):
    return steps(n, lambda l: l ^ 1)


def ring_swap(n, odd):
    chips = n // 2

    def partner(l):
        y = l >> 1
        y = chips - 1 - y if odd else y ^ 1
        return (y << 1) | (l & 1)

    return steps(n, partner)


def level_sum(other, own, meanwhile):
    n = lax.axis_size("lev")
    core, even, odd = core_swap(n), ring_swap(n, False), ring_swap(n, True)

    def send(x, perm):
        return lax.ppermute(x, "lev", perm)

    def reduced(x, perm):
        mid = x.shape[0] // 2
        return x[mid:] + send(x[:mid], perm)

    def summed(x, perm):
        return x + send(x, perm)

    together = lax.optimization_barrier
    mine = send(other, core)
    mid = own.shape[0] // 2
    p, q = own[:mid] + mine[:mid], own[mid:] + mine[mid:]
    p, q = together((reduced(p, even), reduced(q, odd)))
    p, q = together((summed(p, odd), summed(q, even)))
    *got, used = together((send(p, even), send(q, odd), meanwhile(p, q)))
    own = jnp.concatenate([got[0], p, got[1], q])
    return send(own, core), got, used


def own_order():
    l = lax.axis_index("lev")
    y, c = l >> 1, l & 1
    first, second = (y ^ (y >> 1)) & 1, y >> 1
    keep = (1 - c) << 4
    one = keep | ((1 - first) << 2)
    two = keep | ((1 - second) << 2)
    return one, two


def gram_sum(x):
    n, m = lax.axis_size("lev"), lax.axis_size("tile")

    for perm in (core_swap(n), ring_swap(n, False), ring_swap(n, True)):
        x = x + lax.ppermute(x, "lev", perm)
    for fn in (
        lambda t: t ^ 1,
        lambda t: (t & ~3) | (3 - (t & 3)),
        lambda t: (t & ~7) | (7 - (t & 7)),
        lambda t: t ^ 8,
        lambda t: (t & 7) | ((3 - (t >> 3)) << 3),
    ):
        x = x + lax.ppermute(x, "tile", steps(m, fn))
    return x


def from_neighbours(lower_piece, upper_piece, axis):
    count = lax.axis_size(axis)
    below = lax.ppermute(lower_piece, axis, [(i, i + 1) for i in range(count - 1)])
    above = lax.ppermute(upper_piece, axis, [(i + 1, i) for i in range(count - 1)])
    return below, above


PARAMS = pltpu.CompilerParams(vmem_limit_bytes=16 << 20)


def shape(*dims, dtype=F32):
    return jax.ShapeDtypeStruct(dims, dtype)


NEAR = ((0, 4), (4, 4))
PARTS = ((0, 4), (4, 4))
tied = lax.optimization_barrier


def call(kernel, outs, *args, scratch=(), name=None, **static):
    def body(*refs):
        kernel(*refs, **static)

    return pl.pallas_call(
        body,
        out_shape=outs,
        scratch_shapes=list(scratch),
        compiler_params=PARAMS,
        name=name,
    )(*args)


def shards(probes, sigma, obs_count, obs_cell, obs_rinv, obs_jac):
    levels, rows, cols, width = probes.shape
    cells = rows * cols
    rim = REACH * cols
    bins, slots = obs_cell.shape
    total = bins * slots
    half = total // 2
    ring = jnp.stack(split(jnp.asarray(ring_matrix(cols, 256))))

    def field(n):
        return (shape(n, cells, width), shape(n, rim, width), shape(n, rim, width))

    def banded(across, head, tail):
        n = across.shape[0]
        north, south = from_neighbours(tail, head, "tile")
        edge = (n, REACH, cols, width)
        return north.reshape(edge), across.reshape(n, rows, cols, width), south.reshape(edge)

    flat = probes.reshape(levels, cells, width)

    def rims(after, base, n):
        source = flat if after is None else tied((flat, after))[0]
        edge = shape(n, rim, width)
        head, tail = call(
            rim_kernel, (edge, edge), source, ring, base=base, name="rim" + str(base)
        )
        north, south = from_neighbours(tail, head, "tile")
        return north.reshape(n, REACH, cols, width), south.reshape(n, REACH, cols, width)

    near = rims(None, *NEAR[0])
    local = jnp.concatenate(
        [obs_jac, sigma.reshape(levels, cells // slots, slots).transpose(1, 0, 2)]
    )
    below, above = from_neighbours(local, local, "lev")
    live = jnp.arange(slots, dtype=jnp.int32)[None, :] < obs_count[:, None]
    rinv = jnp.where(live, obs_rinv, 0.0)
    packed = call(
        pack_kernel, shape(bins, 3 * levels + 2, slots), below, local, above, rinv, obs_cell,
        name="pack"
    )
    sent = lax.all_to_all(packed, "tile", split_axis=0, concat_axis=0, tiled=True)
    turned, pick, place = call(
        prepare_kernel,
        (
            shape(total, 2 * levels),
            shape(total, cells, dtype=BF16),
            shape(cells, total, dtype=BF16),
        ),
        sent, below, local, above, name="prepare",
    )
    far = rims(packed, *NEAR[1])

    def grid(n):
        return pltpu.VMEM((n, rows, cols, width), F32)

    base, n = NEAR[0]
    other, own = call(
        column_kernel, (shape(half, width), shape(half, width)),
        *near, flat, ring, turned, pick, scratch=[grid(n), grid(n)], name="column",
    )
    base, n = NEAR[1]
    wide = shape(n // 2, cells, 2 * width, dtype=BF16)
    other, high, low = call(
        column_other_kernel, (shape(half, width), wide, wide),
        *far, flat, ring, other, turned, pick,
        scratch=[grid(n), grid(n)], base=base, name="column_other",
    )
    own = call(
        column_own_kernel, shape(half, width),
        high, low, own, turned, pick, base=base, name="column_own",
    )

    def weights(n):
        return [pltpu.VMEM((n, width), F32)]

    wide = (cells, 2 * width)

    def scatter_kept(p, q):
        return call(
            kept_kernel, shape(levels // 2, *wide), p, q, turned, place,
            scratch=weights(half // 2), name="kept",
        )

    other, got, field_kept = level_sum(other, own, scatter_kept)
    base, n = PARTS[0]
    field_own = call(
        own_kernel, shape(n // 2, *wide), *got, turned, place, field_kept,
        scratch=weights(half // 2), name="own",
    )
    near = call(
        adjoint_kernel, field(n), other, turned, place, field_own, ring,
        scratch=weights(half) + [pltpu.VMEM(wide, F32)], name="adjoint",
    )
    other, _ = tied((other, near[1]))
    fields = [banded(*near)]
    base, n = PARTS[1]
    near = call(
        adjoint_end_kernel, field(n), other, *got, turned, place, field_kept, ring,
        scratch=weights(half + half // 2) + [pltpu.VMEM(wide, F32)], base=base, name="adjoint_end",
    )
    fields.append(banded(*near))

    base, n = PARTS[0]
    first, gram = pl.pallas_call(
        panel_kernel,
        out_shape=(shape(n, rows, cols, width), shape(width, width)),
        compiler_params=PARAMS,
        name="panel",
    )(*fields[0], probes)
    base, n = PARTS[1]

    def end_body(*refs):
        panel_end_kernel(*refs, base=base)

    second, gram = pl.pallas_call(
        end_body,
        out_shape=(shape(n, rows, cols, width), shape(width // 2 + 8, width)),
        compiler_params=PARAMS,
        name="panel_end",
    )(*fields[1], probes, gram)
    panels = [p.reshape(-1, cells, width) for p in (first, second)]
    gram = gram_sum(gram)
    whole = cells * levels * lax.axis_size("tile") * lax.axis_size("lev")

    def factor_body(*refs):
        factor_kernel(*refs, scale=1.0 / whole)

    qpanel, rfac = pl.pallas_call(
        factor_body,
        out_shape=(shape(levels, cells, width), shape(width, width)),
        scratch_shapes=[pltpu.VMEM((width, 2 * width), F32), pltpu.VMEM((width, width), F32)],
        compiler_params=PARAMS,
        name="factor",
    )(gram, *panels)
    return (qpanel.reshape(probes.shape), rfac)


def solution(mesh):
    in_specs = (
        P("lev", "tile", None, None),
        P("lev", "tile", None),
        P("tile"),
        P("tile", None),
        P("tile", None),
        P("tile", "lev", None),
    )
    out_specs = (P("lev", "tile", None, None), P())
    return jax.shard_map(shards, mesh=mesh, in_specs=in_specs, out_specs=out_specs, check_vma=False)
```

```python
import math

import jax
import jax.numpy as jnp
import numpy as np
from jax import lax
from jax.experimental import pallas as pl
from jax.experimental.pallas import tpu as pltpu
from jax.sharding import PartitionSpec as P

F32 = jnp.float32
BF16 = jnp.bfloat16
REACH = 7


def tap_weights():
    profile = [math.exp(-(offset / 6.0) * (offset / 6.0)) for offset in range(-7, 8)]
    scaling = math.sqrt(sum((element * element for element in profile)))
    return [element / scaling for element in profile]


TAPS = tap_weights()


def ring_matrix(cols, size):
    one = np.zeros((cols, cols), np.float64)
    for c in range(cols):
        for d in range(-REACH, REACH + 1):
            one[c, (c + d) % cols] += TAPS[d + REACH]
    return np.kron(np.eye(size // cols), one).astype(np.float32)


def level_matrix(levels):
    at = (levels, 3 * levels)
    d = lax.broadcasted_iota(jnp.int32, at, 1) - lax.broadcasted_iota(jnp.int32, at, 0) - levels
    band = jnp.zeros(at, F32)
    for offset in range(-REACH, REACH + 1):
        band = jnp.where(d == offset, TAPS[offset + REACH], band)
    return band


def split(x):
    hi = x.astype(BF16)
    return hi, (x - hi.astype(F32)).astype(BF16)


def dot(a, b):
    return jnp.dot(a, b, preferred_element_type=F32)


def zonal(mhi, mlo, pair):
    outs = []
    for h in range(2):
        hi, lo = split(pair[256 * h : 256 * h + 256])
        outs.append(dot(mhi, hi) + (dot(mlo, hi) + dot(mhi, lo)))
    return jnp.concatenate(outs, axis=0)


def put_levels(pair, kp, out_ref):
    width = out_ref.shape[-1]
    for j in range(2):
        out_ref[2 * kp + j] = pair[:, width * j : width * j + width]


def finish_zonal(mhi, mlo, out_ref, head_ref, tail_ref):
    levels, cells, _ = out_ref.shape
    rim = head_ref.shape[1]
    for kp in range(levels // 2):
        pair = jnp.concatenate([out_ref[2 * kp], out_ref[2 * kp + 1]], axis=1)
        put_levels(zonal(mhi, mlo, pair), kp, out_ref)
    for k in range(levels):
        head_ref[k] = out_ref[k, :rim]
        tail_ref[k] = out_ref[k, cells - rim :]


def rim_kernel(field_ref, ring_ref, head_ref, tail_ref, *, base):
    rim = head_ref.shape[1]
    mhi, mlo = ring_ref[0], ring_ref[1]
    for kp in range(head_ref.shape[0] // 2):
        k = base + 2 * kp
        pair = zonal(mhi, mlo, jnp.concatenate([field_ref[k], field_ref[k + 1]], axis=1))
        cells, wide = pair.shape
        for j in range(2):
            part = pair[:, wide // 2 * j : wide // 2 * (j + 1)]
            head_ref[2 * kp + j] = part[:rim]
            tail_ref[2 * kp + j] = part[cells - rim :]


def meridional(k, j, north_ref, own_ref, south_ref):
    cut = pl.ds(8 * j, 8)
    rows = jnp.concatenate(
        [north_ref[k, :, cut, :], own_ref[k, :, cut, :], south_ref[k, :, cut, :]], axis=0
    )
    length = own_ref.shape[1]
    total = TAPS[REACH] * rows[REACH : REACH + length]
    for d in range(1, REACH + 1):
        total = total + TAPS[REACH + d] * (
            rows[REACH - d : REACH - d + length] + rows[REACH + d : REACH + d + length]
        )
    return total


CHUNK = 1024
GROUP = 256


def source_at(order, position):
    return position ^ jnp.where((position >> 3) & 1 == 0, order[0], order[1])


def pack_kernel(below_ref, local_ref, above_ref, rinv_ref, cell_ref, packed_ref):
    levels = local_ref.shape[1]
    for s in range(rinv_ref.shape[0]):
        packed_ref[s, :levels] = below_ref[s]
        packed_ref[s, levels : 2 * levels] = local_ref[s]
        packed_ref[s, 2 * levels : 3 * levels] = above_ref[s]
        packed_ref[s, 3 * levels : 3 * levels + 1] = rinv_ref[s : s + 1]
        packed_ref[s, 3 * levels + 1 :] = cell_ref[s : s + 1].astype(F32)


def prepare_kernel(
    sent_ref, below_ref, local_ref, above_ref,
    turned_ref, pick_ref, place_ref,
):
    sources, deep, slots = sent_ref.shape
    cells = place_ref.shape[0]
    levels = local_ref.shape[1]
    wide = 3 * levels
    band, order = level_matrix(levels), own_order()
    sigma = jnp.concatenate(
        [
            jnp.concatenate([below_ref[i], local_ref[i], above_ref[i]], axis=0)
            for i in range(sources, local_ref.shape[0])
        ],
        axis=1,
    )
    stacked = jnp.concatenate(split(sigma), axis=0)
    cell_down = lax.broadcasted_iota(jnp.int32, (cells, slots), 0).astype(F32)
    cell_along = lax.broadcasted_iota(jnp.int32, (slots, cells), 1).astype(F32)

    def pair_pass(first):
        froms = [source_at(order, first + i) for i in range(2)]
        hots = []
        for source in froms:
            here = sent_ref[source, deep - 1 : deep]
            hots.append(jnp.where(cell_down == here, 1.0, 0.0).astype(BF16))
        onehot = jnp.concatenate(hots, axis=1)
        place_ref[:, pl.ds(pl.multiple_of(slots * first, 2 * slots), 2 * slots)] = onehot
        picked = dot(stacked, onehot)
        jac = jnp.concatenate([sent_ref[source, :wide] for source in froms], axis=1)
        spread = jnp.dot(
            band,
            jac * (picked[:wide] + picked[wide:]),
            precision=lax.Precision.HIGHEST,
            preferred_element_type=F32,
        )
        for i in range(2):
            at = pl.ds(pl.multiple_of(slots * (first + i), slots), slots)
            extra = jnp.broadcast_to(sent_ref[froms[i], deep - 2 : deep - 1], (levels, slots))
            cell = jnp.broadcast_to(sent_ref[froms[i], deep - 1 : deep], (levels, slots))
            turned_ref[at, :levels] = spread[:, slots * i : slots * i + slots].T
            turned_ref[at, levels:] = extra.T
            pick_ref[at, :] = jnp.where(cell_along == cell.T[:, :1], 1.0, 0.0).astype(BF16)

    def step(g, carry):
        for i in range(4):
            pair_pass(8 * g + 2 * i)
        return carry

    lax.fori_loop(0, sources // 8, step, 0)


def smoothed_rows(north_ref, field_ref, south_ref, ring_ref, near_ref, w_ref, base):
    levels, rows, cols, width = w_ref.shape
    mhi, mlo = ring_ref[0], ring_ref[1]
    for kp in range(levels // 2):
        k = base + 2 * kp
        pair = zonal(mhi, mlo, jnp.concatenate([field_ref[k], field_ref[k + 1]], axis=1))
        for j in range(2):
            near_ref[2 * kp + j] = pair[:, width * j : width * (j + 1)].reshape(rows, cols, width)

    def level_pass(k, carry):
        for j in range(cols // 8):
            w_ref[k, :, pl.ds(8 * j, 8), :] = meridional(k, j, north_ref, near_ref, south_ref)
        return carry

    lax.fori_loop(0, levels, level_pass, 0)


def level_pair(w_ref, kp):
    _, rows, cols, width = w_ref.shape
    flat = (rows * cols, width)
    return split(
        jnp.concatenate([w_ref[2 * kp].reshape(flat), w_ref[2 * kp + 1].reshape(flat)], axis=1)
    )


def observed(dst_ref, before_ref, turned_ref, pick_ref, pairs, base, start):
    width = dst_ref.shape[1]

    def chunk_pass(c, carry):
        to = pl.ds(pl.multiple_of(c * CHUNK, CHUNK), CHUNK)
        at = pl.ds(pl.multiple_of(start + c * CHUNK, CHUNK), CHUNK)
        pick = pick_ref[at, :]
        total = None
        if before_ref is not None:
            total = before_ref[at, :]
        for kp, (hi, lo) in enumerate(pairs):
            k = base + 2 * kp
            seen = dot(pick, hi) + dot(pick, lo)
            part = (
                turned_ref[at, k : k + 1] * seen[:, :width]
                + turned_ref[at, k + 1 : k + 2] * seen[:, width:]
            )
            total = part if total is None else total + part
        dst_ref[to, :] = total
        return carry

    lax.fori_loop(0, dst_ref.shape[0] // CHUNK, chunk_pass, 0)


def column_kernel(
    north_ref, south_ref, field_ref, ring_ref, turned_ref, pick_ref,
    part_ref,
    near_ref, w_ref,
):
    smoothed_rows(north_ref, field_ref, south_ref, ring_ref, near_ref, w_ref, 0)
    pairs = [level_pair(w_ref, kp) for kp in range(w_ref.shape[0] // 2)]
    observed(part_ref, None, turned_ref, pick_ref, pairs, 0, 0)


def column_other_kernel(
    north_ref, south_ref, field_ref, ring_ref, before_ref, turned_ref, pick_ref,
    other_ref, hi_ref, lo_ref,
    near_ref, w_ref, *, base,
):
    smoothed_rows(north_ref, field_ref, south_ref, ring_ref, near_ref, w_ref, base)
    pairs = []
    for kp in range(w_ref.shape[0] // 2):
        hi, lo = level_pair(w_ref, kp)
        hi_ref[kp], lo_ref[kp] = hi, lo
        pairs.append((hi, lo))
    observed(other_ref, before_ref, turned_ref, pick_ref, pairs, base, 0)


def column_own_kernel(hi_ref, lo_ref, before_ref, turned_ref, pick_ref, own_ref, *, base):
    pairs = [(hi_ref[kp], lo_ref[kp]) for kp in range(hi_ref.shape[0])]
    observed(own_ref, before_ref, turned_ref, pick_ref, pairs, base, own_ref.shape[0])


def weigh(runs, turned_ref, weighted_ref):
    row = 0
    for sum_ref, start in runs:
        count = sum_ref.shape[0]
        weight = turned_ref[start : start + count, 8:9]
        weighted_ref[row : row + count] = sum_ref[...] * weight
        row += count


def aligned(start, size):
    return pl.ds(start if isinstance(start, int) else pl.multiple_of(start, size), size)


def scatter(run, field_ref, weighted_ref, turned_ref, place_ref, k, unrolled=True):
    row, start, size, count, stride = run

    def chunk(i):
        to = aligned(start + stride * i, size)
        weighted = weighted_ref[aligned(row + size * i, size), :]
        pair = jnp.concatenate(
            [turned_ref[to, k : k + 1] * weighted, turned_ref[to, k + 1 : k + 2] * weighted],
            axis=1,
        )
        hi, lo = split(pair)
        place = place_ref[:, to]
        return dot(place, hi) + dot(place, lo)

    def chunk_pass(i, carry):
        field_ref[...] += chunk(i)
        return carry

    if unrolled:
        field_ref[...] += sum(chunk(i) for i in range(count))
    else:
        lax.fori_loop(0, count, chunk_pass, 0)


def kept_kernel(p_ref, q_ref, turned_ref, place_ref, field_ref, weighted_ref):
    half, n = turned_ref.shape[0] // 2, p_ref.shape[0]
    weigh(((p_ref, half + n), (q_ref, half + 3 * n)), turned_ref, weighted_ref)
    field_ref[...] = jnp.zeros(field_ref.shape, F32)
    for kp in range(field_ref.shape[0]):
        run = (0, half + n, n, 2, 2 * n)
        scatter(run, field_ref.at[kp], weighted_ref, turned_ref, place_ref, 2 * kp, False)


def own_kernel(p_ref, q_ref, turned_ref, place_ref, kept_ref, field_ref, weighted_ref):
    half, n = turned_ref.shape[0] // 2, p_ref.shape[0]
    weigh(((p_ref, half), (q_ref, half + 2 * n)), turned_ref, weighted_ref)
    for kp in range(field_ref.shape[0]):
        field_ref[kp] = kept_ref[kp]
        run = (0, half, n, 2, 2 * n)
        scatter(run, field_ref.at[kp], weighted_ref, turned_ref, place_ref, 2 * kp)


def adjoint_kernel(
    other_ref, turned_ref, place_ref, field_ref, ring_ref,
    out_ref, head_ref, tail_ref,
    weighted_ref, sum_ref,
):
    half = other_ref.shape[0]
    weigh(((other_ref, 0),), turned_ref, weighted_ref)
    for kp in range(out_ref.shape[0] // 2):
        sum_ref[...] = field_ref[kp]
        run = (0, 0, CHUNK, half // CHUNK, CHUNK)
        scatter(run, sum_ref, weighted_ref, turned_ref, place_ref, 2 * kp)
        put_levels(sum_ref[...], kp, out_ref)
    finish_zonal(ring_ref[0], ring_ref[1], out_ref, head_ref, tail_ref)


def adjoint_end_kernel(
    other_ref, p_ref, q_ref, turned_ref, place_ref, kept_ref, ring_ref,
    out_ref, head_ref, tail_ref,
    weighted_ref, sum_ref, *, base,
):
    half, n = other_ref.shape[0], p_ref.shape[0]
    runs = ((other_ref, 0), (p_ref, half), (q_ref, half + 2 * n))
    weigh(runs, turned_ref, weighted_ref)
    for kp in range(out_ref.shape[0] // 2):
        k = base + 2 * kp
        sum_ref[...] = kept_ref[k // 2]
        for run in ((0, 0, CHUNK, half // CHUNK, CHUNK), (half, half, n, 2, 2 * n)):
            scatter(run, sum_ref, weighted_ref, turned_ref, place_ref, k)
        put_levels(sum_ref[...], kp, out_ref)
    finish_zonal(ring_ref[0], ring_ref[1], out_ref, head_ref, tail_ref)


def panel_part(north_ref, own_ref, south_ref, probes_ref, panel_ref, base):
    levels, rows, cols, width = own_ref.shape

    def level_pass(k, carry):
        for j in range(cols // 8):
            cut = pl.ds(8 * j, 8)
            panel_ref[k, :, cut, :] = probes_ref[base + k, :, cut, :] + meridional(
                k, j, north_ref, own_ref, south_ref
            )
        hi, lo = split(panel_ref[k].reshape(rows * cols, width))
        turn = (((0,), (0,)), ((), ()))
        cross = lax.dot_general(hi, lo, turn, preferred_element_type=F32)
        main = lax.dot_general(hi, hi, turn, preferred_element_type=F32)
        return carry[0] + main, carry[1] + cross

    zero = jnp.zeros((width, width), F32)
    main, cross = lax.fori_loop(0, levels, level_pass, (zero, zero))
    return main + (cross + cross.T)


def panel_kernel(north_ref, own_ref, south_ref, probes_ref, panel_ref, gram_ref):
    gram_ref[...] = panel_part(north_ref, own_ref, south_ref, probes_ref, panel_ref, 0)


def panel_end_kernel(
    north_ref, own_ref, south_ref, probes_ref, before_ref, panel_ref, packed_ref, *, base
):
    gram = before_ref[...] + panel_part(
        north_ref, own_ref, south_ref, probes_ref, panel_ref, base
    )
    packed_ref[...] = packed_gram(gram)


def packed_gram(gram):
    width = gram.shape[0]
    mid = width // 2
    row = lax.broadcasted_iota(jnp.int32, (mid, width), 0)
    col = lax.broadcasted_iota(jnp.int32, (mid, width), 1)
    top, low = gram[:mid], pltpu.roll(gram[mid:], mid, axis=1)
    body = jnp.where(col >= row, top, low)
    diag = jnp.sum(jnp.where(col == row, low, 0.0), axis=0, keepdims=True)
    return jnp.concatenate([body, jnp.broadcast_to(diag, (8, width))], axis=0)


def unpacked_gram(packed):
    width = packed.shape[1]
    mid = width // 2
    row = lax.broadcasted_iota(jnp.int32, (mid, width), 0)
    col = lax.broadcasted_iota(jnp.int32, (mid, width), 1)
    body = packed[:mid]
    turned = jnp.concatenate([body, body], axis=0).T
    top = jnp.where(col >= row, body, turned[:mid])
    far = col - mid
    body, flip = pltpu.roll(body, mid, axis=1), pltpu.roll(turned[:mid], mid, axis=1)
    diag = pltpu.roll(packed[mid:], mid, axis=1)[:1]
    corner = jnp.where(row > far, body, jnp.where(row < far, flip, diag))
    return jnp.concatenate([top, jnp.where(col < mid, turned[mid:], corner)], axis=0)


BLOCK = 8


def split3(x):
    hi, rest = split(x)
    mid = (x - hi.astype(F32)).astype(BF16)
    lo = (x - hi.astype(F32) - mid.astype(F32)).astype(BF16)
    return hi, mid, lo


def factor_kernel(gram_ref, low_ref, high_ref, q_ref, rfac_ref, both_ref, inv_ref, *, scale):
    width = gram_ref.shape[1]
    down = lax.broadcasted_iota(jnp.int32, (BLOCK, width), 0)
    along = lax.broadcasted_iota(jnp.int32, (BLOCK, width), 1)
    rows_all = lax.broadcasted_iota(jnp.int32, (width, width), 0)
    cols_all = lax.broadcasted_iota(jnp.int32, (width, width), 1)
    both_ref[:, :width] = unpacked_gram(gram_ref[...]) * scale
    both_ref[:, width:] = jnp.where(rows_all == cols_all, 1.0, 0.0)
    for start in range(0, width, BLOCK):
        block = both_ref[start : start + BLOCK, :]
        a, w = block[:, :width], block[:, width:]
        a = jnp.where(along >= start, a, 0.0)
        lanes = [
            jnp.broadcast_to(a[:, start + b : start + b + 1], (BLOCK, width)) for b in range(BLOCK)
        ]
        pivots = jnp.zeros((BLOCK, width), F32)
        for p in range(BLOCK):
            pivot = jnp.broadcast_to(lanes[p][p : p + 1], (BLOCK, width))
            pivots = jnp.where(down == p, pivot, pivots)
            if p == BLOCK - 1:
                break
            f = jnp.where(down > p, lanes[p] * (1.0 / pivot), 0.0)
            for b in range(p + 1, BLOCK):
                lanes[b] = lanes[b] - f * lanes[b][p : p + 1]
            a = a - f * a[p : p + 1]
            w = w - f * w[p : p + 1]
        roots = lax.rsqrt(pivots)
        roots = roots * (1.5 - 0.5 * pivots * roots * roots)
        u = jnp.where(along >= down + start, a * roots, 0.0)
        w = w * roots
        rfac_ref[start : start + BLOCK, :] = u
        inv_ref[start : start + BLOCK, :] = w
        if start + BLOCK < width:
            right = jnp.concatenate([u, w], axis=1)
            uh, um, ul = split3(u)
            rh, rm, rl = split3(right)
            left = jnp.concatenate([uh, uh, um, uh, ul, um], axis=0)
            right = jnp.concatenate([rh, rm, rh, rl, rh, rm], axis=0)
            both_ref[...] -= lax.dot_general(
                left, right, (((0,), (0,)), ((), ())), preferred_element_type=F32
            )
    ih, il = split(inv_ref[...])
    turn = (((1,), (1,)), ((), ()))
    for src_ref, base in ((low_ref, 0), (high_ref, low_ref.shape[0])):
        for k in range(src_ref.shape[0]):
            hi, lo = split(src_ref[k])
            q_ref[base + k] = lax.dot_general(hi, ih, turn, preferred_element_type=F32) + (
                lax.dot_general(lo, ih, turn, preferred_element_type=F32)
                + lax.dot_general(hi, il, turn, preferred_element_type=F32)
            )


def steps(axis_size, fn):
    return [(i, fn(i)) for i in range(axis_size)]


def core_swap(n):
    return steps(n, lambda l: l ^ 1)


def ring_swap(n, odd):
    chips = n // 2

    def partner(l):
        y = l >> 1
        y = chips - 1 - y if odd else y ^ 1
        return (y << 1) | (l & 1)

    return steps(n, partner)


def level_sum(other, own, meanwhile):
    n = lax.axis_size("lev")
    core, even, odd = core_swap(n), ring_swap(n, False), ring_swap(n, True)

    def send(x, perm):
        return lax.ppermute(x, "lev", perm)

    def reduced(x, perm):
        mid = x.shape[0] // 2
        return x[mid:] + send(x[:mid], perm)

    def summed(x, perm):
        return x + send(x, perm)

    together = lax.optimization_barrier
    mine = send(other, core)
    mid = own.shape[0] // 2
    p, q = own[:mid] + mine[:mid], own[mid:] + mine[mid:]
    p, q = together((reduced(p, even), reduced(q, odd)))
    p, q = together((summed(p, odd), summed(q, even)))
    *got, used = together((send(p, even), send(q, odd), meanwhile(p, q)))
    own = jnp.concatenate([got[0], p, got[1], q])
    return send(own, core), got, used


def own_order():
    l = lax.axis_index("lev")
    y, c = l >> 1, l & 1
    first, second = (y ^ (y >> 1)) & 1, y >> 1
    keep = (1 - c) << 4
    one = keep | ((1 - first) << 2)
    two = keep | ((1 - second) << 2)
    return one, two


def gram_sum(x):
    n, m = lax.axis_size("lev"), lax.axis_size("tile")

    for perm in (core_swap(n), ring_swap(n, False), ring_swap(n, True)):
        x = x + lax.ppermute(x, "lev", perm)
    for fn in (
        lambda t: t ^ 1,
        lambda t: (t & ~3) | (3 - (t & 3)),
        lambda t: (t & ~7) | (7 - (t & 7)),
        lambda t: t ^ 8,
        lambda t: (t & 7) | ((3 - (t >> 3)) << 3),
    ):
        x = x + lax.ppermute(x, "tile", steps(m, fn))
    return x


def from_neighbours(lower_piece, upper_piece, axis):
    count = lax.axis_size(axis)
    below = lax.ppermute(lower_piece, axis, [(i, i + 1) for i in range(count - 1)])
    above = lax.ppermute(upper_piece, axis, [(i + 1, i) for i in range(count - 1)])
    return below, above


PARAMS = pltpu.CompilerParams(vmem_limit_bytes=16 << 20)


def shape(*dims, dtype=F32):
    return jax.ShapeDtypeStruct(dims, dtype)


NEAR = ((0, 4), (4, 4))
PARTS = ((0, 4), (4, 4))
tied = lax.optimization_barrier


def call(kernel, outs, *args, scratch=(), name=None, **static):
    def body(*refs):
        kernel(*refs, **static)

    return pl.pallas_call(
        body,
        out_shape=outs,
        scratch_shapes=list(scratch),
        compiler_params=PARAMS,
        name=name,
    )(*args)


def shards(probes, sigma, obs_count, obs_cell, obs_rinv, obs_jac):
    levels, rows, cols, width = probes.shape
    cells = rows * cols
    rim = REACH * cols
    bins, slots = obs_cell.shape
    total = bins * slots
    half = total // 2
    ring = jnp.stack(split(jnp.asarray(ring_matrix(cols, 256))))

    def field(n):
        return (shape(n, cells, width), shape(n, rim, width), shape(n, rim, width))

    def banded(across, head, tail):
        n = across.shape[0]
        north, south = from_neighbours(tail, head, "tile")
        edge = (n, REACH, cols, width)
        return north.reshape(edge), across.reshape(n, rows, cols, width), south.reshape(edge)

    flat = probes.reshape(levels, cells, width)

    def rims(after, base, n):
        source = flat if after is None else tied((flat, after))[0]
        edge = shape(n, rim, width)
        head, tail = call(
            rim_kernel, (edge, edge), source, ring, base=base, name="rim" + str(base)
        )
        north, south = from_neighbours(tail, head, "tile")
        return north.reshape(n, REACH, cols, width), south.reshape(n, REACH, cols, width)

    near = rims(None, *NEAR[0])
    local = jnp.concatenate(
        [obs_jac, sigma.reshape(levels, cells // slots, slots).transpose(1, 0, 2)]
    )
    below, above = from_neighbours(local, local, "lev")
    live = jnp.arange(slots, dtype=jnp.int32)[None, :] < obs_count[:, None]
    rinv = jnp.where(live, obs_rinv, 0.0)
    packed = call(
        pack_kernel, shape(bins, 3 * levels + 2, slots), below, local, above, rinv, obs_cell,
        name="pack"
    )
    sent = lax.all_to_all(packed, "tile", split_axis=0, concat_axis=0, tiled=True)
    turned, pick, place = call(
        prepare_kernel,
        (
            shape(total, 2 * levels),
            shape(total, cells, dtype=BF16),
            shape(cells, total, dtype=BF16),
        ),
        sent, below, local, above, name="prepare",
    )
    far = rims(packed, *NEAR[1])

    def grid(n):
        return pltpu.VMEM((n, rows, cols, width), F32)

    base, n = NEAR[0]
    column = call(
        column_kernel, shape(total, width),
        *near, flat, ring, turned, pick, scratch=[grid(n), grid(n)], name="column",
    )
    base, n = NEAR[1]
    wide = shape(n // 2, cells, 2 * width, dtype=BF16)
    other, high, low = call(
        column_other_kernel, (shape(half, width), wide, wide),
        *far, flat, ring, column, turned, pick,
        scratch=[grid(n), grid(n)], base=base, name="column_other",
    )
    own = call(
        column_own_kernel, shape(half, width),
        high, low, column, turned, pick, base=base, name="column_own",
    )

    def weights(n):
        return [pltpu.VMEM((n, width), F32)]

    wide = (cells, 2 * width)

    def scatter_kept(p, q):
        return call(
            kept_kernel, shape(levels // 2, *wide), p, q, turned, place,
            scratch=weights(half // 2), name="kept",
        )

    other, got, field_kept = level_sum(other, own, scatter_kept)
    base, n = PARTS[0]
    field_own = call(
        own_kernel, shape(n // 2, *wide), *got, turned, place, field_kept,
        scratch=weights(half // 2), name="own",
    )
    near = call(
        adjoint_kernel, field(n), other, turned, place, field_own, ring,
        scratch=weights(half) + [pltpu.VMEM(wide, F32)], name="adjoint",
    )
    other, _ = tied((other, near[1]))
    fields = [banded(*near)]
    base, n = PARTS[1]
    near = call(
        adjoint_end_kernel, field(n), other, *got, turned, place, field_kept, ring,
        scratch=weights(half + half // 2) + [pltpu.VMEM(wide, F32)], base=base, name="adjoint_end",
    )
    fields.append(banded(*near))

    base, n = PARTS[0]
    first, gram = pl.pallas_call(
        panel_kernel,
        out_shape=(shape(n, rows, cols, width), shape(width, width)),
        compiler_params=PARAMS,
        name="panel",
    )(*fields[0], probes)
    base, n = PARTS[1]

    def end_body(*refs):
        panel_end_kernel(*refs, base=base)

    second, gram = pl.pallas_call(
        end_body,
        out_shape=(shape(n, rows, cols, width), shape(width // 2 + 8, width)),
        compiler_params=PARAMS,
        name="panel_end",
    )(*fields[1], probes, gram)
    panels = [p.reshape(-1, cells, width) for p in (first, second)]
    gram = gram_sum(gram)
    whole = cells * levels * lax.axis_size("tile") * lax.axis_size("lev")

    def factor_body(*refs):
        factor_kernel(*refs, scale=1.0 / whole)

    qpanel, rfac = pl.pallas_call(
        factor_body,
        out_shape=(shape(levels, cells, width), shape(width, width)),
        scratch_shapes=[pltpu.VMEM((width, 2 * width), F32), pltpu.VMEM((width, width), F32)],
        compiler_params=PARAMS,
        name="factor",
    )(gram, *panels)
    return (qpanel.reshape(probes.shape), rfac)


def solution(mesh):
    in_specs = (
        P("lev", "tile", None, None),
        P("lev", "tile", None),
        P("tile"),
        P("tile", None),
        P("tile", None),
        P("tile", "lev", None),
    )
    out_specs = (P("lev", "tile", None, None), P())
    return jax.shard_map(shards, mesh=mesh, in_specs=in_specs, out_specs=out_specs, check_vma=False)
```

```python
import math

import jax
import jax.numpy as jnp
import numpy as np
from jax import lax
from jax.experimental import pallas as pl
from jax.experimental.pallas import tpu as pltpu
from jax.sharding import PartitionSpec as P

F32 = jnp.float32
BF16 = jnp.bfloat16
REACH = 7


def tap_weights():
    profile = [math.exp(-(offset / 6.0) * (offset / 6.0)) for offset in range(-7, 8)]
    scaling = math.sqrt(sum((element * element for element in profile)))
    return [element / scaling for element in profile]


TAPS = tap_weights()


def ring_matrix(cols, size):
    one = np.zeros((cols, cols), np.float64)
    for c in range(cols):
        for d in range(-REACH, REACH + 1):
            one[c, (c + d) % cols] += TAPS[d + REACH]
    return np.kron(np.eye(size // cols), one).astype(np.float32)


def level_matrix(levels):
    at = (levels, 3 * levels)
    d = lax.broadcasted_iota(jnp.int32, at, 1) - lax.broadcasted_iota(jnp.int32, at, 0) - levels
    band = jnp.zeros(at, F32)
    for offset in range(-REACH, REACH + 1):
        band = jnp.where(d == offset, TAPS[offset + REACH], band)
    return band


def split(x):
    hi = x.astype(BF16)
    return hi, (x - hi.astype(F32)).astype(BF16)


def dot(a, b):
    return jnp.dot(a, b, preferred_element_type=F32)


def zonal(mhi, mlo, pair):
    outs = []
    for h in range(2):
        hi, lo = split(pair[256 * h : 256 * h + 256])
        outs.append(dot(mhi, hi) + (dot(mlo, hi) + dot(mhi, lo)))
    return jnp.concatenate(outs, axis=0)


def put_levels(pair, kp, out_ref):
    width = out_ref.shape[-1]
    for j in range(2):
        out_ref[2 * kp + j] = pair[:, width * j : width * j + width]


def finish_zonal(mhi, mlo, out_ref, head_ref, tail_ref):
    levels, cells, _ = out_ref.shape
    rim = head_ref.shape[1]
    for kp in range(levels // 2):
        pair = jnp.concatenate([out_ref[2 * kp], out_ref[2 * kp + 1]], axis=1)
        put_levels(zonal(mhi, mlo, pair), kp, out_ref)
    for k in range(levels):
        head_ref[k] = out_ref[k, :rim]
        tail_ref[k] = out_ref[k, cells - rim :]


def rim_kernel(field_ref, ring_ref, head_ref, tail_ref, *, base):
    rim = head_ref.shape[1]
    mhi, mlo = ring_ref[0], ring_ref[1]
    for kp in range(head_ref.shape[0] // 2):
        k = base + 2 * kp
        pair = zonal(mhi, mlo, jnp.concatenate([field_ref[k], field_ref[k + 1]], axis=1))
        cells, wide = pair.shape
        for j in range(2):
            part = pair[:, wide // 2 * j : wide // 2 * (j + 1)]
            head_ref[2 * kp + j] = part[:rim]
            tail_ref[2 * kp + j] = part[cells - rim :]


def meridional(k, j, north_ref, own_ref, south_ref):
    cut = pl.ds(8 * j, 8)
    rows = jnp.concatenate(
        [north_ref[k, :, cut, :], own_ref[k, :, cut, :], south_ref[k, :, cut, :]], axis=0
    )
    length = own_ref.shape[1]
    total = TAPS[REACH] * rows[REACH : REACH + length]
    for d in range(1, REACH + 1):
        total = total + TAPS[REACH + d] * (
            rows[REACH - d : REACH - d + length] + rows[REACH + d : REACH + d + length]
        )
    return total


CHUNK = 1024
GROUP = 256


def source_at(order, position):
    return position ^ jnp.where((position >> 3) & 1 == 0, order[0], order[1])


def pack_kernel(below_ref, local_ref, above_ref, rinv_ref, cell_ref, packed_ref):
    levels = local_ref.shape[1]
    for s in range(rinv_ref.shape[0]):
        packed_ref[s, :levels] = below_ref[s]
        packed_ref[s, levels : 2 * levels] = local_ref[s]
        packed_ref[s, 2 * levels : 3 * levels] = above_ref[s]
        packed_ref[s, 3 * levels : 3 * levels + 1] = rinv_ref[s : s + 1]
        packed_ref[s, 3 * levels + 1 :] = cell_ref[s : s + 1].astype(F32)


def prepare_kernel(
    sent_ref, below_ref, local_ref, above_ref,
    turned_ref, pick_ref, place_ref,
):
    sources, deep, slots = sent_ref.shape
    cells = place_ref.shape[0]
    levels = local_ref.shape[1]
    wide = 3 * levels
    band, order = level_matrix(levels), own_order()
    sigma = jnp.concatenate(
        [
            jnp.concatenate([below_ref[i], local_ref[i], above_ref[i]], axis=0)
            for i in range(sources, local_ref.shape[0])
        ],
        axis=1,
    )
    stacked = jnp.concatenate(split(sigma), axis=0)
    cell_down = lax.broadcasted_iota(jnp.int32, (cells, slots), 0).astype(F32)
    cell_along = lax.broadcasted_iota(jnp.int32, (slots, cells), 1).astype(F32)

    def pair_pass(first):
        froms = [source_at(order, first + i) for i in range(2)]
        hots = []
        for source in froms:
            here = sent_ref[source, deep - 1 : deep]
            hots.append(jnp.where(cell_down == here, 1.0, 0.0).astype(BF16))
        onehot = jnp.concatenate(hots, axis=1)
        place_ref[:, pl.ds(pl.multiple_of(slots * first, 2 * slots), 2 * slots)] = onehot
        picked = dot(stacked, onehot)
        jac = jnp.concatenate([sent_ref[source, :wide] for source in froms], axis=1)
        spread = jnp.dot(
            band,
            jac * (picked[:wide] + picked[wide:]),
            precision=lax.Precision.HIGHEST,
            preferred_element_type=F32,
        )
        for i in range(2):
            at = pl.ds(pl.multiple_of(slots * (first + i), slots), slots)
            extra = jnp.broadcast_to(sent_ref[froms[i], deep - 2 : deep - 1], (levels, slots))
            cell = jnp.broadcast_to(sent_ref[froms[i], deep - 1 : deep], (levels, slots))
            turned_ref[at, :levels] = spread[:, slots * i : slots * i + slots].T
            turned_ref[at, levels:] = extra.T
            pick_ref[at, :] = jnp.where(cell_along == cell.T[:, :1], 1.0, 0.0).astype(BF16)

    def step(g, carry):
        for i in range(4):
            pair_pass(8 * g + 2 * i)
        return carry

    lax.fori_loop(0, sources // 8, step, 0)


def zonal_rows(field_ref, ring_ref, near_ref, base):
    levels, rows, cols, width = near_ref.shape
    mhi, mlo = ring_ref[0], ring_ref[1]
    for kp in range(levels // 2):
        k = base + 2 * kp
        pair = zonal(mhi, mlo, jnp.concatenate([field_ref[k], field_ref[k + 1]], axis=1))
        for j in range(2):
            near_ref[2 * kp + j] = pair[:, width * j : width * (j + 1)].reshape(rows, cols, width)


def smoothed_rows(north_ref, near_ref, south_ref, w_ref):
    levels, _, cols, _ = w_ref.shape

    def level_pass(k, carry):
        for j in range(cols // 8):
            w_ref[k, :, pl.ds(8 * j, 8), :] = meridional(k, j, north_ref, near_ref, south_ref)
        return carry

    lax.fori_loop(0, levels, level_pass, 0)


def level_pair(w_ref, kp):
    _, rows, cols, width = w_ref.shape
    flat = (rows * cols, width)
    return split(
        jnp.concatenate([w_ref[2 * kp].reshape(flat), w_ref[2 * kp + 1].reshape(flat)], axis=1)
    )


def observed(dst_ref, before_ref, turned_ref, pick_ref, pairs, base, start):
    width = dst_ref.shape[1]

    def chunk_pass(c, carry):
        to = pl.ds(pl.multiple_of(c * CHUNK, CHUNK), CHUNK)
        at = pl.ds(pl.multiple_of(start + c * CHUNK, CHUNK), CHUNK)
        pick = pick_ref[at, :]
        total = None
        if before_ref is not None:
            total = before_ref[at, :]
        for kp, (hi, lo) in enumerate(pairs):
            k = base + 2 * kp
            seen = dot(pick, hi) + dot(pick, lo)
            part = (
                turned_ref[at, k : k + 1] * seen[:, :width]
                + turned_ref[at, k + 1 : k + 2] * seen[:, width:]
            )
            total = part if total is None else total + part
        dst_ref[to, :] = total
        return carry

    lax.fori_loop(0, dst_ref.shape[0] // CHUNK, chunk_pass, 0)


def column_kernel(
    north_ref, south_ref, field_ref, ring_ref, turned_ref, pick_ref,
    part_ref, far_ref,
    near_ref, w_ref,
):
    zonal_rows(field_ref, ring_ref, near_ref, 0)
    zonal_rows(field_ref, ring_ref, far_ref, near_ref.shape[0])
    smoothed_rows(north_ref, near_ref, south_ref, w_ref)
    pairs = [level_pair(w_ref, kp) for kp in range(w_ref.shape[0] // 2)]
    observed(part_ref, None, turned_ref, pick_ref, pairs, 0, 0)


def column_other_kernel(
    north_ref, south_ref, far_ref, before_ref, turned_ref, pick_ref,
    other_ref, hi_ref, lo_ref,
    w_ref, *, base,
):
    smoothed_rows(north_ref, far_ref, south_ref, w_ref)
    pairs = []
    for kp in range(w_ref.shape[0] // 2):
        hi, lo = level_pair(w_ref, kp)
        hi_ref[kp], lo_ref[kp] = hi, lo
        pairs.append((hi, lo))
    observed(other_ref, before_ref, turned_ref, pick_ref, pairs, base, 0)


def column_own_kernel(hi_ref, lo_ref, before_ref, turned_ref, pick_ref, own_ref, *, base):
    pairs = [(hi_ref[kp], lo_ref[kp]) for kp in range(hi_ref.shape[0])]
    observed(own_ref, before_ref, turned_ref, pick_ref, pairs, base, own_ref.shape[0])


def weigh(runs, turned_ref, weighted_ref):
    row = 0
    for sum_ref, start in runs:
        count = sum_ref.shape[0]
        weight = turned_ref[start : start + count, 8:9]
        weighted_ref[row : row + count] = sum_ref[...] * weight
        row += count


def aligned(start, size):
    return pl.ds(start if isinstance(start, int) else pl.multiple_of(start, size), size)


def scatter(run, field_ref, weighted_ref, turned_ref, place_ref, k, unrolled=True):
    row, start, size, count, stride = run

    def chunk(i):
        to = aligned(start + stride * i, size)
        weighted = weighted_ref[aligned(row + size * i, size), :]
        pair = jnp.concatenate(
            [turned_ref[to, k : k + 1] * weighted, turned_ref[to, k + 1 : k + 2] * weighted],
            axis=1,
        )
        hi, lo = split(pair)
        place = place_ref[:, to]
        return dot(place, hi) + dot(place, lo)

    def chunk_pass(i, carry):
        field_ref[...] += chunk(i)
        return carry

    if unrolled:
        field_ref[...] += sum(chunk(i) for i in range(count))
    else:
        lax.fori_loop(0, count, chunk_pass, 0)


def kept_kernel(p_ref, q_ref, turned_ref, place_ref, field_ref, weighted_ref):
    half, n = turned_ref.shape[0] // 2, p_ref.shape[0]
    weigh(((p_ref, half + n), (q_ref, half + 3 * n)), turned_ref, weighted_ref)
    field_ref[...] = jnp.zeros(field_ref.shape, F32)
    for kp in range(field_ref.shape[0]):
        run = (0, half + n, n, 2, 2 * n)
        scatter(run, field_ref.at[kp], weighted_ref, turned_ref, place_ref, 2 * kp, False)


def own_kernel(p_ref, q_ref, turned_ref, place_ref, kept_ref, field_ref, weighted_ref):
    half, n = turned_ref.shape[0] // 2, p_ref.shape[0]
    weigh(((p_ref, half), (q_ref, half + 2 * n)), turned_ref, weighted_ref)
    for kp in range(field_ref.shape[0]):
        field_ref[kp] = kept_ref[kp]
        run = (0, half, n, 2, 2 * n)
        scatter(run, field_ref.at[kp], weighted_ref, turned_ref, place_ref, 2 * kp)


def adjoint_kernel(
    other_ref, turned_ref, place_ref, field_ref, ring_ref,
    out_ref, head_ref, tail_ref,
    weighted_ref, sum_ref,
):
    half = other_ref.shape[0]
    weigh(((other_ref, 0),), turned_ref, weighted_ref)
    for kp in range(out_ref.shape[0] // 2):
        sum_ref[...] = field_ref[kp]
        run = (0, 0, CHUNK, half // CHUNK, CHUNK)
        scatter(run, sum_ref, weighted_ref, turned_ref, place_ref, 2 * kp)
        put_levels(sum_ref[...], kp, out_ref)
    finish_zonal(ring_ref[0], ring_ref[1], out_ref, head_ref, tail_ref)


def adjoint_end_kernel(
    other_ref, p_ref, q_ref, turned_ref, place_ref, kept_ref, ring_ref,
    out_ref, head_ref, tail_ref,
    weighted_ref, sum_ref, *, base,
):
    half, n = other_ref.shape[0], p_ref.shape[0]
    runs = ((other_ref, 0), (p_ref, half), (q_ref, half + 2 * n))
    weigh(runs, turned_ref, weighted_ref)
    for kp in range(out_ref.shape[0] // 2):
        k = base + 2 * kp
        sum_ref[...] = kept_ref[k // 2]
        for run in ((0, 0, CHUNK, half // CHUNK, CHUNK), (half, half, n, 2, 2 * n)):
            scatter(run, sum_ref, weighted_ref, turned_ref, place_ref, k)
        put_levels(sum_ref[...], kp, out_ref)
    finish_zonal(ring_ref[0], ring_ref[1], out_ref, head_ref, tail_ref)


def panel_part(north_ref, own_ref, south_ref, probes_ref, panel_ref, base):
    levels, rows, cols, width = own_ref.shape

    def level_pass(k, carry):
        for j in range(cols // 8):
            cut = pl.ds(8 * j, 8)
            panel_ref[k, :, cut, :] = probes_ref[base + k, :, cut, :] + meridional(
                k, j, north_ref, own_ref, south_ref
            )
        hi, lo = split(panel_ref[k].reshape(rows * cols, width))
        turn = (((0,), (0,)), ((), ()))
        both = jnp.concatenate([hi, lo], axis=1)
        return carry + lax.dot_general(hi, both, turn, preferred_element_type=F32)

    both = lax.fori_loop(0, levels, level_pass, jnp.zeros((width, 2 * width), F32))
    main, cross = both[:, :width], both[:, width:]
    return main + (cross + cross.T)


def panel_kernel(north_ref, own_ref, south_ref, probes_ref, panel_ref, gram_ref):
    gram_ref[...] = panel_part(north_ref, own_ref, south_ref, probes_ref, panel_ref, 0)


def panel_end_kernel(
    north_ref, own_ref, south_ref, probes_ref, before_ref, panel_ref, packed_ref, *, base
):
    gram = before_ref[...] + panel_part(
        north_ref, own_ref, south_ref, probes_ref, panel_ref, base
    )
    packed_ref[...] = packed_gram(gram)


def packed_gram(gram):
    width = gram.shape[0]
    mid = width // 2
    row = lax.broadcasted_iota(jnp.int32, (mid, width), 0)
    col = lax.broadcasted_iota(jnp.int32, (mid, width), 1)
    top, low = gram[:mid], pltpu.roll(gram[mid:], mid, axis=1)
    body = jnp.where(col >= row, top, low)
    diag = jnp.sum(jnp.where(col == row, low, 0.0), axis=0, keepdims=True)
    return jnp.concatenate([body, jnp.broadcast_to(diag, (8, width))], axis=0)


def unpacked_gram(packed):
    width = packed.shape[1]
    mid = width // 2
    row = lax.broadcasted_iota(jnp.int32, (mid, width), 0)
    col = lax.broadcasted_iota(jnp.int32, (mid, width), 1)
    body = packed[:mid]
    turned = jnp.concatenate([body, body], axis=0).T
    top = jnp.where(col >= row, body, turned[:mid])
    far = col - mid
    body, flip = pltpu.roll(body, mid, axis=1), pltpu.roll(turned[:mid], mid, axis=1)
    diag = pltpu.roll(packed[mid:], mid, axis=1)[:1]
    corner = jnp.where(row > far, body, jnp.where(row < far, flip, diag))
    return jnp.concatenate([top, jnp.where(col < mid, turned[mid:], corner)], axis=0)


BLOCK = 8


def split3(x):
    hi, rest = split(x)
    mid = (x - hi.astype(F32)).astype(BF16)
    lo = (x - hi.astype(F32) - mid.astype(F32)).astype(BF16)
    return hi, mid, lo


def factor_kernel(gram_ref, low_ref, high_ref, q_ref, rfac_ref, both_ref, inv_ref, *, scale):
    width = gram_ref.shape[1]
    down = lax.broadcasted_iota(jnp.int32, (BLOCK, width), 0)
    along = lax.broadcasted_iota(jnp.int32, (BLOCK, width), 1)
    rows_all = lax.broadcasted_iota(jnp.int32, (width, width), 0)
    cols_all = lax.broadcasted_iota(jnp.int32, (width, width), 1)
    both_ref[:, :width] = unpacked_gram(gram_ref[...]) * scale
    both_ref[:, width:] = jnp.where(rows_all == cols_all, 1.0, 0.0)
    for start in range(0, width, BLOCK):
        block = both_ref[start : start + BLOCK, :]
        a, w = block[:, :width], block[:, width:]
        a = jnp.where(along >= start, a, 0.0)
        lanes = [
            jnp.broadcast_to(a[:, start + b : start + b + 1], (BLOCK, width)) for b in range(BLOCK)
        ]
        pivots = jnp.zeros((BLOCK, width), F32)
        for p in range(BLOCK):
            pivot = jnp.broadcast_to(lanes[p][p : p + 1], (BLOCK, width))
            pivots = jnp.where(down == p, pivot, pivots)
            if p == BLOCK - 1:
                break
            f = jnp.where(down > p, lanes[p] * (1.0 / pivot), 0.0)
            for b in range(p + 1, BLOCK):
                lanes[b] = lanes[b] - f * lanes[b][p : p + 1]
            a = a - f * a[p : p + 1]
            w = w - f * w[p : p + 1]
        roots = lax.rsqrt(pivots)
        roots = roots * (1.5 - 0.5 * pivots * roots * roots)
        u = jnp.where(along >= down + start, a * roots, 0.0)
        w = w * roots
        rfac_ref[start : start + BLOCK, :] = u
        inv_ref[start : start + BLOCK, :] = w
        if start + BLOCK < width:
            right = jnp.concatenate([u, w], axis=1)
            uh, um, ul = split3(u)
            rh, rm, rl = split3(right)
            left = jnp.concatenate([uh, uh, um, uh, ul, um], axis=0)
            right = jnp.concatenate([rh, rm, rh, rl, rh, rm], axis=0)
            update = lax.dot_general(
                left, right, (((0,), (0,)), ((), ())), preferred_element_type=F32
            )
            both_ref[start + BLOCK :] -= update[start + BLOCK :]
    ih, il = split(inv_ref[...])
    inv_both = jnp.concatenate([ih, il], axis=0)
    turn = (((1,), (1,)), ((), ()))
    for src_ref, base in ((low_ref, 0), (high_ref, low_ref.shape[0])):
        for k in range(src_ref.shape[0]):
            hi, lo = split(src_ref[k])
            wide = lax.dot_general(hi, inv_both, turn, preferred_element_type=F32)
            low = lax.dot_general(lo, ih, turn, preferred_element_type=F32)
            q_ref[base + k] = wide[:, :width] + (low + wide[:, width:])


def steps(axis_size, fn):
    return [(i, fn(i)) for i in range(axis_size)]


def core_swap(n):
    return steps(n, lambda l: l ^ 1)


def ring_swap(n, odd):
    chips = n // 2

    def partner(l):
        y = l >> 1
        y = chips - 1 - y if odd else y ^ 1
        return (y << 1) | (l & 1)

    return steps(n, partner)


def level_sum(other, own, meanwhile):
    n = lax.axis_size("lev")
    core, even, odd = core_swap(n), ring_swap(n, False), ring_swap(n, True)

    def send(x, perm):
        return lax.ppermute(x, "lev", perm)

    def reduced(x, perm):
        mid = x.shape[0] // 2
        return x[mid:] + send(x[:mid], perm)

    def summed(x, perm):
        return x + send(x, perm)

    together = lax.optimization_barrier
    mine = send(other, core)
    mid = own.shape[0] // 2
    p, q = own[:mid] + mine[:mid], own[mid:] + mine[mid:]
    p, q = together((reduced(p, even), reduced(q, odd)))
    p, q = together((summed(p, odd), summed(q, even)))
    *got, used = together((send(p, even), send(q, odd), meanwhile(p, q)))
    own = jnp.concatenate([got[0], p, got[1], q])
    return send(own, core), got, used


def own_order():
    l = lax.axis_index("lev")
    y, c = l >> 1, l & 1
    first, second = (y ^ (y >> 1)) & 1, y >> 1
    keep = (1 - c) << 4
    one = keep | ((1 - first) << 2)
    two = keep | ((1 - second) << 2)
    return one, two


def gram_sum(x):
    n, m = lax.axis_size("lev"), lax.axis_size("tile")

    for perm in (core_swap(n), ring_swap(n, False), ring_swap(n, True)):
        x = x + lax.ppermute(x, "lev", perm)
    for fn in (
        lambda t: t ^ 1,
        lambda t: (t & ~3) | (3 - (t & 3)),
        lambda t: (t & ~7) | (7 - (t & 7)),
        lambda t: t ^ 8,
        lambda t: (t & 7) | ((3 - (t >> 3)) << 3),
    ):
        x = x + lax.ppermute(x, "tile", steps(m, fn))
    return x


def from_neighbours(lower_piece, upper_piece, axis):
    count = lax.axis_size(axis)
    below = lax.ppermute(lower_piece, axis, [(i, i + 1) for i in range(count - 1)])
    above = lax.ppermute(upper_piece, axis, [(i + 1, i) for i in range(count - 1)])
    return below, above


PARAMS = pltpu.CompilerParams(vmem_limit_bytes=16 << 20)


def shape(*dims, dtype=F32):
    return jax.ShapeDtypeStruct(dims, dtype)


NEAR = ((0, 4), (4, 4))
PARTS = ((0, 4), (4, 4))
tied = lax.optimization_barrier


def call(kernel, outs, *args, scratch=(), name=None, **static):
    def body(*refs):
        kernel(*refs, **static)

    return pl.pallas_call(
        body,
        out_shape=outs,
        scratch_shapes=list(scratch),
        compiler_params=PARAMS,
        name=name,
    )(*args)


def shards(probes, sigma, obs_count, obs_cell, obs_rinv, obs_jac):
    levels, rows, cols, width = probes.shape
    cells = rows * cols
    rim = REACH * cols
    bins, slots = obs_cell.shape
    total = bins * slots
    half = total // 2
    ring = jnp.stack(split(jnp.asarray(ring_matrix(cols, 256))))

    def field(n):
        return (shape(n, cells, width), shape(n, rim, width), shape(n, rim, width))

    def banded(across, head, tail):
        n = across.shape[0]
        north, south = from_neighbours(tail, head, "tile")
        edge = (n, REACH, cols, width)
        return north.reshape(edge), across.reshape(n, rows, cols, width), south.reshape(edge)

    flat = probes.reshape(levels, cells, width)

    def rims(after, base, n):
        source = flat if after is None else tied((flat, after))[0]
        edge = shape(n, rim, width)
        head, tail = call(
            rim_kernel, (edge, edge), source, ring, base=base, name="rim" + str(base)
        )
        north, south = from_neighbours(tail, head, "tile")
        return north.reshape(n, REACH, cols, width), south.reshape(n, REACH, cols, width)

    near = rims(None, *NEAR[0])
    local = jnp.concatenate(
        [obs_jac, sigma.reshape(levels, cells // slots, slots).transpose(1, 0, 2)]
    )
    below, above = from_neighbours(local, local, "lev")
    live = jnp.arange(slots, dtype=jnp.int32)[None, :] < obs_count[:, None]
    rinv = jnp.where(live, obs_rinv, 0.0)
    packed = call(
        pack_kernel, shape(bins, 3 * levels + 2, slots), below, local, above, rinv, obs_cell,
        name="pack"
    )
    sent = lax.all_to_all(packed, "tile", split_axis=0, concat_axis=0, tiled=True)
    turned, pick, place = call(
        prepare_kernel,
        (
            shape(total, 2 * levels),
            shape(total, cells, dtype=BF16),
            shape(cells, total, dtype=BF16),
        ),
        sent, below, local, above, name="prepare",
    )
    far = rims(packed, *NEAR[1])

    def grid(n):
        return pltpu.VMEM((n, rows, cols, width), F32)

    base, n = NEAR[0]
    column, far_rows = call(
        column_kernel, (shape(total, width), shape(NEAR[1][1], rows, cols, width)),
        *near, flat, ring, turned, pick, scratch=[grid(n), grid(n)], name="column",
    )
    base, n = NEAR[1]
    wide = shape(n // 2, cells, 2 * width, dtype=BF16)
    other, high, low = call(
        column_other_kernel, (shape(half, width), wide, wide),
        *far, far_rows, column, turned, pick, scratch=[grid(n)], base=base, name="column_other",
    )
    own = call(
        column_own_kernel, shape(half, width),
        high, low, column, turned, pick, base=base, name="column_own",
    )

    def weights(n):
        return [pltpu.VMEM((n, width), F32)]

    wide = (cells, 2 * width)

    def scatter_kept(p, q):
        return call(
            kept_kernel, shape(levels // 2, *wide), p, q, turned, place,
            scratch=weights(half // 2), name="kept",
        )

    other, got, field_kept = level_sum(other, own, scatter_kept)
    base, n = PARTS[0]
    field_own = call(
        own_kernel, shape(n // 2, *wide), *got, turned, place, field_kept,
        scratch=weights(half // 2), name="own",
    )
    near = call(
        adjoint_kernel, field(n), other, turned, place, field_own, ring,
        scratch=weights(half) + [pltpu.VMEM(wide, F32)], name="adjoint",
    )
    other, _ = tied((other, near[1]))
    fields = [banded(*near)]
    base, n = PARTS[1]
    near = call(
        adjoint_end_kernel, field(n), other, *got, turned, place, field_kept, ring,
        scratch=weights(half + half // 2) + [pltpu.VMEM(wide, F32)], base=base, name="adjoint_end",
    )
    fields.append(banded(*near))

    base, n = PARTS[0]
    first, gram = pl.pallas_call(
        panel_kernel,
        out_shape=(shape(n, rows, cols, width), shape(width, width)),
        compiler_params=PARAMS,
        name="panel",
    )(*fields[0], probes)
    base, n = PARTS[1]

    def end_body(*refs):
        panel_end_kernel(*refs, base=base)

    second, gram = pl.pallas_call(
        end_body,
        out_shape=(shape(n, rows, cols, width), shape(width // 2 + 8, width)),
        compiler_params=PARAMS,
        name="panel_end",
    )(*fields[1], probes, gram)
    panels = [p.reshape(-1, cells, width) for p in (first, second)]
    gram = gram_sum(gram)
    whole = cells * levels * lax.axis_size("tile") * lax.axis_size("lev")

    def factor_body(*refs):
        factor_kernel(*refs, scale=1.0 / whole)

    qpanel, rfac = pl.pallas_call(
        factor_body,
        out_shape=(shape(levels, cells, width), shape(width, width)),
        scratch_shapes=[pltpu.VMEM((width, 2 * width), F32), pltpu.VMEM((width, width), F32)],
        compiler_params=PARAMS,
        name="factor",
    )(gram, *panels)
    return (qpanel.reshape(probes.shape), rfac)


def solution(mesh):
    in_specs = (
        P("lev", "tile", None, None),
        P("lev", "tile", None),
        P("tile"),
        P("tile", None),
        P("tile", None),
        P("tile", "lev", None),
    )
    out_specs = (P("lev", "tile", None, None), P())
    return jax.shard_map(shards, mesh=mesh, in_specs=in_specs, out_specs=out_specs, check_vma=False)
```

```python
import math

import jax
import jax.numpy as jnp
import numpy as np
from jax import lax
from jax.experimental import pallas as pl
from jax.experimental.pallas import tpu as pltpu
from jax.sharding import PartitionSpec as P

F32 = jnp.float32
BF16 = jnp.bfloat16
REACH = 7


def tap_weights():
    profile = [math.exp(-(offset / 6.0) * (offset / 6.0)) for offset in range(-7, 8)]
    scaling = math.sqrt(sum((element * element for element in profile)))
    return [element / scaling for element in profile]


TAPS = tap_weights()


def ring_matrix(cols, size):
    one = np.zeros((cols, cols), np.float64)
    for c in range(cols):
        for d in range(-REACH, REACH + 1):
            one[c, (c + d) % cols] += TAPS[d + REACH]
    return np.kron(np.eye(size // cols), one).astype(np.float32)


def level_matrix(levels):
    at = (levels, 3 * levels)
    d = lax.broadcasted_iota(jnp.int32, at, 1) - lax.broadcasted_iota(jnp.int32, at, 0) - levels
    band = jnp.zeros(at, F32)
    for offset in range(-REACH, REACH + 1):
        band = jnp.where(d == offset, TAPS[offset + REACH], band)
    return band


def split(x):
    hi = x.astype(BF16)
    return hi, (x - hi.astype(F32)).astype(BF16)


def dot(a, b):
    return jnp.dot(a, b, preferred_element_type=F32)


def zonal(mhi, mlo, pair):
    outs = []
    for h in range(2):
        hi, lo = split(pair[256 * h : 256 * h + 256])
        outs.append(dot(mhi, hi) + (dot(mlo, hi) + dot(mhi, lo)))
    return jnp.concatenate(outs, axis=0)


def put_levels(pair, kp, out_ref):
    width = out_ref.shape[-1]
    for j in range(2):
        out_ref[2 * kp + j] = pair[:, width * j : width * j + width]


def finish_zonal(mhi, mlo, out_ref, head_ref, tail_ref):
    levels, cells, _ = out_ref.shape
    rim = head_ref.shape[1]
    for kp in range(levels // 2):
        pair = jnp.concatenate([out_ref[2 * kp], out_ref[2 * kp + 1]], axis=1)
        put_levels(zonal(mhi, mlo, pair), kp, out_ref)
    for k in range(levels):
        head_ref[k] = out_ref[k, :rim]
        tail_ref[k] = out_ref[k, cells - rim :]


def rim_kernel(field_ref, ring_ref, head_ref, tail_ref, *, base):
    rim = head_ref.shape[1]
    mhi, mlo = ring_ref[0], ring_ref[1]
    for kp in range(head_ref.shape[0] // 2):
        k = base + 2 * kp
        pair = zonal(mhi, mlo, jnp.concatenate([field_ref[k], field_ref[k + 1]], axis=1))
        cells, wide = pair.shape
        for j in range(2):
            part = pair[:, wide // 2 * j : wide // 2 * (j + 1)]
            head_ref[2 * kp + j] = part[:rim]
            tail_ref[2 * kp + j] = part[cells - rim :]


def meridional(k, j, north_ref, own_ref, south_ref):
    cut = pl.ds(8 * j, 8)
    rows = jnp.concatenate(
        [north_ref[k, :, cut, :], own_ref[k, :, cut, :], south_ref[k, :, cut, :]], axis=0
    )
    length = own_ref.shape[1]
    total = TAPS[REACH] * rows[REACH : REACH + length]
    for d in range(1, REACH + 1):
        total = total + TAPS[REACH + d] * (
            rows[REACH - d : REACH - d + length] + rows[REACH + d : REACH + d + length]
        )
    return total


CHUNK = 1024
GROUP = 256


def source_at(order, position):
    return position ^ jnp.where((position >> 3) & 1 == 0, order[0], order[1])


def pack_kernel(below_ref, local_ref, above_ref, rinv_ref, cell_ref, packed_ref):
    levels = local_ref.shape[1]
    for s in range(rinv_ref.shape[0]):
        packed_ref[s, :levels] = below_ref[s]
        packed_ref[s, levels : 2 * levels] = local_ref[s]
        packed_ref[s, 2 * levels : 3 * levels] = above_ref[s]
        packed_ref[s, 3 * levels : 3 * levels + 1] = rinv_ref[s : s + 1]
        packed_ref[s, 3 * levels + 1 :] = cell_ref[s : s + 1].astype(F32)


def prepare_kernel(
    sent_ref, below_ref, local_ref, above_ref,
    turned_ref, pick_ref, place_ref,
):
    sources, deep, slots = sent_ref.shape
    cells = place_ref.shape[0]
    levels = local_ref.shape[1]
    wide = 3 * levels
    band, order = level_matrix(levels), own_order()
    main = band.astype(BF16).astype(F32)
    taps = jnp.concatenate([main, band - main, main], axis=1).astype(BF16)
    sigma = jnp.concatenate(
        [
            jnp.concatenate([below_ref[i], local_ref[i], above_ref[i]], axis=0)
            for i in range(sources, local_ref.shape[0])
        ],
        axis=1,
    )
    stacked = jnp.concatenate(split(sigma), axis=0)
    cell_down = lax.broadcasted_iota(jnp.int32, (cells, slots), 0).astype(F32)
    cell_along = lax.broadcasted_iota(jnp.int32, (slots, cells), 1).astype(F32)

    def pair_pass(first):
        froms = [source_at(order, first + i) for i in range(2)]
        hots = []
        for source in froms:
            here = sent_ref[source, deep - 1 : deep]
            hots.append(jnp.where(cell_down == here, 1.0, 0.0).astype(BF16))
        onehot = jnp.concatenate(hots, axis=1)
        place_ref[:, pl.ds(pl.multiple_of(slots * first, 2 * slots), 2 * slots)] = onehot
        picked = dot(stacked, onehot)
        jac = jnp.concatenate([sent_ref[source, :wide] for source in froms], axis=1)
        jac = jac * (picked[:wide] + picked[wide:])
        main = jac.astype(BF16).astype(F32)
        spread = dot(taps, jnp.concatenate([main, main, jac - main], axis=0).astype(BF16))
        for i in range(2):
            at = pl.ds(pl.multiple_of(slots * (first + i), slots), slots)
            extra = jnp.broadcast_to(sent_ref[froms[i], deep - 2 : deep - 1], (levels, slots))
            cell = jnp.broadcast_to(sent_ref[froms[i], deep - 1 : deep], (levels, slots))
            turned_ref[at, :levels] = spread[:, slots * i : slots * i + slots].T
            turned_ref[at, levels:] = extra.T
            pick_ref[at, :] = jnp.where(cell_along == cell.T[:, :1], 1.0, 0.0).astype(BF16)

    def step(g, carry):
        for i in range(4):
            pair_pass(8 * g + 2 * i)
        return carry

    lax.fori_loop(0, sources // 8, step, 0)


def zonal_rows(field_ref, ring_ref, near_ref, base):
    levels, rows, cols, width = near_ref.shape
    mhi, mlo = ring_ref[0], ring_ref[1]
    for kp in range(levels // 2):
        k = base + 2 * kp
        pair = zonal(mhi, mlo, jnp.concatenate([field_ref[k], field_ref[k + 1]], axis=1))
        for j in range(2):
            near_ref[2 * kp + j] = pair[:, width * j : width * (j + 1)].reshape(rows, cols, width)


def smoothed_rows(north_ref, near_ref, south_ref, w_ref):
    levels, _, cols, _ = w_ref.shape

    def level_pass(k, carry):
        for j in range(cols // 8):
            w_ref[k, :, pl.ds(8 * j, 8), :] = meridional(k, j, north_ref, near_ref, south_ref)
        return carry

    lax.fori_loop(0, levels, level_pass, 0)


def level_pair(w_ref, kp):
    _, rows, cols, width = w_ref.shape
    flat = (rows * cols, width)
    return split(
        jnp.concatenate([w_ref[2 * kp].reshape(flat), w_ref[2 * kp + 1].reshape(flat)], axis=1)
    )


def observed(dst_ref, before_ref, turned_ref, pick_ref, pairs, base, start):
    width = dst_ref.shape[1]

    def chunk_pass(c, carry):
        to = pl.ds(pl.multiple_of(c * CHUNK, CHUNK), CHUNK)
        at = pl.ds(pl.multiple_of(start + c * CHUNK, CHUNK), CHUNK)
        pick = pick_ref[at, :]
        total = None
        if before_ref is not None:
            total = before_ref[at, :]
        for kp, (hi, lo) in enumerate(pairs):
            k = base + 2 * kp
            seen = dot(pick, hi) + dot(pick, lo)
            part = (
                turned_ref[at, k : k + 1] * seen[:, :width]
                + turned_ref[at, k + 1 : k + 2] * seen[:, width:]
            )
            total = part if total is None else total + part
        dst_ref[to, :] = total
        return carry

    lax.fori_loop(0, dst_ref.shape[0] // CHUNK, chunk_pass, 0)


def column_kernel(
    north_ref, south_ref, field_ref, ring_ref, turned_ref, pick_ref,
    part_ref, far_ref,
    near_ref, w_ref,
):
    zonal_rows(field_ref, ring_ref, near_ref, 0)
    zonal_rows(field_ref, ring_ref, far_ref, near_ref.shape[0])
    smoothed_rows(north_ref, near_ref, south_ref, w_ref)
    pairs = [level_pair(w_ref, kp) for kp in range(w_ref.shape[0] // 2)]
    observed(part_ref, None, turned_ref, pick_ref, pairs, 0, 0)


def column_other_kernel(
    north_ref, south_ref, far_ref, before_ref, turned_ref, pick_ref,
    other_ref, hi_ref, lo_ref,
    w_ref, *, base,
):
    smoothed_rows(north_ref, far_ref, south_ref, w_ref)
    pairs = []
    for kp in range(w_ref.shape[0] // 2):
        hi, lo = level_pair(w_ref, kp)
        hi_ref[kp], lo_ref[kp] = hi, lo
        pairs.append((hi, lo))
    observed(other_ref, before_ref, turned_ref, pick_ref, pairs, base, 0)


def column_own_kernel(hi_ref, lo_ref, before_ref, turned_ref, pick_ref, own_ref, *, base):
    pairs = [(hi_ref[kp], lo_ref[kp]) for kp in range(hi_ref.shape[0])]
    observed(own_ref, before_ref, turned_ref, pick_ref, pairs, base, own_ref.shape[0])


def weigh(runs, turned_ref, weighted_ref):
    row = 0
    for sum_ref, start in runs:
        count = sum_ref.shape[0]
        weight = turned_ref[start : start + count, 8:9]
        weighted_ref[row : row + count] = sum_ref[...] * weight
        row += count


def aligned(start, size):
    return pl.ds(start if isinstance(start, int) else pl.multiple_of(start, size), size)


def scatter(run, field_ref, weighted_ref, turned_ref, place_ref, k, unrolled=True):
    row, start, size, count, stride = run

    def chunk(i):
        to = aligned(start + stride * i, size)
        weighted = weighted_ref[aligned(row + size * i, size), :]
        pair = jnp.concatenate(
            [turned_ref[to, k : k + 1] * weighted, turned_ref[to, k + 1 : k + 2] * weighted],
            axis=1,
        )
        hi, lo = split(pair)
        place = place_ref[:, to]
        return dot(place, hi) + dot(place, lo)

    def chunk_pass(i, carry):
        field_ref[...] += chunk(i)
        return carry

    if unrolled:
        field_ref[...] += sum(chunk(i) for i in range(count))
    else:
        lax.fori_loop(0, count, chunk_pass, 0)


def kept_kernel(p_ref, q_ref, turned_ref, place_ref, field_ref, weighted_ref):
    half, n = turned_ref.shape[0] // 2, p_ref.shape[0]
    weigh(((p_ref, half + n), (q_ref, half + 3 * n)), turned_ref, weighted_ref)
    field_ref[...] = jnp.zeros(field_ref.shape, F32)
    for kp in range(field_ref.shape[0]):
        run = (0, half + n, n, 2, 2 * n)
        scatter(run, field_ref.at[kp], weighted_ref, turned_ref, place_ref, 2 * kp, False)


def own_kernel(p_ref, q_ref, turned_ref, place_ref, kept_ref, field_ref, weighted_ref):
    half, n = turned_ref.shape[0] // 2, p_ref.shape[0]
    weigh(((p_ref, half), (q_ref, half + 2 * n)), turned_ref, weighted_ref)
    for kp in range(field_ref.shape[0]):
        field_ref[kp] = kept_ref[kp]
        run = (0, half, n, 2, 2 * n)
        scatter(run, field_ref.at[kp], weighted_ref, turned_ref, place_ref, 2 * kp)


def adjoint_kernel(
    other_ref, turned_ref, place_ref, field_ref, ring_ref,
    out_ref, head_ref, tail_ref,
    weighted_ref, sum_ref,
):
    half = other_ref.shape[0]
    weigh(((other_ref, 0),), turned_ref, weighted_ref)
    for kp in range(out_ref.shape[0] // 2):
        sum_ref[...] = field_ref[kp]
        run = (0, 0, CHUNK, half // CHUNK, CHUNK)
        scatter(run, sum_ref, weighted_ref, turned_ref, place_ref, 2 * kp)
        put_levels(sum_ref[...], kp, out_ref)
    finish_zonal(ring_ref[0], ring_ref[1], out_ref, head_ref, tail_ref)


def adjoint_end_kernel(
    other_ref, p_ref, q_ref, turned_ref, place_ref, kept_ref, ring_ref,
    out_ref, head_ref, tail_ref,
    weighted_ref, sum_ref, *, base,
):
    half, n = other_ref.shape[0], p_ref.shape[0]
    runs = ((other_ref, 0), (p_ref, half), (q_ref, half + 2 * n))
    weigh(runs, turned_ref, weighted_ref)
    for kp in range(out_ref.shape[0] // 2):
        k = base + 2 * kp
        sum_ref[...] = kept_ref[k // 2]
        for run in ((0, 0, CHUNK, half // CHUNK, CHUNK), (half, half, n, 2, 2 * n)):
            scatter(run, sum_ref, weighted_ref, turned_ref, place_ref, k)
        put_levels(sum_ref[...], kp, out_ref)
    finish_zonal(ring_ref[0], ring_ref[1], out_ref, head_ref, tail_ref)


def panel_part(north_ref, own_ref, south_ref, probes_ref, panel_ref, base):
    levels, rows, cols, width = own_ref.shape

    def level_pass(k, carry):
        for j in range(cols // 8):
            cut = pl.ds(8 * j, 8)
            panel_ref[k, :, cut, :] = probes_ref[base + k, :, cut, :] + meridional(
                k, j, north_ref, own_ref, south_ref
            )
        hi, lo = split(panel_ref[k].reshape(rows * cols, width))
        turn = (((0,), (0,)), ((), ()))
        both = jnp.concatenate([hi, lo], axis=1)
        return carry + lax.dot_general(hi, both, turn, preferred_element_type=F32)

    both = lax.fori_loop(0, levels, level_pass, jnp.zeros((width, 2 * width), F32))
    main, cross = both[:, :width], both[:, width:]
    return main + (cross + cross.T)


def panel_kernel(north_ref, own_ref, south_ref, probes_ref, panel_ref, gram_ref):
    gram_ref[...] = panel_part(north_ref, own_ref, south_ref, probes_ref, panel_ref, 0)


def panel_end_kernel(
    north_ref, own_ref, south_ref, probes_ref, before_ref, panel_ref, packed_ref, *, base
):
    gram = before_ref[...] + panel_part(
        north_ref, own_ref, south_ref, probes_ref, panel_ref, base
    )
    packed_ref[...] = packed_gram(gram)


def packed_gram(gram):
    width = gram.shape[0]
    mid = width // 2
    row = lax.broadcasted_iota(jnp.int32, (mid, width), 0)
    col = lax.broadcasted_iota(jnp.int32, (mid, width), 1)
    top, low = gram[:mid], pltpu.roll(gram[mid:], mid, axis=1)
    body = jnp.where(col >= row, top, low)
    diag = jnp.sum(jnp.where(col == row, low, 0.0), axis=0, keepdims=True)
    return jnp.concatenate([body, jnp.broadcast_to(diag, (8, width))], axis=0)


def unpacked_gram(packed):
    width = packed.shape[1]
    mid = width // 2
    row = lax.broadcasted_iota(jnp.int32, (mid, width), 0)
    col = lax.broadcasted_iota(jnp.int32, (mid, width), 1)
    body = packed[:mid]
    turned = jnp.concatenate([body, body], axis=0).T
    top = jnp.where(col >= row, body, turned[:mid])
    far = col - mid
    body, flip = pltpu.roll(body, mid, axis=1), pltpu.roll(turned[:mid], mid, axis=1)
    diag = pltpu.roll(packed[mid:], mid, axis=1)[:1]
    corner = jnp.where(row > far, body, jnp.where(row < far, flip, diag))
    return jnp.concatenate([top, jnp.where(col < mid, turned[mid:], corner)], axis=0)


BLOCK = 8


def split3(x):
    hi, rest = split(x)
    mid = (x - hi.astype(F32)).astype(BF16)
    lo = (x - hi.astype(F32) - mid.astype(F32)).astype(BF16)
    return hi, mid, lo


def factor_kernel(gram_ref, low_ref, high_ref, q_ref, rfac_ref, both_ref, inv_ref, *, scale):
    width = gram_ref.shape[1]
    down = lax.broadcasted_iota(jnp.int32, (BLOCK, width), 0)
    along = lax.broadcasted_iota(jnp.int32, (BLOCK, width), 1)
    rows_all = lax.broadcasted_iota(jnp.int32, (width, width), 0)
    cols_all = lax.broadcasted_iota(jnp.int32, (width, width), 1)
    both_ref[:, :width] = unpacked_gram(gram_ref[...]) * scale
    both_ref[:, width:] = jnp.where(rows_all == cols_all, 1.0, 0.0)
    for start in range(0, width, BLOCK):
        block = both_ref[start : start + BLOCK, :]
        a, w = block[:, :width], block[:, width:]
        a = jnp.where(along >= start, a, 0.0)
        lanes = [
            jnp.broadcast_to(a[:, start + b : start + b + 1], (BLOCK, width)) for b in range(BLOCK)
        ]
        pivots = jnp.zeros((BLOCK, width), F32)
        for p in range(BLOCK):
            pivot = jnp.broadcast_to(lanes[p][p : p + 1], (BLOCK, width))
            pivots = jnp.where(down == p, pivot, pivots)
            if p == BLOCK - 1:
                break
            f = jnp.where(down > p, lanes[p] * (1.0 / pivot), 0.0)
            for b in range(p + 1, BLOCK):
                lanes[b] = lanes[b] - f * lanes[b][p : p + 1]
            a = a - f * a[p : p + 1]
            w = w - f * w[p : p + 1]
        roots = lax.rsqrt(pivots)
        roots = roots * (1.5 - 0.5 * pivots * roots * roots)
        u = jnp.where(along >= down + start, a * roots, 0.0)
        w = w * roots
        rfac_ref[start : start + BLOCK, :] = u
        inv_ref[start : start + BLOCK, :] = w
        if start + BLOCK < width:
            right = jnp.concatenate([u, w], axis=1)
            uh, um, ul = split3(u)
            rh, rm, rl = split3(right)
            left = jnp.concatenate([uh, uh, um, uh, ul, um], axis=0)
            right = jnp.concatenate([rh, rm, rh, rl, rh, rm], axis=0)
            update = lax.dot_general(
                left, right, (((0,), (0,)), ((), ())), preferred_element_type=F32
            )
            both_ref[start + BLOCK :] -= update[start + BLOCK :]
    ih, il = split(inv_ref[...])
    inv_both = jnp.concatenate([ih, il], axis=0)
    turn = (((1,), (1,)), ((), ()))
    for src_ref, base in ((low_ref, 0), (high_ref, low_ref.shape[0])):
        for k in range(src_ref.shape[0]):
            hi, lo = split(src_ref[k])
            wide = lax.dot_general(hi, inv_both, turn, preferred_element_type=F32)
            low = lax.dot_general(lo, ih, turn, preferred_element_type=F32)
            q_ref[base + k] = wide[:, :width] + (low + wide[:, width:])


def steps(axis_size, fn):
    return [(i, fn(i)) for i in range(axis_size)]


def core_swap(n):
    return steps(n, lambda l: l ^ 1)


def ring_swap(n, odd):
    chips = n // 2

    def partner(l):
        y = l >> 1
        y = chips - 1 - y if odd else y ^ 1
        return (y << 1) | (l & 1)

    return steps(n, partner)


def level_sum(other, own, meanwhile):
    n = lax.axis_size("lev")
    core, even, odd = core_swap(n), ring_swap(n, False), ring_swap(n, True)

    def send(x, perm):
        return lax.ppermute(x, "lev", perm)

    def reduced(x, perm):
        mid = x.shape[0] // 2
        return x[mid:] + send(x[:mid], perm)

    def summed(x, perm):
        return x + send(x, perm)

    together = lax.optimization_barrier
    mine = send(other, core)
    mid = own.shape[0] // 2
    p, q = own[:mid] + mine[:mid], own[mid:] + mine[mid:]
    p, q = together((reduced(p, even), reduced(q, odd)))
    p, q = together((summed(p, odd), summed(q, even)))
    *got, used = together((send(p, even), send(q, odd), meanwhile(p, q)))
    own = jnp.concatenate([got[0], p, got[1], q])
    return send(own, core), got, used


def own_order():
    l = lax.axis_index("lev")
    y, c = l >> 1, l & 1
    first, second = (y ^ (y >> 1)) & 1, y >> 1
    keep = (1 - c) << 4
    one = keep | ((1 - first) << 2)
    two = keep | ((1 - second) << 2)
    return one, two


def gram_sum(x):
    n, m = lax.axis_size("lev"), lax.axis_size("tile")

    for perm in (core_swap(n), ring_swap(n, False), ring_swap(n, True)):
        x = x + lax.ppermute(x, "lev", perm)
    for fn in (
        lambda t: t ^ 1,
        lambda t: (t & ~3) | (3 - (t & 3)),
        lambda t: (t & ~7) | (7 - (t & 7)),
        lambda t: t ^ 8,
        lambda t: (t & 7) | ((3 - (t >> 3)) << 3),
    ):
        x = x + lax.ppermute(x, "tile", steps(m, fn))
    return x


def from_neighbours(lower_piece, upper_piece, axis):
    count = lax.axis_size(axis)
    below = lax.ppermute(lower_piece, axis, [(i, i + 1) for i in range(count - 1)])
    above = lax.ppermute(upper_piece, axis, [(i + 1, i) for i in range(count - 1)])
    return below, above


PARAMS = pltpu.CompilerParams(vmem_limit_bytes=16 << 20)


def shape(*dims, dtype=F32):
    return jax.ShapeDtypeStruct(dims, dtype)


NEAR = ((0, 4), (4, 4))
PARTS = ((0, 4), (4, 4))
tied = lax.optimization_barrier


def call(kernel, outs, *args, scratch=(), name=None, **static):
    def body(*refs):
        kernel(*refs, **static)

    return pl.pallas_call(
        body,
        out_shape=outs,
        scratch_shapes=list(scratch),
        compiler_params=PARAMS,
        name=name,
    )(*args)


def shards(probes, sigma, obs_count, obs_cell, obs_rinv, obs_jac):
    levels, rows, cols, width = probes.shape
    cells = rows * cols
    rim = REACH * cols
    bins, slots = obs_cell.shape
    total = bins * slots
    half = total // 2
    ring = jnp.stack(split(jnp.asarray(ring_matrix(cols, 256))))

    def field(n):
        return (shape(n, cells, width), shape(n, rim, width), shape(n, rim, width))

    def banded(across, head, tail):
        n = across.shape[0]
        north, south = from_neighbours(tail, head, "tile")
        edge = (n, REACH, cols, width)
        return north.reshape(edge), across.reshape(n, rows, cols, width), south.reshape(edge)

    flat = probes.reshape(levels, cells, width)

    def rims(after, base, n):
        source = flat if after is None else tied((flat, after))[0]
        edge = shape(n, rim, width)
        head, tail = call(
            rim_kernel, (edge, edge), source, ring, base=base, name="rim" + str(base)
        )
        north, south = from_neighbours(tail, head, "tile")
        return north.reshape(n, REACH, cols, width), south.reshape(n, REACH, cols, width)

    near = rims(None, *NEAR[0])
    local = jnp.concatenate(
        [obs_jac, sigma.reshape(levels, cells // slots, slots).transpose(1, 0, 2)]
    )
    below, above = from_neighbours(local, local, "lev")
    live = jnp.arange(slots, dtype=jnp.int32)[None, :] < obs_count[:, None]
    rinv = jnp.where(live, obs_rinv, 0.0)
    packed = call(
        pack_kernel, shape(bins, 3 * levels + 2, slots), below, local, above, rinv, obs_cell,
        name="pack"
    )
    sent = lax.all_to_all(packed, "tile", split_axis=0, concat_axis=0, tiled=True)
    turned, pick, place = call(
        prepare_kernel,
        (
            shape(total, 2 * levels),
            shape(total, cells, dtype=BF16),
            shape(cells, total, dtype=BF16),
        ),
        sent, below, local, above, name="prepare",
    )
    far = rims(packed, *NEAR[1])

    def grid(n):
        return pltpu.VMEM((n, rows, cols, width), F32)

    base, n = NEAR[0]
    column, far_rows = call(
        column_kernel, (shape(total, width), shape(NEAR[1][1], rows, cols, width)),
        *near, flat, ring, turned, pick, scratch=[grid(n), grid(n)], name="column",
    )
    base, n = NEAR[1]
    wide = shape(n // 2, cells, 2 * width, dtype=BF16)
    other, high, low = call(
        column_other_kernel, (shape(half, width), wide, wide),
        *far, far_rows, column, turned, pick, scratch=[grid(n)], base=base, name="column_other",
    )
    own = call(
        column_own_kernel, shape(half, width),
        high, low, column, turned, pick, base=base, name="column_own",
    )

    def weights(n):
        return [pltpu.VMEM((n, width), F32)]

    wide = (cells, 2 * width)

    def scatter_kept(p, q):
        return call(
            kept_kernel, shape(levels // 2, *wide), p, q, turned, place,
            scratch=weights(half // 2), name="kept",
        )

    other, got, field_kept = level_sum(other, own, scatter_kept)
    base, n = PARTS[0]
    field_own = call(
        own_kernel, shape(n // 2, *wide), *got, turned, place, field_kept,
        scratch=weights(half // 2), name="own",
    )
    near = call(
        adjoint_kernel, field(n), other, turned, place, field_own, ring,
        scratch=weights(half) + [pltpu.VMEM(wide, F32)], name="adjoint",
    )
    other, _ = tied((other, near[1]))
    fields = [banded(*near)]
    base, n = PARTS[1]
    near = call(
        adjoint_end_kernel, field(n), other, *got, turned, place, field_kept, ring,
        scratch=weights(half + half // 2) + [pltpu.VMEM(wide, F32)], base=base, name="adjoint_end",
    )
    fields.append(banded(*near))

    base, n = PARTS[0]
    first, gram = pl.pallas_call(
        panel_kernel,
        out_shape=(shape(n, rows, cols, width), shape(width, width)),
        compiler_params=PARAMS,
        name="panel",
    )(*fields[0], probes)
    base, n = PARTS[1]

    def end_body(*refs):
        panel_end_kernel(*refs, base=base)

    second, gram = pl.pallas_call(
        end_body,
        out_shape=(shape(n, rows, cols, width), shape(width // 2 + 8, width)),
        compiler_params=PARAMS,
        name="panel_end",
    )(*fields[1], probes, gram)
    panels = [p.reshape(-1, cells, width) for p in (first, second)]
    gram = gram_sum(gram)
    whole = cells * levels * lax.axis_size("tile") * lax.axis_size("lev")

    def factor_body(*refs):
        factor_kernel(*refs, scale=1.0 / whole)

    qpanel, rfac = pl.pallas_call(
        factor_body,
        out_shape=(shape(levels, cells, width), shape(width, width)),
        scratch_shapes=[pltpu.VMEM((width, 2 * width), F32), pltpu.VMEM((width, width), F32)],
        compiler_params=PARAMS,
        name="factor",
    )(gram, *panels)
    return (qpanel.reshape(probes.shape), rfac)


def solution(mesh):
    in_specs = (
        P("lev", "tile", None, None),
        P("lev", "tile", None),
        P("tile"),
        P("tile", None),
        P("tile", None),
        P("tile", "lev", None),
    )
    out_specs = (P("lev", "tile", None, None), P())
    return jax.shard_map(shards, mesh=mesh, in_specs=in_specs, out_specs=out_specs, check_vma=False)
```
